128 devices in a mesh: gz: 32 (over y, x, core), ma: 4 (over z).
Axes of the slice: x: 4, y: 4, z: 4, core: 2. Of those that a mesh axis runs over, the one named last changes fastest.
Arguments:
- bricks: bfloat16 [16384, 2048], P(('gz', 'ma')), may hold values from -7 to 7
- owners: int32 [16384, 1], P(('gz', 'ma')), may hold values from 0 to 127; in each aligned block of 128 rows (0 to 127, 128 to 255, ...) at most 2 rows name the same one
- tile_ids: int32 [16384], P(('gz', 'ma')), may hold values from 0 to 511
- counts: int32 [128], P(('gz', 'ma')), may hold values from 64 to 128, as said below
Outputs:
- brick_potential: bfloat16 [16384, 2048], P(('gz', 'ma'))
The draws below stay inside these ranges and needn't reach their ends.
Inputs may be any that keep to these rules, and one draw needn't show every extreme that they name: `owners`: in the rows of one atom domain no device is named by more than 2 rows, and in every draw some device is named by exactly 2 rows of some domain. `counts`: some atom domain uses all 128 of its bricks.
All inputs are finite; a program needn't handle non-finite values.
Results may differ from the reference program's by a relative error of at most 0.0013.
Values may be sent and summed in bfloat16 or wider, within the bound.
A program may use at most 192 MiB of HBM per device.

```python
import math
import jax
import jax.numpy as jnp
import numpy as np
from jax import lax

NX = 512
NY = 512
SCREEN = 16
BZ = 4
BX = 8
BY = 64
CZ = 16
BRICK_DEV = 128
NZ = 512
DOMAINS = 128
CAP = 2
CELLS = 2048
TILES_DEV = 512
N_GZ = 32
N_MA = 4


def draw_counts(key, part):
    values = jax.random.randint(key, (DOMAINS,), BRICK_DEV // 2, BRICK_DEV + 1, dtype=jnp.int32)
    chosen = jax.random.randint(jax.random.fold_in(key, 7), (), 0, DOMAINS, dtype=jnp.int32)
    positions = jnp.arange(DOMAINS, dtype=jnp.int32)
    return jnp.where(positions == chosen, BRICK_DEV, values).astype(jnp.int32)


def draw_bricks(key, part):
    rough_key = jax.random.fold_in(key, 11)
    level_key = jax.random.fold_in(key, 13)
    shape = (DOMAINS * BRICK_DEV, CELLS)
    level = jax.random.uniform(level_key, (DOMAINS * BRICK_DEV, 1), jnp.float32, 0.5, 1.5)
    rough = jnp.clip(jax.random.normal(rough_key, shape, jnp.float32), -6.0, 6.0)
    base_level = 0.012
    values = rough + base_level * level
    return values.astype(jnp.bfloat16)


def place_ends(array, stream_key, smallest, high):
    extent = array.shape
    place = [jax.random.randint(jax.random.fold_in(stream_key, axis), (), 0, extent[axis]) for axis in range(len(extent))]
    array = array.at[tuple(place)].set(smallest)
    longest = extent.index(max(extent))
    place[longest] = (place[longest] + 1) % extent[longest]
    return array.at[tuple(place)].set(high)


def assign_block(rng, own, number, rows, amount, top, reach, lean):
    order = jax.random.permutation(rng, amount)
    crowded, common = shares(amount, rows * top, reach, lean, True), shares(amount, rows * top, reach, lean, False)
    places = jnp.arange(amount)

    def named(lengths, rotation):
        used = int((lengths > 0).sum())
        fixed = max(1, used // 4)
        passed = fixed + (places - fixed + rotation * (used - fixed)) % max(1, amount - fixed)
        return jnp.zeros((amount,), jnp.int32).at[order[jnp.where(places < fixed, places, passed)]].set(jnp.asarray(lengths, jnp.int32))

    lengths = jnp.where(number % 4 == 0, named(crowded, number // 4), named(common, number - number // 4 - 1))
    mixed = jax.random.permutation(jax.random.fold_in(own, 3), amount)
    donor, sink = mixed[0:amount // 2 * 2:2], mixed[1:amount // 2 * 2:2]
    margin = jnp.minimum(lengths[donor] - 1, reach - lengths[sink]) // 2
    margin = jnp.where((donor == order[0]) | (sink == order[0]) | (lengths[sink] == 0), 0, jnp.maximum(margin, 0))
    passed = jax.random.randint(jax.random.fold_in(own, 4), (amount // 2,), 0, 1 << 20) % (margin + 1)
    lengths = lengths.at[donor].add(-passed).at[sink].add(passed)
    items = jnp.searchsorted(jnp.cumsum(lengths), jnp.arange(rows * top), side="right").astype(jnp.int32)
    grid = items.reshape(top, rows).T
    grid = grid[jax.random.permutation(jax.random.fold_in(own, 1), rows)]
    rotation = jax.random.randint(jax.random.fold_in(own, 2), (rows, 1), 0, top)
    return jnp.take_along_axis(grid, (jnp.arange(top)[None, :] + rotation) % top, axis=1)


def shares(number_of, total, reach, slope, full):
    loads = [(1 << 20) // math.isqrt(standing ** slope) + 1 for standing in range(1, number_of + 1)]
    largest = reach if full else min(reach, max(-(-total // number_of), total * loads[0] // sum(loads)))
    least = 1 if total - largest >= number_of - 1 else 0
    holding, spare = [largest] + [least] * (number_of - 1), total - largest - least * (number_of - 1)
    while spare > 0:
        free = [i for i in range(1, number_of) if holding[i] < largest] or [i for i in range(1, number_of) if holding[i] < reach]
        pool, budget = sum([loads[i] for i in free]), spare
        for i in free:
            addition = min(reach - holding[i], max(1, budget * loads[i] // pool), spare)
            holding[i] = holding[i] + addition
            spare = spare - addition
    return np.array(holding)


def setup_inputs(seed: int = 0) -> dict:
    streams_of = jax.random.split(jax.random.key(seed), 5)
    bricks = draw_bricks(jax.random.fold_in(streams_of[4], 71), 0)
    owners_keys = jax.random.split(jax.random.fold_in(streams_of[1], 1), (DOMAINS * BRICK_DEV) // BRICK_DEV)
    owners_turns = jax.random.permutation(jax.random.fold_in(streams_of[1], 3), (DOMAINS * BRICK_DEV) // BRICK_DEV)
    owners = jax.vmap(lambda own, number: assign_block(jax.random.fold_in(streams_of[1], 2), own, number, BRICK_DEV, DOMAINS, 1, CAP, 2))(owners_keys, owners_turns).reshape((DOMAINS * BRICK_DEV, 1))
    tile_ids = place_ends(jax.random.randint(streams_of[2], (DOMAINS * BRICK_DEV,), 0, TILES_DEV), jax.random.fold_in(streams_of[2], 1), 0, TILES_DEV - 1).astype(jnp.int32)
    counts = draw_counts(jax.random.fold_in(streams_of[4], 71), 0)
    return dict(bricks=bricks, owners=owners, tile_ids=tile_ids, counts=counts)


def hartley(length):
    indices = jnp.arange(length, dtype=jnp.int32)
    products = indices[:, None] * indices[None, :] % length
    angles = 2.0 * math.pi / length * products.astype(jnp.float32)
    return (jnp.cos(angles) + jnp.sin(angles)) / math.sqrt(length)

def second_difference(length, indices):
    return 2.0 - 2.0 * jnp.cos(2.0 * math.pi / length * indices.astype(jnp.float32))

def thomas(right_side, diagonal):
    start_zero = jnp.zeros(right_side.shape[1:], jnp.float32)

    def down(state_pair, plane):
        factor = 1.0 / (diagonal - state_pair[0])
        partial_value = (plane + state_pair[1]) * factor
        return ((factor, partial_value), (factor, partial_value))
    _, (factors, partials) = lax.scan(down, (start_zero, start_zero), right_side)

    def upward(beyond, factor_partial):
        solved = factor_partial[1] + factor_partial[0] * beyond
        return (solved, solved)
    _, solutions = lax.scan(upward, start_zero, (factors, partials), reverse=True)
    return solutions

def reference(bricks, owners, tile_ids, counts):
    local_x = NX // N_MA
    local_y = NY // N_MA
    row_order = jnp.arange(DOMAINS * BRICK_DEV, dtype=jnp.int32)
    is_live = row_order % BRICK_DEV < counts[row_order // BRICK_DEV]
    segment = owners[:, 0] * TILES_DEV + tile_ids
    loaded = jnp.where(is_live[:, None], bricks.astype(jnp.float32), jnp.zeros((), jnp.float32))
    placed = jax.ops.segment_sum(loaded, segment, num_segments=DOMAINS * TILES_DEV)
    charge = placed.reshape(N_GZ, N_MA, CZ // BZ, local_x // BX, NY // BY, BZ, BX, BY)
    charge = charge.transpose(0, 2, 5, 1, 3, 6, 4, 7).reshape(NZ, NX, NY)
    table_x = hartley(NX)
    table_y = hartley(NY)
    lam_x = second_difference(NX, jnp.arange(NX, dtype=jnp.int32))
    lam_y_all = second_difference(NY, jnp.arange(NY, dtype=jnp.int32))
    screening = 1.0 / (SCREEN * SCREEN)
    highest = lax.Precision.HIGHEST

    def solve_block(total, block):
        start = block * local_y
        rows_y = lax.dynamic_slice_in_dim(table_y, start, local_y, 0)
        lam_y = lax.dynamic_slice_in_dim(lam_y_all, start, local_y, 0)
        spec_y = jnp.einsum('zxy,ky->zxk', charge, rows_y, precision=highest)
        spectrum = jnp.einsum('zxk,jx->zjk', spec_y, table_x, precision=highest)
        diagonal = 2.0 + screening + lam_x[:, None] + lam_y[None, :]
        modal = thomas(spectrum, diagonal)
        back_x = jnp.einsum('zjk,jx->zxk', modal, table_x, precision=highest)
        return (total + jnp.einsum('zxk,ky->zxy', back_x, rows_y, precision=highest), None)
    potential, _ = lax.scan(solve_block, jnp.zeros((NZ, NX, NY), jnp.float32), jnp.arange(N_MA, dtype=jnp.int32))
    tiles_all = potential.reshape(N_GZ, CZ // BZ, BZ, N_MA, local_x // BX, BX, NY // BY, BY)
    tiles_all = tiles_all.transpose(0, 3, 1, 4, 6, 2, 5, 7).reshape(DOMAINS * TILES_DEV, CELLS)
    picked = tiles_all[segment]
    return jnp.where(is_live[:, None], picked, jnp.zeros((), jnp.float32)).astype(jnp.bfloat16)
```

```python
import math

import jax
import jax.numpy as jnp
import ml_dtypes
import numpy as np
from jax import lax
from jax.experimental import pallas as pl
from jax.experimental.pallas import tpu as pltpu
from jax.sharding import PartitionSpec as P

N = 512
HALF = 256
SCREEN = 16
F32 = jnp.float32
BF16 = jnp.bfloat16
MESH = pl.DeviceIdType.MESH
SLOTS = 256
CELLS = 2048
WIDE = CELLS + 128
ROWS = 128


def split_table(table):
    high = table.astype(ml_dtypes.bfloat16)
    low = (table - high.astype(np.float64)).astype(ml_dtypes.bfloat16)
    return high, low


def parity_table(parity, points):
    modes = 2 * np.arange(HALF) + parity
    angle = 2.0 * math.pi / N * ((modes[:, None] * points[None, :]) % N)
    return (np.cos(angle) + np.sin(angle)) / math.sqrt(N)


def stacked(tables):
    return np.stack([np.stack(split_table(t)) for t in tables])


def tables():
    natural = np.arange(HALF)
    m, ix, tx = np.meshgrid(np.arange(2), np.arange(8), np.arange(16), indexing="ij")
    order = (m * 128 + tx * 8 + ix).reshape(-1)
    y_tables = [parity_table(p, natural) for p in (0, 1)]
    x_tables = [parity_table(p, order) for p in (0, 1)]
    y_in = stacked([t.T for t in y_tables])
    y_out = stacked(y_tables)
    x_in = stacked(x_tables)
    x_out = stacked([t.T for t in x_tables])
    return y_in, y_out, x_in, x_out


def mode_rates(m):
    k = np.arange(128)
    columns = np.stack([2 * ((c % 2) * 128 + k) + c // 2 for c in range(4)])
    rows = np.concatenate([2 * np.arange(HALF) + p for p in (0, 1)])

    def second_difference(index):
        return (4.0 * np.sin(math.pi / N * index) ** 2).astype(np.float32)

    lam_k = lax.dynamic_index_in_dim(jnp.asarray(second_difference(columns)), m, 0, keepdims=True)
    lam_j = jnp.asarray(second_difference(rows))[:, None]
    excess = 1.0 / (SCREEN * SCREEN) + lam_j + lam_k
    root = jnp.sqrt(excess * (excess + 4.0))
    return jnp.stack([2.0 / (2.0 + excess + root), 1.0 / root])


def handler(owner):
    core = (owner // 4) % 2
    y, t, m = owner // 32, (owner // 8) % 4, owner % 4
    return jnp.where(core == 1, y * 32 + m * 8 + 4 + t, owner)


def iota(shape, axis):
    return lax.broadcasted_iota(jnp.int32, shape, axis)


def slot_column_row(owners_ref):
    target = handler(owners_ref[...])
    column = jnp.broadcast_to(target, (ROWS, ROWS))
    row = jnp.transpose(column.astype(F32)).astype(jnp.int32)
    same = column == row
    i, j = iota((ROWS, ROWS), 0), iota((ROWS, ROWS), 1)
    within_column = jnp.sum(jnp.where(same & (j < i), 1.0, 0.0), axis=1, keepdims=True)
    within_row = jnp.sum(jnp.where(same & (i < j), 1.0, 0.0), axis=0, keepdims=True)
    slot_column = target * 2 + within_column.astype(jnp.int32)
    slot_row = row[0:1, :] * 2 + within_row.astype(jnp.int32)
    return slot_column, slot_row


def pack_kernel(counts_ref, bricks_ref, owners_ref, ids_ref, out_ref):
    _, slot_row = slot_column_row(owners_ref)
    live = iota((SLOTS, ROWS), 1) < counts_ref[0]
    picker = jnp.where((iota((SLOTS, ROWS), 0) == slot_row) & live, 1.0, 0.0).astype(BF16)
    ids = ids_ref[...]
    sub = iota((ROWS, ROWS), 0)
    meta = jnp.where(sub == 0, ids // 8, jnp.where(sub == 1, ids % 8, 0))
    meta = jnp.transpose(meta.astype(F32)).astype(BF16)
    for part in range(4):
        span = slice(part * 512, part * 512 + 512)
        out_ref[:, span] = jnp.dot(
            picker, bricks_ref[:, span], preferred_element_type=F32
        ).astype(BF16)
    out_ref[:, CELLS:] = jnp.dot(picker, meta, preferred_element_type=F32).astype(BF16)


def unpack_kernel(counts_ref, owners_ref, replies_ref, out_ref):
    slot_column, _ = slot_column_row(owners_ref)
    live = iota((ROWS, SLOTS), 0) < counts_ref[0]
    picker = jnp.where((iota((ROWS, SLOTS), 1) == slot_column) & live, 1.0, 0.0).astype(BF16)
    for part in range(4):
        span = slice(part * 512, part * 512 + 512)
        out_ref[:, span] = jnp.dot(
            picker, replies_ref[:, span], preferred_element_type=F32
        ).astype(BF16)


def halves(value):
    high = value.astype(BF16)
    return high, (value - high.astype(F32)).astype(BF16)


def three(a_high, a_low, b_high, b_low):
    total = jnp.dot(a_high, b_high, preferred_element_type=F32)
    total += jnp.dot(a_high, b_low, preferred_element_type=F32)
    total += jnp.dot(a_low, b_high, preferred_element_type=F32)
    return total


def coded(value):
    top = jnp.max(jnp.abs(value), axis=0, keepdims=True)
    step = jnp.maximum(top, 1e-30) * (1.0 / 32767.0)
    return jnp.round(value * (1.0 / step)).astype(jnp.int32).astype(jnp.int16), step


def decoded(code, step):
    return code.astype(jnp.int32).astype(F32) * step


def field_kernel(
    inc_ref, rates_ref, yin_ref, yout_ref, xin_ref, xout_ref, out_ref,
    place, xhi, xlo, sq, sstep, rq, rstep, spec, ends_out, ends_in, carry_out, carry_in,
    mhi, mlo, sq2, sstep2, rq2, rstep2, tiles,
    line_send, line_recv, ends_send, ends_recv, carry_send, carry_recv, back_send, back_recv, own_sem,
):
    gz, ma = lax.axis_index("gz"), lax.axis_index("ma")
    y, x, core = gz // 8, (gz // 2) % 4, gz % 2
    m = core * x + (1 - core) * ma
    t = core * ma + (1 - core) * x
    slab = y * 8 + t * 2 + core

    def line_peer(p):
        return (y * 8 + (core * p + (1 - core) * x) * 2 + core, core * ma + (1 - core) * p)

    def slab_peer(g):
        gy, gt, gc = g // 8, (g // 2) % 4, g % 2
        return (gy * 8 + (gc * m + (1 - gc) * gt) * 2 + gc, gc * gt + (1 - gc) * m)

    barrier = pltpu.get_barrier_semaphore()
    for d in range(1, 4):
        pl.semaphore_signal(barrier, inc=1, device_id=line_peer((m + d) % 4), device_id_type=MESH)

    def greet(d, _):
        pl.semaphore_signal(barrier, inc=1, device_id=slab_peer((slab + d) % 32), device_id_type=MESH)
        return 0

    lax.fori_loop(1, 32, greet, 0)

    meta = inc_ref[:, CELLS:].astype(F32)
    meta_rows = jnp.transpose(meta)
    q_row, ty_row = meta_rows[0:1, :].astype(jnp.int32), meta_rows[1:2, :].astype(jnp.int32)
    for p in range(2):
        for ty in range(4):
            hit = q_row == iota((64, SLOTS), 0)
            second = -1.0 if p else 1.0
            value = jnp.where(ty_row == ty, 1.0, 0.0) + jnp.where(ty_row == ty + 4, second, 0.0)
            first = (p * 4 + ty) * 64
            place[first : first + 64, :] = jnp.where(hit, value, 0.0).astype(BF16)
    low_half = iota((64, 128), 1) < 64

    for tile in range(16):
        iz, pair = tile // 4, tile % 4
        laid = jnp.dot(
            place[...], inc_ref[:, tile * 128 : tile * 128 + 128], preferred_element_type=F32
        )
        for p in range(2):
            for half in range(2):
                first = (p * 4 + half * 2) * 64
                te, to = laid[first : first + 64, :], laid[first + 64 : first + 128, :]
                even = jnp.where(low_half, te, pltpu.roll(to, 64, 1))
                odd = jnp.where(low_half, pltpu.roll(te, 64, 1), to)
                for k, value in enumerate((even, odd)):
                    row = (iz * 8 + pair * 2 + k) * 64
                    high, low = halves(value)
                    xhi[p, row : row + 64, half * 128 : half * 128 + 128] = high
                    xlo[p, row : row + 64, half * 128 : half * 128 + 128] = low

    pl.semaphore_wait(barrier, 34)

    def line_copies(iz, d, source, source_step, target, target_step, send, recv):
        peer = (m + d) % 4
        a = pltpu.make_async_remote_copy(
            src_ref=source.at[peer, iz], dst_ref=target.at[m, iz],
            send_sem=send.at[0, d - 1, iz], recv_sem=recv.at[0, d - 1, iz],
            device_id=line_peer(peer), device_id_type=MESH,
        )
        b = pltpu.make_async_remote_copy(
            src_ref=source_step.at[peer, iz], dst_ref=target_step.at[m, iz],
            send_sem=send.at[1, d - 1, iz], recv_sem=recv.at[1, d - 1, iz],
            device_id=line_peer(peer), device_id_type=MESH,
        )
        return a, b

    def own_copies(iz, which, source, source_step, target, target_step):
        a = pltpu.make_async_copy(source.at[m, iz], target.at[m, iz], own_sem.at[which, 0, iz])
        b = pltpu.make_async_copy(source_step.at[m, iz], target_step.at[m, iz], own_sem.at[which, 1, iz])
        return a, b

    forward = (sq, sstep, rq, rstep)
    for iz in range(4):
        rows = slice(iz * 512, iz * 512 + 512)
        for p in range(2):
            value = three(xhi[p, rows, :], xlo[p, rows, :], yin_ref[p, 0], yin_ref[p, 1])
            code, step = coded(value)
            for h in range(2):
                sq[p * 2 + h, iz] = code[:, h * 128 : h * 128 + 128].reshape(8, 4, 16, 128)
                sstep[p * 2 + h, iz] = jnp.broadcast_to(step[:, h * 128 : h * 128 + 128], (8, 128))
        for d in range(1, 4):
            for copy in line_copies(iz, d, *forward, line_send, line_recv):
                copy.start()
        for copy in own_copies(iz, 0, *forward):
            copy.start()

    for iz in range(4):
        for d in range(1, 4):
            for copy in line_copies(iz, d, *forward, line_send, line_recv):
                copy.wait_recv()
        for copy in own_copies(iz, 0, *forward):
            copy.wait()
        for tz in range(0, 4, 2):
            lines = []
            for source in range(4):
                step = rstep[source, iz][0:1, :]
                planes = [decoded(rq[source, iz, :, z].reshape(128, 128), step) for z in (tz, tz + 1)]
                lines.append(jnp.concatenate(planes, axis=1))
            for p in range(2):
                if p == 0:
                    folded = jnp.concatenate([lines[0] + lines[2], lines[1] + lines[3]], axis=0)
                else:
                    folded = jnp.concatenate([lines[0] - lines[2], lines[1] - lines[3]], axis=0)
                high, low = halves(folded)
                value = three(xin_ref[p, 0], xin_ref[p, 1], high, low)
                for k in range(2):
                    spec[(tz + k) * 4 + iz, p * 256 : p * 256 + 256, :] = value[:, k * 128 : k * 128 + 128]

    def slab_ends(b, _):
        rows = pl.ds(pl.multiple_of(b * 16, 16), 16)
        rate = rates_ref[0, rows, :]
        planes = [spec[z, rows, :] for z in range(16)]
        right, left = planes[0], planes[15]
        for z in range(1, 16):
            right = right * rate + planes[z]
            left = left * rate + planes[15 - z]
        ends_out[b, 0] = right
        ends_out[b, 1] = left
        return 0

    lax.fori_loop(0, 32, slab_ends, 0)

    def ends_copy(d):
        peer = (slab + d) % 32
        return pltpu.make_async_remote_copy(
            src_ref=ends_out.at[peer], dst_ref=ends_in.at[slab],
            send_sem=ends_send.at[d], recv_sem=ends_recv.at[d],
            device_id=slab_peer(peer), device_id_type=MESH,
        )

    def carry_copy(d):
        peer = (slab + d) % 32
        return pltpu.make_async_remote_copy(
            src_ref=carry_out.at[peer], dst_ref=carry_in.at[slab],
            send_sem=carry_send.at[d], recv_sem=carry_recv.at[d],
            device_id=slab_peer(peer), device_id_type=MESH,
        )

    def loop(body):
        def step(d, _):
            body(d)
            return 0

        lax.fori_loop(1, 32, step, 0)

    loop(lambda d: ends_copy(d).start())
    own_ends = pltpu.make_async_copy(ends_out.at[slab], ends_in.at[slab], own_sem.at[2, 0, 0])
    own_ends.start()
    loop(lambda d: ends_copy(d).wait_recv())
    own_ends.wait()

    rate = rates_ref[0, pl.ds(pl.multiple_of(slab * 16, 16), 16), :]
    r2 = rate * rate
    r4 = r2 * r2
    r8 = r4 * r4
    hop = r8 * r8
    far = hop
    for _ in range(5):
        far = far * far
    far = far * rate
    zero = jnp.zeros((16, 128), F32)
    total_right, total_left = zero, zero
    for g in range(32):
        total_right = total_right * hop + ends_in[g, 0]
        total_left = total_left * hop + ends_in[31 - g, 1]
    scale = -rate / (1.0 - far * far)
    right = scale * (total_left - far * total_right)
    left = scale * (total_right - far * total_left)
    for g in range(32):
        carry_out[g, 0] = right
        carry_out[31 - g, 1] = left
        right = right * hop + ends_in[g, 0]
        left = left * hop + ends_in[31 - g, 1]

    loop(lambda d: carry_copy(d).start())
    own_carry = pltpu.make_async_copy(carry_out.at[slab], carry_in.at[slab], own_sem.at[2, 1, 0])
    own_carry.start()
    loop(lambda d: carry_copy(d).wait_recv())
    own_carry.wait()

    def filters(b, _):
        rows = pl.ds(pl.multiple_of(b * 16, 16), 16)
        rate, gain = rates_ref[0, rows, :], rates_ref[1, rows, :]
        planes = [spec[z, rows, :] for z in range(16)]
        right, left = carry_in[b, 0], carry_in[b, 1]
        beyond = [None] * 16
        for z in range(15, -1, -1):
            beyond[z] = left * rate
            left = planes[z] + beyond[z]
        for z in range(16):
            right = planes[z] + right * rate
            high, low = halves((right + beyond[z]) * gain)
            mhi[z, rows, :] = high
            mlo[z, rows, :] = low
        return 0

    lax.fori_loop(0, 32, filters, 0)

    backward = (sq2, sstep2, rq2, rstep2)
    for iz in range(4):
        parts = []
        for tz in range(0, 4, 2):
            sums = []
            for p in range(2):
                rows = slice(p * 256, p * 256 + 256)
                high = jnp.concatenate([mhi[(tz + k) * 4 + iz, rows, :] for k in range(2)], axis=1)
                low = jnp.concatenate([mlo[(tz + k) * 4 + iz, rows, :] for k in range(2)], axis=1)
                sums.append(three(xout_ref[p, 0], xout_ref[p, 1], high, low))
            parts.append((sums[0] + sums[1], sums[0] - sums[1]))
        for target in range(4):
            span = slice((target % 2) * 128, (target % 2) * 128 + 128)
            blocks = []
            for tz in range(4):
                block = parts[tz // 2][target // 2][span, (tz % 2) * 128 : (tz % 2) * 128 + 128]
                blocks.append(block)
            top = blocks[0]
            for block in blocks:
                top = jnp.maximum(jnp.abs(top), jnp.abs(block))
            top = jnp.maximum(jnp.max(top, axis=0, keepdims=True), 1e-30)
            step = top * (1.0 / 32767.0)
            inverse = 1.0 / step
            for tz in range(4):
                code = jnp.round(blocks[tz] * inverse).astype(jnp.int32).astype(jnp.int16)
                sq2[target, iz, :, tz] = code.reshape(8, 16, 128)
            sstep2[target, iz] = jnp.broadcast_to(step, (8, 128))
        for d in range(1, 4):
            for copy in line_copies(iz, d, *backward, back_send, back_recv):
                copy.start()
        for copy in own_copies(iz, 1, *backward):
            copy.start()

    for iz in range(4):
        for d in range(1, 4):
            for copy in line_copies(iz, d, *backward, back_send, back_recv):
                copy.wait_recv()
        for copy in own_copies(iz, 1, *backward):
            copy.wait()
        sums = []
        for p in range(2):
            pieces = [
                decoded(rq2[p * 2 + h, iz].reshape(512, 128), rstep2[p * 2 + h, iz][0:1, :])
                for h in range(2)
            ]
            high, low = halves(jnp.concatenate(pieces, axis=1))
            sums.append(three(high, low, yout_ref[p, 0], yout_ref[p, 1]))
        for top, value in enumerate((sums[0] + sums[1], sums[0] - sums[1])):
            for half in range(2):
                lanes = slice(half * 128, half * 128 + 128)
                ty = top * 4 + half * 2
                for pair in range(4):
                    even = value[pair * 128 : pair * 128 + 64, lanes]
                    odd = value[pair * 128 + 64 : pair * 128 + 128, lanes]
                    span = slice((iz * 4 + pair) * 128, (iz * 4 + pair) * 128 + 128)
                    first = jnp.where(low_half, even, pltpu.roll(odd, 64, 1))
                    second = jnp.where(low_half, pltpu.roll(even, 64, 1), odd)
                    tiles[ty * 64 : ty * 64 + 64, span] = first.astype(BF16)
                    tiles[ty * 64 + 64 : ty * 64 + 128, span] = second.astype(BF16)

    q_column = meta[:, 0:1].astype(jnp.int32)
    ty_column = meta[:, 1:2].astype(jnp.int32)
    wanted = ty_column * 64 + q_column
    picker = jnp.where(iota((SLOTS, 512), 1) == wanted, 1.0, 0.0).astype(BF16)
    for part in range(4):
        span = slice(part * 512, part * 512 + 512)
        out_ref[:, span] = jnp.dot(picker, tiles[:, span], preferred_element_type=F32).astype(BF16)

    for iz in range(4):
        for d in range(1, 4):
            for copy in line_copies(iz, d, *forward, line_send, line_recv):
                copy.wait_send()
            for copy in line_copies(iz, d, *backward, back_send, back_recv):
                copy.wait_send()
    loop(lambda d: ends_copy(d).wait_send())
    loop(lambda d: carry_copy(d).wait_send())


VMEM_LIMIT = 60 * 1024 * 1024


def on_device(bricks, owners, tile_ids, counts):
    gz, ma = lax.axis_index("gz"), lax.axis_index("ma")
    m = jnp.where(gz % 2 == 1, (gz // 2) % 4, ma)
    vmem = pl.BlockSpec(memory_space=pltpu.VMEM)
    smem = pl.BlockSpec(memory_space=pltpu.SMEM)
    outgoing = pl.pallas_call(
        pack_kernel,
        out_shape=jax.ShapeDtypeStruct((SLOTS, WIDE), BF16),
        in_specs=[smem, vmem, vmem, vmem],
        out_specs=vmem,
        name="pack",
    )(counts, bricks, owners, tile_ids.reshape(1, ROWS))
    incoming = lax.all_to_all(outgoing, ("gz", "ma"), split_axis=0, concat_axis=0, tiled=True)
    rates = mode_rates(m)
    y_in, y_out, x_in, x_out = (jnp.asarray(t) for t in tables())
    codes = pltpu.VMEM((4, 4, 8, 4, 16, 128), jnp.int16)
    steps = pltpu.VMEM((4, 4, 8, 128), F32)
    share = pltpu.VMEM((32, 2, 16, 128), F32)
    replies = pl.pallas_call(
        field_kernel,
        out_shape=jax.ShapeDtypeStruct((SLOTS, CELLS), BF16),
        in_specs=[vmem] * 6,
        out_specs=vmem,
        scratch_shapes=[
            pltpu.VMEM((512, SLOTS), BF16),
            pltpu.VMEM((2, 2048, HALF), BF16),
            pltpu.VMEM((2, 2048, HALF), BF16),
            codes, steps, codes, steps,
            pltpu.VMEM((16, 512, 128), F32),
            share, share, share, share,
            pltpu.VMEM((16, 512, 128), BF16),
            pltpu.VMEM((16, 512, 128), BF16),
            codes, steps, codes, steps,
            pltpu.VMEM((512, CELLS), BF16),
            pltpu.SemaphoreType.DMA((2, 3, 4)),
            pltpu.SemaphoreType.DMA((2, 3, 4)),
            pltpu.SemaphoreType.DMA((32,)),
            pltpu.SemaphoreType.DMA((32,)),
            pltpu.SemaphoreType.DMA((32,)),
            pltpu.SemaphoreType.DMA((32,)),
            pltpu.SemaphoreType.DMA((2, 3, 4)),
            pltpu.SemaphoreType.DMA((2, 3, 4)),
            pltpu.SemaphoreType.DMA((3, 2, 4)),
        ],
        compiler_params=pltpu.CompilerParams(
            collective_id=0, has_side_effects=True, vmem_limit_bytes=VMEM_LIMIT
        ),
        name="field",
    )(incoming, rates, y_in, y_out, x_in, x_out)
    returned = lax.all_to_all(replies, ("gz", "ma"), split_axis=0, concat_axis=0, tiled=True)
    return pl.pallas_call(
        unpack_kernel,
        out_shape=jax.ShapeDtypeStruct((ROWS, CELLS), BF16),
        in_specs=[smem, vmem, vmem],
        out_specs=vmem,
        name="unpack",
    )(counts, owners, returned)


def solution(mesh):
    in_specs = (P(("gz", "ma"), None), P(("gz", "ma"), None), P(("gz", "ma")), P(("gz", "ma")))
    out_specs = P(("gz", "ma"), None)
    return jax.shard_map(
        on_device, mesh=mesh, in_specs=in_specs, out_specs=out_specs, check_vma=False
    )
```

```python
import math

import jax
import jax.numpy as jnp
import ml_dtypes
import numpy as np
from jax import lax
from jax.experimental import pallas as pl
from jax.experimental.pallas import tpu as pltpu
from jax.sharding import PartitionSpec as P

N = 512
HALF = 256
SCREEN = 16
F32 = jnp.float32
BF16 = jnp.bfloat16
MESH = pl.DeviceIdType.MESH
SLOTS = 256
CELLS = 2048
ROWS = 128


def split_table(table):
    high = table.astype(ml_dtypes.bfloat16)
    low = (table - high.astype(np.float64)).astype(ml_dtypes.bfloat16)
    return high, low


def parity_table(parity, points):
    modes = 2 * np.arange(HALF) + parity
    angle = 2.0 * math.pi / N * ((modes[:, None] * points[None, :]) % N)
    return (np.cos(angle) + np.sin(angle)) / math.sqrt(N)


def stacked(tables):
    return np.stack([np.stack(split_table(t)) for t in tables])


def tables():
    natural = np.arange(HALF)
    m, ix, tx = np.meshgrid(np.arange(2), np.arange(8), np.arange(16), indexing="ij")
    order = (m * 128 + tx * 8 + ix).reshape(-1)
    y_tables = [parity_table(p, natural) for p in (0, 1)]
    x_tables = [parity_table(p, order) for p in (0, 1)]
    y_in = stacked([t.T for t in y_tables])
    y_out = stacked(y_tables)
    x_in = stacked(x_tables)
    x_out = stacked([t.T for t in x_tables])
    return y_in, y_out, x_in, x_out


def mode_rates(m):
    k = np.arange(128)
    columns = np.stack([2 * ((c % 2) * 128 + k) + c // 2 for c in range(4)])
    rows = np.concatenate([2 * np.arange(HALF) + p for p in (0, 1)])

    def second_difference(index):
        return (4.0 * np.sin(math.pi / N * index) ** 2).astype(np.float32)

    lam_k = lax.dynamic_index_in_dim(jnp.asarray(second_difference(columns)), m, 0, keepdims=True)
    lam_j = jnp.asarray(second_difference(rows))[:, None]
    excess = 1.0 / (SCREEN * SCREEN) + lam_j + lam_k
    root = jnp.sqrt(excess * (excess + 4.0))
    return jnp.stack([2.0 / (2.0 + excess + root), 1.0 / root])


def handler(owner):
    core = (owner // 4) % 2
    y, t, m = owner // 32, (owner // 8) % 4, owner % 4
    return jnp.where(core == 1, y * 32 + m * 8 + 4 + t, owner)


def iota(shape, axis):
    return lax.broadcasted_iota(jnp.int32, shape, axis)


def pickers(owners_ref, count):
    target = handler(owners_ref[...])
    column = jnp.broadcast_to(target, (ROWS, ROWS))
    row = jnp.transpose(column.astype(F32)).astype(jnp.int32)
    same = column == row
    i, j = iota((ROWS, ROWS), 0), iota((ROWS, ROWS), 1)
    within_column = jnp.sum(jnp.where(same & (j < i), 1.0, 0.0), axis=1, keepdims=True)
    within_row = jnp.sum(jnp.where(same & (i < j), 1.0, 0.0), axis=0, keepdims=True)
    slot_column = target + ROWS * within_column.astype(jnp.int32)
    slot_row = row[0:1, :] + ROWS * within_row.astype(jnp.int32)
    down = (iota((SLOTS, ROWS), 0) == slot_row) & (iota((SLOTS, ROWS), 1) < count)
    across = (iota((ROWS, SLOTS), 1) == slot_column) & (iota((ROWS, SLOTS), 0) < count)
    return jnp.where(down, 1.0, 0.0).astype(BF16), jnp.where(across, 1.0, 0.0).astype(BF16)


def halves(value):
    high = value.astype(BF16)
    return high, (value - high.astype(F32)).astype(BF16)


def three(a_high, a_low, b_high, b_low):
    total = jnp.dot(a_high, b_high, preferred_element_type=F32)
    total += jnp.dot(a_high, b_low, preferred_element_type=F32)
    total += jnp.dot(a_low, b_high, preferred_element_type=F32)
    return total


def coded(value):
    top = jnp.max(jnp.abs(value), axis=0, keepdims=True)
    step = jnp.maximum(top, 1e-30) * (1.0 / 32767.0)
    return jnp.round(value * (1.0 / step)).astype(jnp.int32).astype(jnp.int16), step


def decoded(code, step):
    return code.astype(jnp.int32).astype(F32) * step


def field_kernel(
    counts_ref, bricks_ref, owners_ref, ids_ref, rates_ref, yin_ref, yout_ref, xin_ref, xout_ref, out_ref,
    stage, brick_out, brick_in, meta_out, meta_in, meta, reply_out, reply_in, unpick, fetch, place, xhi, xlo, sq, sstep, rq, rstep, spec, ends_out, ends_in, carry_out, carry_in,
    mhi, mlo, sq2, sstep2, rq2, rstep2, tiles,
    brick_send, brick_recv, meta_sem, reply_send, reply_recv, line_send, line_recv, ends_sem, carry_sem, back_send, back_recv, own_sem,
):
    gz, ma = lax.axis_index("gz"), lax.axis_index("ma")
    y, x, core = gz // 8, (gz // 2) % 4, gz % 2
    m = core * x + (1 - core) * ma
    t = core * ma + (1 - core) * x
    slab = y * 8 + t * 2 + core

    def line_peer(p):
        return (y * 8 + (core * p + (1 - core) * x) * 2 + core, core * ma + (1 - core) * p)

    def slab_peer(g):
        gy, gt, gc = g // 8, (g // 2) % 4, g % 2
        return (gy * 8 + (gc * m + (1 - gc) * gt) * 2 + gc, gc * gt + (1 - gc) * m)

    me = gz * 4 + ma
    barrier = pltpu.get_barrier_semaphore()

    def loop(stop, body):
        def step(d, _):
            body(d)
            return 0

        lax.fori_loop(1, stop, step, 0)

    def device(d):
        peer = (me + d) % 128
        return peer, (peer // 4, peer % 4)

    loop(128, lambda d: pl.semaphore_signal(barrier, inc=1, device_id=device(d)[1], device_id_type=MESH))

    def exchange(source, target, send, recv):
        def copy(d):
            peer, where = device(d)
            return pltpu.make_async_remote_copy(
                src_ref=source.at[peer], dst_ref=target.at[me], send_sem=send, recv_sem=recv,
                device_id=where, device_id_type=MESH,
            )

        loop(128, lambda d: copy(d).start())
        pltpu.make_async_copy(source.at[me], target.at[me], recv).start()

    def arrived(target, recv):
        pltpu.make_async_copy(target, target, recv).wait()

    def sent(source, send):
        some = source.at[pl.ds(0, 127)]
        pltpu.make_async_copy(some, some, send).wait()

    def to_blocks(part, block):
        for slot in range(2):
            stage[pl.ds(slot * 8 + part, 128, stride=16), :] = block[slot * 128 : slot * 128 + 128, :]

    def from_blocks(part):
        slots = [stage[pl.ds(slot * 8 + part, 128, stride=16), :] for slot in range(2)]
        return jnp.concatenate(slots, axis=0).astype(BF16)

    pick, unpick[...] = pickers(owners_ref, counts_ref[0])
    ids = ids_ref[...]
    lane_row = iota((ROWS, ROWS), 0)
    for slot in range(2):
        info = jnp.where(lane_row == 2 * slot, ids // 8, jnp.where(lane_row == 2 * slot + 1, ids % 8, 0))
        info = jnp.transpose(info.astype(F32)).astype(BF16)
        part = jnp.dot(pick[slot * 128 : slot * 128 + 128, :], info, preferred_element_type=F32)
        meta[...] = part if slot == 0 else meta[...] + part

    def spread(i, _):
        meta_out[i] = meta[pl.ds(i, 1), :]
        return 0

    lax.fori_loop(0, 128, spread, 0)
    for half in range(2):
        for part in range(8):
            lanes = slice((half * 8 + part) * 128, (half * 8 + part) * 128 + 128)
            to_blocks(part, jnp.dot(pick, bricks_ref[:, lanes], preferred_element_type=F32))
        brick_out[half] = stage[...].astype(BF16).reshape(128, 16, 128)
        if half == 0:
            pl.semaphore_wait(barrier, 127)
            exchange(meta_out, meta_in, meta_sem.at[0], meta_sem.at[1])
        exchange(brick_out.at[half], brick_in.at[half], brick_send.at[half], brick_recv.at[half])

    arrived(meta_in, meta_sem.at[1])

    def collect(i, _):
        meta[pl.ds(i, 1), :] = meta_in[i]
        return 0

    lax.fori_loop(0, 128, collect, 0)

    known = meta[...]
    meta_rows = jnp.transpose(known)
    q_row = jnp.concatenate([meta_rows[0:1, :], meta_rows[2:3, :]], axis=1).astype(jnp.int32)
    ty_row = jnp.concatenate([meta_rows[1:2, :], meta_rows[3:4, :]], axis=1).astype(jnp.int32)
    for p in range(2):
        for ty in range(4):
            hit = q_row == iota((64, SLOTS), 0)
            second = -1.0 if p else 1.0
            value = jnp.where(ty_row == ty, 1.0, 0.0) + jnp.where(ty_row == ty + 4, second, 0.0)
            first = (p * 4 + ty) * 64
            place[first : first + 64, :] = jnp.where(hit, value, 0.0).astype(BF16)
    low_half = iota((64, 128), 1) < 64

    def deposit(half):
        arrived(brick_in.at[half], brick_recv.at[half])
        stage[...] = brick_in[half].reshape(2048, 128).astype(F32)
        for part in range(8):
            tile = half * 8 + part
            iz, pair = tile // 4, tile % 4
            laid = jnp.dot(place[...], from_blocks(part), preferred_element_type=F32)
            for p in range(2):
                for side in range(2):
                    first = (p * 4 + side * 2) * 64
                    te, to = laid[first : first + 64, :], laid[first + 64 : first + 128, :]
                    even = jnp.where(low_half, te, pltpu.roll(to, 64, 1))
                    odd = jnp.where(low_half, pltpu.roll(te, 64, 1), to)
                    for k, value in enumerate((even, odd)):
                        row = (iz * 8 + pair * 2 + k) * 64
                        high, low = halves(value)
                        xhi[p, row : row + 64, side * 128 : side * 128 + 128] = high
                        xlo[p, row : row + 64, side * 128 : side * 128 + 128] = low

    def line_copies(iz, d, source, source_step, target, target_step, send, recv):
        peer = (m + d) % 4
        a = pltpu.make_async_remote_copy(
            src_ref=source.at[peer, iz], dst_ref=target.at[m, iz],
            send_sem=send.at[0, d - 1, iz], recv_sem=recv.at[0, d - 1, iz],
            device_id=line_peer(peer), device_id_type=MESH,
        )
        b = pltpu.make_async_remote_copy(
            src_ref=source_step.at[peer, iz], dst_ref=target_step.at[m, iz],
            send_sem=send.at[1, d - 1, iz], recv_sem=recv.at[1, d - 1, iz],
            device_id=line_peer(peer), device_id_type=MESH,
        )
        return a, b

    def own_copies(iz, which, source, source_step, target, target_step):
        a = pltpu.make_async_copy(source.at[m, iz], target.at[m, iz], own_sem.at[which, 0, iz])
        b = pltpu.make_async_copy(source_step.at[m, iz], target_step.at[m, iz], own_sem.at[which, 1, iz])
        return a, b

    forward = (sq, sstep, rq, rstep)
    for iz in range(4):
        if iz % 2 == 0:
            deposit(iz // 2)
        rows = slice(iz * 512, iz * 512 + 512)
        for p in range(2):
            value = three(xhi[p, rows, :], xlo[p, rows, :], yin_ref[p, 0], yin_ref[p, 1])
            code, step = coded(value)
            for h in range(2):
                sq[p * 2 + h, iz] = code[:, h * 128 : h * 128 + 128].reshape(8, 4, 16, 128)
                sstep[p * 2 + h, iz] = jnp.broadcast_to(step[:, h * 128 : h * 128 + 128], (8, 128))
        for d in range(1, 4):
            for copy in line_copies(iz, d, *forward, line_send, line_recv):
                copy.start()
        for copy in own_copies(iz, 0, *forward):
            copy.start()

    for iz in range(4):
        for d in range(1, 4):
            for copy in line_copies(iz, d, *forward, line_send, line_recv):
                copy.wait_recv()
        for copy in own_copies(iz, 0, *forward):
            copy.wait()
        for tz in range(0, 4, 2):
            lines = []
            for source in range(4):
                step = rstep[source, iz][0:1, :]
                planes = [decoded(rq[source, iz, :, z].reshape(128, 128), step) for z in (tz, tz + 1)]
                lines.append(jnp.concatenate(planes, axis=1))
            for p in range(2):
                if p == 0:
                    folded = jnp.concatenate([lines[0] + lines[2], lines[1] + lines[3]], axis=0)
                else:
                    folded = jnp.concatenate([lines[0] - lines[2], lines[1] - lines[3]], axis=0)
                high, low = halves(folded)
                value = three(xin_ref[p, 0], xin_ref[p, 1], high, low)
                for k in range(2):
                    spec[(tz + k) * 4 + iz, p * 256 : p * 256 + 256, :] = value[:, k * 128 : k * 128 + 128]

    def slab_ends(b, _):
        rows = pl.ds(pl.multiple_of(b * 16, 16), 16)
        rate = rates_ref[0, rows, :]
        planes = [spec[z, rows, :] for z in range(16)]
        right, left = planes[0], planes[15]
        for z in range(1, 16):
            right = right * rate + planes[z]
            left = left * rate + planes[15 - z]
        ends_out[b, 0] = right
        ends_out[b, 1] = left
        return 0

    lax.fori_loop(0, 32, slab_ends, 0)

    def slab_exchange(source, target, send, recv):
        def copy(d):
            peer = (slab + d) % 32
            return pltpu.make_async_remote_copy(
                src_ref=source.at[peer], dst_ref=target.at[slab], send_sem=send, recv_sem=recv,
                device_id=slab_peer(peer), device_id_type=MESH,
            )

        loop(32, lambda d: copy(d).start())
        pltpu.make_async_copy(source.at[slab], target.at[slab], recv).start()

    slab_exchange(ends_out, ends_in, ends_sem.at[0], ends_sem.at[1])
    arrived(ends_in, ends_sem.at[1])

    rate = rates_ref[0, pl.ds(pl.multiple_of(slab * 16, 16), 16), :]
    r2 = rate * rate
    r4 = r2 * r2
    r8 = r4 * r4
    hop = r8 * r8
    far = hop
    for _ in range(5):
        far = far * far
    far = far * rate
    zero = jnp.zeros((16, 128), F32)
    total_right, total_left = zero, zero
    for g in range(32):
        total_right = total_right * hop + ends_in[g, 0]
        total_left = total_left * hop + ends_in[31 - g, 1]
    scale = -rate / (1.0 - far * far)
    right = scale * (total_left - far * total_right)
    left = scale * (total_right - far * total_left)
    for g in range(32):
        carry_out[g, 0] = right
        carry_out[31 - g, 1] = left
        right = right * hop + ends_in[g, 0]
        left = left * hop + ends_in[31 - g, 1]

    slab_exchange(carry_out, carry_in, carry_sem.at[0], carry_sem.at[1])
    arrived(carry_in, carry_sem.at[1])

    def filters(b, _):
        rows = pl.ds(pl.multiple_of(b * 16, 16), 16)
        rate, gain = rates_ref[0, rows, :], rates_ref[1, rows, :]
        planes = [spec[z, rows, :] for z in range(16)]
        right, left = carry_in[b, 0], carry_in[b, 1]
        beyond = [None] * 16
        for z in range(15, -1, -1):
            beyond[z] = left * rate
            left = planes[z] + beyond[z]
        for z in range(16):
            right = planes[z] + right * rate
            high, low = halves((right + beyond[z]) * gain)
            mhi[z, rows, :] = high
            mlo[z, rows, :] = low
        return 0

    lax.fori_loop(0, 32, filters, 0)

    backward = (sq2, sstep2, rq2, rstep2)
    for iz in range(4):
        parts = []
        for tz in range(0, 4, 2):
            sums = []
            for p in range(2):
                rows = slice(p * 256, p * 256 + 256)
                high = jnp.concatenate([mhi[(tz + k) * 4 + iz, rows, :] for k in range(2)], axis=1)
                low = jnp.concatenate([mlo[(tz + k) * 4 + iz, rows, :] for k in range(2)], axis=1)
                sums.append(three(xout_ref[p, 0], xout_ref[p, 1], high, low))
            parts.append((sums[0] + sums[1], sums[0] - sums[1]))
        for target in range(4):
            span = slice((target % 2) * 128, (target % 2) * 128 + 128)
            blocks = []
            for tz in range(4):
                block = parts[tz // 2][target // 2][span, (tz % 2) * 128 : (tz % 2) * 128 + 128]
                blocks.append(block)
            top = blocks[0]
            for block in blocks:
                top = jnp.maximum(jnp.abs(top), jnp.abs(block))
            top = jnp.maximum(jnp.max(top, axis=0, keepdims=True), 1e-30)
            step = top * (1.0 / 32767.0)
            inverse = 1.0 / step
            for tz in range(4):
                code = jnp.round(blocks[tz] * inverse).astype(jnp.int32).astype(jnp.int16)
                sq2[target, iz, :, tz] = code.reshape(8, 16, 128)
            sstep2[target, iz] = jnp.broadcast_to(step, (8, 128))
        for d in range(1, 4):
            for copy in line_copies(iz, d, *backward, back_send, back_recv):
                copy.start()
        for copy in own_copies(iz, 1, *backward):
            copy.start()

    wanted = [
        (known[:, 2 * slot + 1 : 2 * slot + 2] * 64 + known[:, 2 * slot : 2 * slot + 1]).astype(jnp.int32)
        for slot in range(2)
    ]
    wanted = jnp.concatenate(wanted, axis=0)
    fetch[...] = jnp.where(iota((SLOTS, 512), 1) == wanted, 1.0, 0.0).astype(BF16)

    def reply(half):
        for part in range(8):
            lanes = slice((half * 8 + part) * 128, (half * 8 + part) * 128 + 128)
            to_blocks(part, jnp.dot(fetch[...], tiles[:, lanes], preferred_element_type=F32))
        reply_out[half] = stage[...].astype(BF16).reshape(128, 16, 128)
        exchange(reply_out.at[half], reply_in.at[half], reply_send.at[half], reply_recv.at[half])

    for iz in range(4):
        for d in range(1, 4):
            for copy in line_copies(iz, d, *backward, back_send, back_recv):
                copy.wait_recv()
        for copy in own_copies(iz, 1, *backward):
            copy.wait()
        sums = []
        for p in range(2):
            pieces = [
                decoded(rq2[p * 2 + h, iz].reshape(512, 128), rstep2[p * 2 + h, iz][0:1, :])
                for h in range(2)
            ]
            high, low = halves(jnp.concatenate(pieces, axis=1))
            sums.append(three(high, low, yout_ref[p, 0], yout_ref[p, 1]))
        for top, value in enumerate((sums[0] + sums[1], sums[0] - sums[1])):
            for half in range(2):
                lanes = slice(half * 128, half * 128 + 128)
                ty = top * 4 + half * 2
                for pair in range(4):
                    even = value[pair * 128 : pair * 128 + 64, lanes]
                    odd = value[pair * 128 + 64 : pair * 128 + 128, lanes]
                    span = slice((iz * 4 + pair) * 128, (iz * 4 + pair) * 128 + 128)
                    first = jnp.where(low_half, even, pltpu.roll(odd, 64, 1))
                    second = jnp.where(low_half, pltpu.roll(even, 64, 1), odd)
                    tiles[ty * 64 : ty * 64 + 64, span] = first.astype(BF16)
                    tiles[ty * 64 + 64 : ty * 64 + 128, span] = second.astype(BF16)
        if iz % 2 == 1:
            reply(iz // 2)

    for half in range(2):
        arrived(reply_in.at[half], reply_recv.at[half])
        stage[...] = reply_in[half].reshape(2048, 128).astype(F32)
        for part in range(8):
            lanes = slice((half * 8 + part) * 128, (half * 8 + part) * 128 + 128)
            out_ref[:, lanes] = jnp.dot(
                unpick[...], from_blocks(part), preferred_element_type=F32
            ).astype(BF16)

    sent(meta_out, meta_sem.at[0])
    for half in range(2):
        sent(brick_out.at[half], brick_send.at[half])
        sent(reply_out.at[half], reply_send.at[half])
    for source, sem in ((ends_out, ends_sem), (carry_out, carry_sem)):
        some = source.at[pl.ds(0, 31)]
        pltpu.make_async_copy(some, some, sem.at[0]).wait()
    for iz in range(4):
        for d in range(1, 4):
            for copy in line_copies(iz, d, *forward, line_send, line_recv):
                copy.wait_send()
            for copy in line_copies(iz, d, *backward, back_send, back_recv):
                copy.wait_send()


VMEM_LIMIT = 60 * 1024 * 1024


def on_device(bricks, owners, tile_ids, counts):
    gz, ma = lax.axis_index("gz"), lax.axis_index("ma")
    m = jnp.where(gz % 2 == 1, (gz // 2) % 4, ma)
    vmem = pl.BlockSpec(memory_space=pltpu.VMEM)
    smem = pl.BlockSpec(memory_space=pltpu.SMEM)
    rates = mode_rates(m)
    y_in, y_out, x_in, x_out = (jnp.asarray(t) for t in tables())
    codes = pltpu.VMEM((4, 4, 8, 4, 16, 128), jnp.int16)
    steps = pltpu.VMEM((4, 4, 8, 128), F32)
    share = pltpu.VMEM((32, 2, 16, 128), F32)
    blocks = pltpu.VMEM((2, 128, 16, 128), BF16)
    notes = pltpu.VMEM((128, 1, 128), F32)
    pair = pltpu.SemaphoreType.DMA((2,))
    line = pltpu.SemaphoreType.DMA((2, 3, 4))
    return pl.pallas_call(
        field_kernel,
        out_shape=jax.ShapeDtypeStruct((ROWS, CELLS), BF16),
        in_specs=[smem] + [vmem] * 8,
        out_specs=vmem,
        scratch_shapes=[
            pltpu.VMEM((2048, 128), F32),
            blocks, blocks, notes, notes,
            pltpu.VMEM((128, 128), F32),
            blocks, blocks,
            pltpu.VMEM((ROWS, SLOTS), BF16),
            pltpu.VMEM((SLOTS, 512), BF16),
            pltpu.VMEM((512, SLOTS), BF16),
            pltpu.VMEM((2, 2048, HALF), BF16),
            pltpu.VMEM((2, 2048, HALF), BF16),
            codes, steps, codes, steps,
            pltpu.VMEM((16, 512, 128), F32),
            share, share, share, share,
            pltpu.VMEM((16, 512, 128), BF16),
            pltpu.VMEM((16, 512, 128), BF16),
            codes, steps, codes, steps,
            pltpu.VMEM((512, CELLS), BF16),
            pair, pair, pair, pair, pair, line, line, pair, pair, line, line,
            pltpu.SemaphoreType.DMA((2, 2, 4)),
        ],
        compiler_params=pltpu.CompilerParams(
            collective_id=0, has_side_effects=True, vmem_limit_bytes=VMEM_LIMIT
        ),
        name="field",
    )(counts, bricks, owners, tile_ids.reshape(1, ROWS), rates, y_in, y_out, x_in, x_out)


def solution(mesh):
    in_specs = (P(("gz", "ma"), None), P(("gz", "ma"), None), P(("gz", "ma")), P(("gz", "ma")))
    out_specs = P(("gz", "ma"), None)
    return jax.shard_map(
        on_device, mesh=mesh, in_specs=in_specs, out_specs=out_specs, check_vma=False
    )
```

```python
import math

import jax
import jax.numpy as jnp
import ml_dtypes
import numpy as np
from jax import lax
from jax.experimental import pallas as pl
from jax.experimental.pallas import tpu as pltpu
from jax.sharding import PartitionSpec as P

N = 512
HALF = 256
SCREEN = 16
F32 = jnp.float32
BF16 = jnp.bfloat16
LOGICAL = pl.DeviceIdType.LOGICAL
SLOTS = 256
CELLS = 2048
ROWS = 128


def split_table(table):
    high = table.astype(ml_dtypes.bfloat16)
    low = (table - high.astype(np.float64)).astype(ml_dtypes.bfloat16)
    return high, low


def parity_table(parity, points):
    modes = 2 * np.arange(HALF) + parity
    angle = 2.0 * math.pi / N * ((modes[:, None] * points[None, :]) % N)
    return (np.cos(angle) + np.sin(angle)) / math.sqrt(N)


def stacked(tables):
    return np.stack([np.stack(split_table(t)) for t in tables])


def tables():
    natural = np.arange(HALF)
    m, ix, tx = np.meshgrid(np.arange(2), np.arange(8), np.arange(16), indexing="ij")
    order = (m * 128 + tx * 8 + ix).reshape(-1)
    y_tables = [parity_table(p, natural) for p in (0, 1)]
    x_tables = [parity_table(p, order) for p in (0, 1)]
    y_in = stacked([t.T for t in y_tables])
    y_out = stacked(y_tables)
    x_in = stacked(x_tables)
    x_out = stacked([t.T for t in x_tables])
    return y_in, y_out, x_in, x_out


def second_differences():
    k = np.arange(128)
    rows = [2 * (128 * (c % 2) + k) + c // 2 for c in range(4)]
    values = (4.0 * np.sin(math.pi / N * np.stack(rows)) ** 2).astype(np.float32)
    return np.concatenate([values, values])


def handler(owner):
    core = (owner // 4) % 2
    y, t, m = owner // 32, (owner // 8) % 4, owner % 4
    place = (m - t - y + 8) % 4
    return jnp.where(core == 1, y * 32 + place * 8 + 4 + t, y * 32 + t * 8 + place)


def iota(shape, axis):
    return lax.broadcasted_iota(jnp.int32, shape, axis)


def pickers(owners_ref, count):
    row = jnp.broadcast_to(handler(owners_ref[...]), (ROWS, ROWS))
    column = jnp.transpose(row.astype(F32)).astype(jnp.int32)
    target = column[:, 0:1]
    same = column == row
    i, j = iota((ROWS, ROWS), 0), iota((ROWS, ROWS), 1)
    within_column = jnp.sum(jnp.where(same & (j < i), 1.0, 0.0), axis=1, keepdims=True)
    within_row = jnp.sum(jnp.where(same & (i < j), 1.0, 0.0), axis=0, keepdims=True)
    slot_column = target + ROWS * within_column.astype(jnp.int32)
    slot_row = row[0:1, :] + ROWS * within_row.astype(jnp.int32)
    down = (iota((SLOTS, ROWS), 0) == slot_row) & (iota((SLOTS, ROWS), 1) < count)
    across = (iota((ROWS, SLOTS), 1) == slot_column) & (iota((ROWS, SLOTS), 0) < count)
    return jnp.where(down, 1.0, 0.0).astype(BF16), jnp.where(across, 1.0, 0.0).astype(BF16)


def halves(value):
    high = value.astype(BF16)
    return high, (value - high.astype(F32)).astype(BF16)


def three(a_high, a_low, b_high, b_low):
    total = jnp.dot(a_high, b_high, preferred_element_type=F32)
    total += jnp.dot(a_high, b_low, preferred_element_type=F32)
    total += jnp.dot(a_low, b_high, preferred_element_type=F32)
    return total


def coded(value):
    top = jnp.max(jnp.abs(value), axis=0, keepdims=True)
    step = jnp.maximum(top, 1e-30) * (1.0 / 32767.0)
    return jnp.round(value * (1.0 / step)).astype(jnp.int32).astype(jnp.int16), step


def decoded(code, step):
    return code.astype(jnp.int32).astype(F32) * step


def field_kernel(
    counts_ref, bricks_ref, owners_ref, ids_ref, lam_ref, yin_hbm, yout_hbm, xin_hbm, xout_hbm, out_ref,
    rates_ref, yin_ref, yout_ref, xin_ref, xout_ref, table_sem,
    stage, brick_out, brick_in, meta_out, meta_in, meta, reply_out, reply_in, unpick, fetch, place, xhi, xlo, sq, sstep, rq, rstep, spec, ends_out, ends_in, carry_out, carry_in,
    mhi, mlo, sq2, sstep2, rq2, rstep2, tiles,
    brick_send, brick_recv, meta_sem, reply_send, reply_recv, line_send, line_recv, ends_sem, carry_sem, back_send, back_recv, own_sem,
):
    gz, ma = lax.axis_index("gz"), lax.axis_index("ma")
    y, x, core = gz // 8, (gz // 2) % 4, gz % 2
    me = gz * 4 + ma
    m = (x + y + ma) % 4
    t = core * ma + (1 - core) * x
    slab = y * 8 + t * 2 + core

    def wrap(value, size):
        return jnp.where(value >= size, value - size, value)

    def line_peer(p):
        place = (p - t - y + 8) % 4
        return y * 32 + core * (place * 8 + 4 + t) + (1 - core) * (t * 8 + place)

    def slab_peers():
        for dy in range(4):
            py = wrap(y + dy, 4)
            for dt in range(4):
                pt = wrap(t + dt, 4)
                place = (m - pt - py + 8) % 4
                for dc in range(2):
                    if dy or dt or dc:
                        pc = core if dc == 0 else 1 - core
                        where = py * 32 + jnp.where(pc == 1, place * 8 + 4 + pt, pt * 8 + place)
                        yield py * 8 + pt * 2 + pc, where

    def peers(body):
        def step(i, _):
            for k in range(8):
                body(wrap(me + (i * 8 + k + 1), 128))
            return 0

        lax.fori_loop(0, 15, step, 0)
        for d in range(121, 128):
            body(wrap(me + d, 128))

    tables = ((yin_hbm, yin_ref), (xin_hbm, xin_ref), (xout_hbm, xout_ref), (yout_hbm, yout_ref))
    for i, (source, target) in enumerate(tables):
        pltpu.make_async_copy(source, target, table_sem.at[i]).start()

    def have_table(i):
        pltpu.make_async_copy(*tables[i], table_sem.at[i]).wait()

    barrier = pltpu.get_barrier_semaphore()
    peers(lambda n: pl.semaphore_signal(barrier, inc=1, device_id=n, device_id_type=LOGICAL))

    def exchange(source, target, send, recv):
        def start(n):
            pltpu.make_async_remote_copy(
                src_ref=source.at[n], dst_ref=target.at[me], send_sem=send, recv_sem=recv,
                device_id=n, device_id_type=LOGICAL,
            ).start()

        peers(start)
        pltpu.make_async_copy(source.at[me], target.at[me], recv).start()

    def arrived(target, recv):
        pltpu.make_async_copy(target, target, recv).wait()

    def sent(source, send):
        some = source.at[pl.ds(0, 127)]
        pltpu.make_async_copy(some, some, send).wait()

    def to_blocks(part, block):
        for slot in range(2):
            stage[pl.ds(slot * 8 + part, 128, stride=16), :] = block[slot * 128 : slot * 128 + 128, :]

    def from_blocks(part):
        slots = [stage[pl.ds(slot * 8 + part, 128, stride=16), :] for slot in range(2)]
        return jnp.concatenate(slots, axis=0).astype(BF16)

    pick, unpick[...] = pickers(owners_ref, counts_ref[0])
    ids = ids_ref[...]
    lane_row = iota((ROWS, ROWS), 0)
    for slot in range(2):
        info = jnp.where(lane_row == 2 * slot, ids // 8, jnp.where(lane_row == 2 * slot + 1, ids % 8, 0))
        info = jnp.transpose(info.astype(F32)).astype(BF16)
        part = jnp.dot(pick[slot * 128 : slot * 128 + 128, :], info, preferred_element_type=F32)
        meta[...] = part if slot == 0 else meta[...] + part

    def spread(i, _):
        meta_out[i] = meta[pl.ds(i, 1), :]
        return 0

    lax.fori_loop(0, 128, spread, 0)
    for half in range(2):
        for part in range(8):
            lanes = slice((half * 8 + part) * 128, (half * 8 + part) * 128 + 128)
            to_blocks(part, jnp.dot(pick, bricks_ref[:, lanes], preferred_element_type=F32))
        brick_out[half] = stage[...].astype(BF16).reshape(128, 16, 128)
        if half == 0:
            pl.semaphore_wait(barrier, 127)
        exchange(brick_out.at[half], brick_in.at[half], brick_send.at[half], brick_recv.at[half])
        if half == 0:
            exchange(meta_out, meta_in, meta_sem.at[0], meta_sem.at[1])

    lam_k = lam_ref[pl.ds(4 + m, 1), :]
    for block in range(4):
        lam_j = jnp.transpose(jnp.broadcast_to(lam_ref[block : block + 1, :], (128, 128)))
        excess = 1.0 / (SCREEN * SCREEN) + lam_j + lam_k
        root = jnp.sqrt(excess * (excess + 4.0))
        rates_ref[0, block * 128 : block * 128 + 128, :] = 2.0 / (2.0 + excess + root)
        rates_ref[1, block * 128 : block * 128 + 128, :] = 1.0 / root

    arrived(meta_in, meta_sem.at[1])

    def collect(i, _):
        meta[pl.ds(i, 1), :] = meta_in[i]
        return 0

    lax.fori_loop(0, 128, collect, 0)

    known = meta[...]
    meta_rows = jnp.transpose(known)
    q_row = jnp.concatenate([meta_rows[0:1, :], meta_rows[2:3, :]], axis=1).astype(jnp.int32)
    ty_row = jnp.concatenate([meta_rows[1:2, :], meta_rows[3:4, :]], axis=1).astype(jnp.int32)
    for p in range(2):
        for ty in range(4):
            hit = q_row == iota((64, SLOTS), 0)
            second = -1.0 if p else 1.0
            value = jnp.where(ty_row == ty, 1.0, 0.0) + jnp.where(ty_row == ty + 4, second, 0.0)
            first = (p * 4 + ty) * 64
            place[first : first + 64, :] = jnp.where(hit, value, 0.0).astype(BF16)
    low_half = iota((64, 128), 1) < 64

    def deposit(half):
        arrived(brick_in.at[half], brick_recv.at[half])
        stage[...] = brick_in[half].reshape(2048, 128).astype(F32)
        for part in range(8):
            tile = half * 8 + part
            iz, pair = tile // 4, tile % 4
            laid = jnp.dot(place[...], from_blocks(part), preferred_element_type=F32)
            for p in range(2):
                for side in range(2):
                    first = (p * 4 + side * 2) * 64
                    te, to = laid[first : first + 64, :], laid[first + 64 : first + 128, :]
                    even = jnp.where(low_half, te, pltpu.roll(to, 64, 1))
                    odd = jnp.where(low_half, pltpu.roll(te, 64, 1), to)
                    for k, value in enumerate((even, odd)):
                        row = (iz * 8 + pair * 2 + k) * 64
                        high, low = halves(value)
                        xhi[p, row : row + 64, side * 128 : side * 128 + 128] = high
                        xlo[p, row : row + 64, side * 128 : side * 128 + 128] = low

    def line_copies(iz, d, source, source_step, target, target_step, send, recv):
        peer = (m + d) % 4
        a = pltpu.make_async_remote_copy(
            src_ref=source.at[peer, iz], dst_ref=target.at[m, iz],
            send_sem=send.at[0, d - 1, iz], recv_sem=recv.at[0, d - 1, iz],
            device_id=line_peer(peer), device_id_type=LOGICAL,
        )
        b = pltpu.make_async_remote_copy(
            src_ref=source_step.at[peer, iz], dst_ref=target_step.at[m, iz],
            send_sem=send.at[1, d - 1, iz], recv_sem=recv.at[1, d - 1, iz],
            device_id=line_peer(peer), device_id_type=LOGICAL,
        )
        return a, b

    def own_copies(iz, which, source, source_step, target, target_step):
        a = pltpu.make_async_copy(source.at[m, iz], target.at[m, iz], own_sem.at[which, 0, iz])
        b = pltpu.make_async_copy(source_step.at[m, iz], target_step.at[m, iz], own_sem.at[which, 1, iz])
        return a, b

    have_table(0)
    forward = (sq, sstep, rq, rstep)
    for iz in range(4):
        if iz % 2 == 0:
            deposit(iz // 2)
        rows = slice(iz * 512, iz * 512 + 512)
        for p in range(2):
            value = three(xhi[p, rows, :], xlo[p, rows, :], yin_ref[p, 0], yin_ref[p, 1])
            code, step = coded(value)
            for h in range(2):
                sq[p * 2 + h, iz] = code[:, h * 128 : h * 128 + 128].reshape(8, 4, 16, 128)
                sstep[p * 2 + h, iz] = jnp.broadcast_to(step[:, h * 128 : h * 128 + 128], (8, 128))
        for d in range(1, 4):
            for copy in line_copies(iz, d, *forward, line_send, line_recv):
                copy.start()
        for copy in own_copies(iz, 0, *forward):
            copy.start()

    have_table(1)
    for iz in range(4):
        for d in range(1, 4):
            for copy in line_copies(iz, d, *forward, line_send, line_recv):
                copy.wait_recv()
        for copy in own_copies(iz, 0, *forward):
            copy.wait()
        for tz in range(0, 4, 2):
            lines = []
            for source in range(4):
                step = rstep[source, iz][0:1, :]
                planes = [decoded(rq[source, iz, :, z].reshape(128, 128), step) for z in (tz, tz + 1)]
                lines.append(jnp.concatenate(planes, axis=1))
            for p in range(2):
                if p == 0:
                    folded = jnp.concatenate([lines[0] + lines[2], lines[1] + lines[3]], axis=0)
                else:
                    folded = jnp.concatenate([lines[0] - lines[2], lines[1] - lines[3]], axis=0)
                high, low = halves(folded)
                value = three(xin_ref[p, 0], xin_ref[p, 1], high, low)
                for k in range(2):
                    spec[(tz + k) * 4 + iz, p * 256 : p * 256 + 256, :] = value[:, k * 128 : k * 128 + 128]

    def slab_ends(b, _):
        rows = pl.ds(pl.multiple_of(b * 16, 16), 16)
        rate = rates_ref[0, rows, :]
        planes = [spec[z, rows, :] for z in range(16)]
        right, left = planes[0], planes[15]
        for z in range(1, 16):
            right = right * rate + planes[z]
            left = left * rate + planes[15 - z]
        ends_out[b, 0] = right
        ends_out[b, 1] = left
        return 0

    lax.fori_loop(0, 32, slab_ends, 0)

    def slab_exchange(source, target, send, recv):
        for peer, where in slab_peers():
            pltpu.make_async_remote_copy(
                src_ref=source.at[peer], dst_ref=target.at[slab], send_sem=send, recv_sem=recv,
                device_id=where, device_id_type=LOGICAL,
            ).start()
        pltpu.make_async_copy(source.at[slab], target.at[slab], recv).start()

    slab_exchange(ends_out, ends_in, ends_sem.at[0], ends_sem.at[1])
    arrived(ends_in, ends_sem.at[1])

    rate = rates_ref[0, pl.ds(pl.multiple_of(slab * 16, 16), 16), :]
    r2 = rate * rate
    r4 = r2 * r2
    r8 = r4 * r4
    hop = r8 * r8
    far = hop
    for _ in range(5):
        far = far * far
    far = far * rate
    zero = jnp.zeros((16, 128), F32)
    total_right, total_left = zero, zero
    for g in range(32):
        total_right = total_right * hop + ends_in[g, 0]
        total_left = total_left * hop + ends_in[31 - g, 1]
    scale = -rate / (1.0 - far * far)
    right = scale * (total_left - far * total_right)
    left = scale * (total_right - far * total_left)
    for g in range(32):
        carry_out[g, 0] = right
        carry_out[31 - g, 1] = left
        right = right * hop + ends_in[g, 0]
        left = left * hop + ends_in[31 - g, 1]

    slab_exchange(carry_out, carry_in, carry_sem.at[0], carry_sem.at[1])
    arrived(carry_in, carry_sem.at[1])

    def filters(b, _):
        rows = pl.ds(pl.multiple_of(b * 16, 16), 16)
        rate, gain = rates_ref[0, rows, :], rates_ref[1, rows, :]
        planes = [spec[z, rows, :] for z in range(16)]
        right, left = carry_in[b, 0], carry_in[b, 1]
        beyond = [None] * 16
        for z in range(15, -1, -1):
            beyond[z] = left * rate
            left = planes[z] + beyond[z]
        for z in range(16):
            right = planes[z] + right * rate
            high, low = halves((right + beyond[z]) * gain)
            mhi[z, rows, :] = high
            mlo[z, rows, :] = low
        return 0

    lax.fori_loop(0, 32, filters, 0)

    have_table(2)
    backward = (sq2, sstep2, rq2, rstep2)
    for iz in range(4):
        parts = []
        for tz in range(0, 4, 2):
            sums = []
            for p in range(2):
                rows = slice(p * 256, p * 256 + 256)
                high = jnp.concatenate([mhi[(tz + k) * 4 + iz, rows, :] for k in range(2)], axis=1)
                low = jnp.concatenate([mlo[(tz + k) * 4 + iz, rows, :] for k in range(2)], axis=1)
                sums.append(three(xout_ref[p, 0], xout_ref[p, 1], high, low))
            parts.append((sums[0] + sums[1], sums[0] - sums[1]))
        for target in range(4):
            span = slice((target % 2) * 128, (target % 2) * 128 + 128)
            blocks = []
            for tz in range(4):
                block = parts[tz // 2][target // 2][span, (tz % 2) * 128 : (tz % 2) * 128 + 128]
                blocks.append(block)
            top = blocks[0]
            for block in blocks:
                top = jnp.maximum(jnp.abs(top), jnp.abs(block))
            top = jnp.maximum(jnp.max(top, axis=0, keepdims=True), 1e-30)
            step = top * (1.0 / 32767.0)
            inverse = 1.0 / step
            for tz in range(4):
                code = jnp.round(blocks[tz] * inverse).astype(jnp.int32).astype(jnp.int16)
                sq2[target, iz, :, tz] = code.reshape(8, 16, 128)
            sstep2[target, iz] = jnp.broadcast_to(step, (8, 128))
        for d in range(1, 4):
            for copy in line_copies(iz, d, *backward, back_send, back_recv):
                copy.start()
        for copy in own_copies(iz, 1, *backward):
            copy.start()

    wanted = [
        (known[:, 2 * slot + 1 : 2 * slot + 2] * 64 + known[:, 2 * slot : 2 * slot + 1]).astype(jnp.int32)
        for slot in range(2)
    ]
    wanted = jnp.concatenate(wanted, axis=0)
    fetch[...] = jnp.where(iota((SLOTS, 512), 1) == wanted, 1.0, 0.0).astype(BF16)

    def reply(half):
        for part in range(8):
            lanes = slice((half * 8 + part) * 128, (half * 8 + part) * 128 + 128)
            to_blocks(part, jnp.dot(fetch[...], tiles[:, lanes], preferred_element_type=F32))
        reply_out[half] = stage[...].astype(BF16).reshape(128, 16, 128)
        exchange(reply_out.at[half], reply_in.at[half], reply_send.at[half], reply_recv.at[half])

    have_table(3)
    for iz in range(4):
        for d in range(1, 4):
            for copy in line_copies(iz, d, *backward, back_send, back_recv):
                copy.wait_recv()
        for copy in own_copies(iz, 1, *backward):
            copy.wait()
        sums = []
        for p in range(2):
            pieces = [
                decoded(rq2[p * 2 + h, iz].reshape(512, 128), rstep2[p * 2 + h, iz][0:1, :])
                for h in range(2)
            ]
            high, low = halves(jnp.concatenate(pieces, axis=1))
            sums.append(three(high, low, yout_ref[p, 0], yout_ref[p, 1]))
        for top, value in enumerate((sums[0] + sums[1], sums[0] - sums[1])):
            for half in range(2):
                lanes = slice(half * 128, half * 128 + 128)
                ty = top * 4 + half * 2
                for pair in range(4):
                    even = value[pair * 128 : pair * 128 + 64, lanes]
                    odd = value[pair * 128 + 64 : pair * 128 + 128, lanes]
                    span = slice((iz * 4 + pair) * 128, (iz * 4 + pair) * 128 + 128)
                    first = jnp.where(low_half, even, pltpu.roll(odd, 64, 1))
                    second = jnp.where(low_half, pltpu.roll(even, 64, 1), odd)
                    tiles[ty * 64 : ty * 64 + 64, span] = first.astype(BF16)
                    tiles[ty * 64 + 64 : ty * 64 + 128, span] = second.astype(BF16)
        if iz % 2 == 1:
            reply(iz // 2)

    for half in range(2):
        arrived(reply_in.at[half], reply_recv.at[half])
        stage[...] = reply_in[half].reshape(2048, 128).astype(F32)
        for part in range(8):
            lanes = slice((half * 8 + part) * 128, (half * 8 + part) * 128 + 128)
            out_ref[:, lanes] = jnp.dot(
                unpick[...], from_blocks(part), preferred_element_type=F32
            ).astype(BF16)

    sent(meta_out, meta_sem.at[0])
    for half in range(2):
        sent(brick_out.at[half], brick_send.at[half])
        sent(reply_out.at[half], reply_send.at[half])
    for source, sem in ((ends_out, ends_sem), (carry_out, carry_sem)):
        some = source.at[pl.ds(0, 31)]
        pltpu.make_async_copy(some, some, sem.at[0]).wait()
    for iz in range(4):
        for d in range(1, 4):
            for copy in line_copies(iz, d, *forward, line_send, line_recv):
                copy.wait_send()
            for copy in line_copies(iz, d, *backward, back_send, back_recv):
                copy.wait_send()


VMEM_LIMIT = 60 * 1024 * 1024


def on_device(bricks, owners, tile_ids, counts):
    vmem = pl.BlockSpec(memory_space=pltpu.VMEM)
    smem = pl.BlockSpec(memory_space=pltpu.SMEM)
    y_in, y_out, x_in, x_out = (jnp.asarray(t) for t in tables())
    codes = pltpu.VMEM((4, 4, 8, 4, 16, 128), jnp.int16)
    steps = pltpu.VMEM((4, 4, 8, 128), F32)
    share = pltpu.VMEM((32, 2, 16, 128), F32)
    blocks = pltpu.VMEM((2, 128, 16, 128), BF16)
    table = pltpu.VMEM((2, 2, HALF, HALF), BF16)
    notes = pltpu.VMEM((128, 1, 128), F32)
    pair = pltpu.SemaphoreType.DMA((2,))
    line = pltpu.SemaphoreType.DMA((2, 3, 4))
    return pl.pallas_call(
        field_kernel,
        out_shape=jax.ShapeDtypeStruct((ROWS, CELLS), BF16),
        in_specs=[smem] + [vmem] * 4 + [pl.BlockSpec(memory_space=pl.ANY)] * 4,
        out_specs=vmem,
        scratch_shapes=[
            pltpu.VMEM((2, 512, 128), F32),
            table, table, table, table,
            pltpu.SemaphoreType.DMA((4,)),
            pltpu.VMEM((2048, 128), F32),
            blocks, blocks, notes, notes,
            pltpu.VMEM((128, 128), F32),
            blocks, blocks,
            pltpu.VMEM((ROWS, SLOTS), BF16),
            pltpu.VMEM((SLOTS, 512), BF16),
            pltpu.VMEM((512, SLOTS), BF16),
            pltpu.VMEM((2, 2048, HALF), BF16),
            pltpu.VMEM((2, 2048, HALF), BF16),
            codes, steps, codes, steps,
            pltpu.VMEM((16, 512, 128), F32),
            share, share, share, share,
            pltpu.VMEM((16, 512, 128), BF16),
            pltpu.VMEM((16, 512, 128), BF16),
            codes, steps, codes, steps,
            pltpu.VMEM((512, CELLS), BF16),
            pair, pair, pair, pair, pair, line, line, pair, pair, line, line,
            pltpu.SemaphoreType.DMA((2, 2, 4)),
        ],
        compiler_params=pltpu.CompilerParams(
            collective_id=0, has_side_effects=True, vmem_limit_bytes=VMEM_LIMIT
        ),
        name="field",
    )(counts, bricks, owners.reshape(1, ROWS), tile_ids.reshape(1, ROWS), jnp.asarray(second_differences()), y_in, y_out, x_in, x_out)


def solution(mesh):
    in_specs = (P(("gz", "ma"), None), P(("gz", "ma"), None), P(("gz", "ma")), P(("gz", "ma")))
    out_specs = P(("gz", "ma"), None)
    return jax.shard_map(
        on_device, mesh=mesh, in_specs=in_specs, out_specs=out_specs, check_vma=False
    )
```

```python
import math

import jax
import jax.numpy as jnp
import ml_dtypes
import numpy as np
from jax import lax
from jax.experimental import pallas as pl
from jax.experimental.pallas import tpu as pltpu
from jax.sharding import PartitionSpec as P

N = 512
HALF = 256
SCREEN = 16
F32 = jnp.float32
BF16 = jnp.bfloat16
LOGICAL = pl.DeviceIdType.LOGICAL
SLOTS = 256
CELLS = 2048
ROWS = 128


def split_table(table):
    high = table.astype(ml_dtypes.bfloat16)
    low = (table - high.astype(np.float64)).astype(ml_dtypes.bfloat16)
    return high, low


def parity_table(parity, points):
    modes = 2 * np.arange(HALF) + parity
    angle = 2.0 * math.pi / N * ((modes[:, None] * points[None, :]) % N)
    return (np.cos(angle) + np.sin(angle)) / math.sqrt(N)


def stacked(tables):
    return np.stack([np.stack(split_table(t)) for t in tables])


def tables():
    natural = np.arange(HALF)
    m, ix, tx = np.meshgrid(np.arange(2), np.arange(8), np.arange(16), indexing="ij")
    order = (m * 128 + tx * 8 + ix).reshape(-1)
    y_tables = [parity_table(p, natural) for p in (0, 1)]
    x_tables = [parity_table(p, order) for p in (0, 1)]
    y_in = stacked([t.T for t in y_tables])
    y_out = stacked(y_tables)
    x_in = stacked(x_tables)
    x_out = stacked([t.T for t in x_tables])
    return y_in, y_out, x_in, x_out


def second_differences():
    k = np.arange(128)
    rows = [2 * (128 * (c % 2) + k) + c // 2 for c in range(4)]
    values = (4.0 * np.sin(math.pi / N * np.stack(rows)) ** 2).astype(np.float32)
    return np.concatenate([values, values])


def handler(owner):
    core = (owner // 4) % 2
    y, t, m = owner // 32, (owner // 8) % 4, owner % 4
    place = (m - t - y + 8) % 4
    return jnp.where(core == 1, y * 32 + place * 8 + 4 + t, y * 32 + t * 8 + place)


def iota(shape, axis):
    return lax.broadcasted_iota(jnp.int32, shape, axis)


def pickers(owners_ref, count):
    row = jnp.broadcast_to(handler(owners_ref[...]), (ROWS, ROWS))
    column = jnp.transpose(row.astype(F32)).astype(jnp.int32)
    target = column[:, 0:1]
    same = column == row
    i, j = iota((ROWS, ROWS), 0), iota((ROWS, ROWS), 1)
    within_column = jnp.sum(jnp.where(same & (j < i), 1.0, 0.0), axis=1, keepdims=True)
    within_row = jnp.sum(jnp.where(same & (i < j), 1.0, 0.0), axis=0, keepdims=True)
    slot_column = target + ROWS * within_column.astype(jnp.int32)
    slot_row = row[0:1, :] + ROWS * within_row.astype(jnp.int32)
    down = (iota((SLOTS, ROWS), 0) == slot_row) & (iota((SLOTS, ROWS), 1) < count)
    across = (iota((ROWS, SLOTS), 1) == slot_column) & (iota((ROWS, SLOTS), 0) < count)
    return jnp.where(down, 1.0, 0.0).astype(BF16), jnp.where(across, 1.0, 0.0).astype(BF16)


def halves(value):
    high = value.astype(BF16)
    return high, (value - high.astype(F32)).astype(BF16)


def three(a_high, a_low, b_high, b_low):
    total = jnp.dot(a_high, b_high, preferred_element_type=F32)
    total += jnp.dot(a_high, b_low, preferred_element_type=F32)
    total += jnp.dot(a_low, b_high, preferred_element_type=F32)
    return total


def coded(value):
    top = jnp.max(jnp.abs(value), axis=0, keepdims=True)
    step = jnp.maximum(top, 1e-30) * (1.0 / 32767.0)
    return jnp.round(value * (1.0 / step)).astype(jnp.int32).astype(jnp.int16), step


def decoded(code, step):
    return code.astype(jnp.int32).astype(F32) * step


def field_kernel(
    counts_ref, bricks_ref, owners_ref, ids_ref, lam_ref, yin_hbm, yout_hbm, xin_hbm, xout_hbm, out_ref,
    rates_ref, yin_ref, yout_ref, xin_ref, xout_ref, table_sem,
    stage, brick_out, brick_in, meta_out, meta_in, meta, reply_out, reply_in, unpick, fetch, place, xhi, xlo, sq, sstep, rq, rstep, spec, last, known_ends, known_carry,
    ends_out, ends_in, carry_out, carry_in, ends_step_out, ends_step_in, carry_step_out, carry_step_in,
    mhi, mlo, sq2, sstep2, rq2, rstep2, tiles,
    brick_send, brick_recv, meta_sem, reply_send, reply_recv, line_send, line_recv, ends_sem, carry_sem, ends_step_sem, carry_step_sem, back_send, back_recv, own_sem,
):
    gz, ma = lax.axis_index("gz"), lax.axis_index("ma")
    y, x, core = gz // 8, (gz // 2) % 4, gz % 2
    me = gz * 4 + ma
    m = (x + y + ma) % 4
    t = core * ma + (1 - core) * x
    slab = y * 8 + t * 2 + core

    def wrap(value, size):
        return jnp.where(value >= size, value - size, value)

    def line_peer(p):
        place = (p - t - y + 8) % 4
        return y * 32 + core * (place * 8 + 4 + t) + (1 - core) * (t * 8 + place)

    def slab_peers():
        for dy in range(4):
            py = wrap(y + dy, 4)
            for dt in range(4):
                pt = wrap(t + dt, 4)
                place = (m - pt - py + 8) % 4
                for dc in range(2):
                    if dy or dt or dc:
                        pc = core if dc == 0 else 1 - core
                        where = py * 32 + jnp.where(pc == 1, place * 8 + 4 + pt, pt * 8 + place)
                        yield py * 8 + pt * 2 + pc, where

    def peers(body):
        def step(i, _):
            for k in range(8):
                body(wrap(me + (i * 8 + k + 1), 128))
            return 0

        lax.fori_loop(0, 15, step, 0)
        for d in range(121, 128):
            body(wrap(me + d, 128))

    tables = ((yin_hbm, yin_ref), (xin_hbm, xin_ref), (xout_hbm, xout_ref), (yout_hbm, yout_ref))
    for i, (source, target) in enumerate(tables):
        pltpu.make_async_copy(source, target, table_sem.at[i]).start()

    def have_table(i):
        pltpu.make_async_copy(*tables[i], table_sem.at[i]).wait()

    barrier = pltpu.get_barrier_semaphore()
    peers(lambda n: pl.semaphore_signal(barrier, inc=1, device_id=n, device_id_type=LOGICAL))

    def exchange(source, target, send, recv):
        def start(n):
            pltpu.make_async_remote_copy(
                src_ref=source.at[n], dst_ref=target.at[me], send_sem=send, recv_sem=recv,
                device_id=n, device_id_type=LOGICAL,
            ).start()

        peers(start)
        pltpu.make_async_copy(source.at[me], target.at[me], recv).start()

    def arrived(target, recv):
        pltpu.make_async_copy(target, target, recv).wait()

    def sent(source, send):
        some = source.at[pl.ds(0, 127)]
        pltpu.make_async_copy(some, some, send).wait()

    def to_blocks(part, block):
        for slot in range(2):
            stage[pl.ds(slot * 8 + part, 128, stride=16), :] = block[slot * 128 : slot * 128 + 128, :]

    def from_blocks(part):
        slots = [stage[pl.ds(slot * 8 + part, 128, stride=16), :] for slot in range(2)]
        return jnp.concatenate(slots, axis=0).astype(BF16)

    pick, unpick[...] = pickers(owners_ref, counts_ref[0])
    ids = ids_ref[...]
    lane_row = iota((ROWS, ROWS), 0)
    for slot in range(2):
        info = jnp.where(lane_row == 2 * slot, ids // 8, jnp.where(lane_row == 2 * slot + 1, ids % 8, 0))
        info = jnp.transpose(info.astype(F32)).astype(BF16)
        part = jnp.dot(pick[slot * 128 : slot * 128 + 128, :], info, preferred_element_type=F32)
        meta[...] = part if slot == 0 else meta[...] + part

    def spread(i, _):
        meta_out[i] = meta[pl.ds(i, 1), :]
        return 0

    lax.fori_loop(0, 128, spread, 0)
    for half in range(2):
        for part in range(8):
            lanes = slice((half * 8 + part) * 128, (half * 8 + part) * 128 + 128)
            to_blocks(part, jnp.dot(pick, bricks_ref[:, lanes], preferred_element_type=F32))
        brick_out[half] = stage[...].astype(BF16).reshape(128, 16, 128)
    lam_k = lam_ref[pl.ds(4 + m, 1), :]
    for block in range(4):
        lam_j = jnp.transpose(jnp.broadcast_to(lam_ref[block : block + 1, :], (128, 128)))
        excess = 1.0 / (SCREEN * SCREEN) + lam_j + lam_k
        root = jnp.sqrt(excess * (excess + 4.0))
        rates_ref[0, block * 128 : block * 128 + 128, :] = 2.0 / (2.0 + excess + root)
        rates_ref[1, block * 128 : block * 128 + 128, :] = 1.0 / root

    pl.semaphore_wait(barrier, 127)
    exchange(brick_out.at[0], brick_in.at[0], brick_send.at[0], brick_recv.at[0])
    exchange(meta_out, meta_in, meta_sem.at[0], meta_sem.at[1])
    exchange(brick_out.at[1], brick_in.at[1], brick_send.at[1], brick_recv.at[1])
    arrived(meta_in, meta_sem.at[1])

    def collect(i, _):
        meta[pl.ds(i, 1), :] = meta_in[i]
        return 0

    lax.fori_loop(0, 128, collect, 0)

    known = meta[...]
    meta_rows = jnp.transpose(known)
    q_row = jnp.concatenate([meta_rows[0:1, :], meta_rows[2:3, :]], axis=1).astype(jnp.int32)
    ty_row = jnp.concatenate([meta_rows[1:2, :], meta_rows[3:4, :]], axis=1).astype(jnp.int32)
    for p in range(2):
        for ty in range(4):
            hit = q_row == iota((64, SLOTS), 0)
            second = -1.0 if p else 1.0
            value = jnp.where(ty_row == ty, 1.0, 0.0) + jnp.where(ty_row == ty + 4, second, 0.0)
            first = (p * 4 + ty) * 64
            place[first : first + 64, :] = jnp.where(hit, value, 0.0).astype(BF16)
    low_half = iota((64, 128), 1) < 64

    def deposit(half):
        arrived(brick_in.at[half], brick_recv.at[half])
        stage[...] = brick_in[half].reshape(2048, 128).astype(F32)
        for part in range(8):
            tile = half * 8 + part
            iz, pair = tile // 4, tile % 4
            laid = jnp.dot(place[...], from_blocks(part), preferred_element_type=F32)
            for p in range(2):
                for side in range(2):
                    first = (p * 4 + side * 2) * 64
                    te, to = laid[first : first + 64, :], laid[first + 64 : first + 128, :]
                    even = jnp.where(low_half, te, pltpu.roll(to, 64, 1))
                    odd = jnp.where(low_half, pltpu.roll(te, 64, 1), to)
                    for k, value in enumerate((even, odd)):
                        row = (iz * 8 + pair * 2 + k) * 64
                        high, low = halves(value)
                        xhi[p, row : row + 64, side * 128 : side * 128 + 128] = high
                        xlo[p, row : row + 64, side * 128 : side * 128 + 128] = low

    def line_copies(iz, d, source, source_step, target, target_step, send, recv):
        peer = (m + d) % 4
        a = pltpu.make_async_remote_copy(
            src_ref=source.at[peer, iz], dst_ref=target.at[m, iz],
            send_sem=send.at[0, d - 1, iz], recv_sem=recv.at[0, d - 1, iz],
            device_id=line_peer(peer), device_id_type=LOGICAL,
        )
        b = pltpu.make_async_remote_copy(
            src_ref=source_step.at[peer, iz], dst_ref=target_step.at[m, iz],
            send_sem=send.at[1, d - 1, iz], recv_sem=recv.at[1, d - 1, iz],
            device_id=line_peer(peer), device_id_type=LOGICAL,
        )
        return a, b

    def own_copies(iz, which, source, source_step, target, target_step):
        a = pltpu.make_async_copy(source.at[m, iz], target.at[m, iz], own_sem.at[which, 0, iz])
        b = pltpu.make_async_copy(source_step.at[m, iz], target_step.at[m, iz], own_sem.at[which, 1, iz])
        return a, b

    have_table(0)
    forward = (sq, sstep, rq, rstep)
    for iz in range(4):
        if iz % 2 == 0:
            deposit(iz // 2)
        rows = slice(iz * 512, iz * 512 + 512)
        for p in range(2):
            value = three(xhi[p, rows, :], xlo[p, rows, :], yin_ref[p, 0], yin_ref[p, 1])
            code, step = coded(value)
            for h in range(2):
                sq[p * 2 + h, iz] = code[:, h * 128 : h * 128 + 128].reshape(8, 4, 16, 128)
                sstep[p * 2 + h, iz] = jnp.broadcast_to(step[:, h * 128 : h * 128 + 128], (8, 128))
        for d in range(1, 4):
            for copy in line_copies(iz, d, *forward, line_send, line_recv):
                copy.start()
        for copy in own_copies(iz, 0, *forward):
            copy.start()

    have_table(1)

    def folded(iz, tz):
        lines = []
        for source in range(4):
            step = rstep[source, iz][0:1, :]
            planes = [decoded(rq[source, iz, :, z].reshape(128, 128), step) for z in (tz, tz + 1)]
            lines.append(jnp.concatenate(planes, axis=1))
        plus = jnp.concatenate([lines[0] + lines[2], lines[1] + lines[3]], axis=0)
        minus = jnp.concatenate([lines[0] - lines[2], lines[1] - lines[3]], axis=0)
        return halves(plus), halves(minus)

    def along_x(p, iz, tz, pair):
        value = three(xin_ref[p, 0], xin_ref[p, 1], pair[0], pair[1])
        for k in range(2):
            spec[(tz + k) * 4 + iz, p * 256 : p * 256 + 256, :] = value[:, k * 128 : k * 128 + 128]

    def share_out(codes, steps, g, right, left):
        top = jnp.max(jnp.maximum(jnp.abs(right), jnp.abs(left)), axis=0, keepdims=True)
        step = jnp.maximum(top, 1e-30) * (1.0 / 32767.0)
        both = jnp.concatenate([right, left], axis=0) * (1.0 / step)
        codes[g] = jnp.round(both).astype(jnp.int32).astype(jnp.int16)
        steps[g] = step

    def share_in(codes, steps, g):
        both = decoded(codes[g], steps[g])
        return both[0:8, :], both[8:16, :]

    def slab_ends(p):
        def block(b, _):
            rows = pl.ds(pl.multiple_of(p * 256 + b * 16, 16), 16)
            rate = rates_ref[0, rows, :]
            planes = [spec[z, rows, :] for z in range(16)]
            right, left = planes[0], planes[15]
            for z in range(1, 16):
                right = right * rate + planes[z]
                left = left * rate + planes[15 - z]
            for k in range(2):
                some = slice(k * 8, k * 8 + 8)
                share_out(ends_out.at[p], ends_step_out.at[p], b * 2 + k, right[some, :], left[some, :])
            return 0

        lax.fori_loop(0, 16, block, 0)
        slab_exchange(p, ends_out, ends_in, ends_sem)
        slab_exchange(p, ends_step_out, ends_step_in, ends_step_sem)

    def slab_exchange(p, source, target, sem):
        for peer, where in slab_peers():
            pltpu.make_async_remote_copy(
                src_ref=source.at[p, peer], dst_ref=target.at[p, slab],
                send_sem=sem.at[0, p], recv_sem=sem.at[1, p],
                device_id=where, device_id_type=LOGICAL,
            ).start()
        pltpu.make_async_copy(source.at[p, slab], target.at[p, slab], sem.at[1, p]).start()

    for iz in range(4):
        for d in range(1, 4):
            for copy in line_copies(iz, d, *forward, line_send, line_recv):
                copy.wait_recv()
        for copy in own_copies(iz, 0, *forward):
            copy.wait()
        for tz in range(0, 4, 2):
            plus, minus = folded(iz, tz)
            along_x(0, iz, tz, plus)
            if iz < 3:
                along_x(1, iz, tz, minus)
            else:
                last[tz // 2, 0], last[tz // 2, 1] = minus
    slab_ends(0)
    for tz in range(0, 4, 2):
        along_x(1, 3, tz, (last[tz // 2, 0], last[tz // 2, 1]))
    slab_ends(1)

    def chain(p):
        arrived(ends_in.at[p], ends_sem.at[1, p])
        arrived(ends_step_in.at[p], ends_step_sem.at[1, p])
        rate = rates_ref[0, pl.ds(pl.multiple_of(p * 256 + slab * 8, 8), 8), :]
        r2 = rate * rate
        r4 = r2 * r2
        r8 = r4 * r4
        hop = r8 * r8
        far = hop
        for _ in range(5):
            far = far * far
        far = far * rate
        total_right = total_left = jnp.zeros((8, 128), F32)
        for g in range(32):
            values = share_in(ends_in.at[p], ends_step_in.at[p], g)
            known_ends[g, 0], known_ends[g, 1] = values
            total_right = total_right * hop + values[0]
        for g in range(32):
            total_left = total_left * hop + known_ends[31 - g, 1]
        scale = -rate / (1.0 - far * far)
        right = scale * (total_left - far * total_right)
        left = scale * (total_right - far * total_left)
        for g in range(32):
            known_carry[g, 0] = right
            known_carry[31 - g, 1] = left
            right = right * hop + known_ends[g, 0]
            left = left * hop + known_ends[31 - g, 1]
        for g in range(32):
            share_out(carry_out.at[p], carry_step_out.at[p], g, known_carry[g, 0], known_carry[g, 1])
        slab_exchange(p, carry_out, carry_in, carry_sem)
        slab_exchange(p, carry_step_out, carry_step_in, carry_step_sem)

    chain(0)
    chain(1)

    def filters(p):
        arrived(carry_in.at[p], carry_sem.at[1, p])
        arrived(carry_step_in.at[p], carry_step_sem.at[1, p])

        def block(b, _):
            rows = pl.ds(pl.multiple_of(p * 256 + b * 16, 16), 16)
            rate, gain = rates_ref[0, rows, :], rates_ref[1, rows, :]
            planes = [spec[z, rows, :] for z in range(16)]
            shares = [share_in(carry_in.at[p], carry_step_in.at[p], b * 2 + k) for k in range(2)]
            right = jnp.concatenate([shares[0][0], shares[1][0]], axis=0)
            left = jnp.concatenate([shares[0][1], shares[1][1]], axis=0)
            beyond = [None] * 16
            for z in range(15, -1, -1):
                beyond[z] = left * rate
                left = planes[z] + beyond[z]
            for z in range(16):
                right = planes[z] + right * rate
                high, low = halves((right + beyond[z]) * gain)
                mhi[z, rows, :] = high
                mlo[z, rows, :] = low
            return 0

        lax.fori_loop(0, 16, block, 0)

    filters(0)
    filters(1)

    have_table(2)
    backward = (sq2, sstep2, rq2, rstep2)
    for iz in range(4):
        parts = []
        for tz in range(0, 4, 2):
            sums = []
            for p in range(2):
                rows = slice(p * 256, p * 256 + 256)
                high = jnp.concatenate([mhi[(tz + k) * 4 + iz, rows, :] for k in range(2)], axis=1)
                low = jnp.concatenate([mlo[(tz + k) * 4 + iz, rows, :] for k in range(2)], axis=1)
                sums.append(three(xout_ref[p, 0], xout_ref[p, 1], high, low))
            parts.append((sums[0] + sums[1], sums[0] - sums[1]))
        for target in range(4):
            span = slice((target % 2) * 128, (target % 2) * 128 + 128)
            blocks = []
            for tz in range(4):
                block = parts[tz // 2][target // 2][span, (tz % 2) * 128 : (tz % 2) * 128 + 128]
                blocks.append(block)
            top = blocks[0]
            for block in blocks:
                top = jnp.maximum(jnp.abs(top), jnp.abs(block))
            top = jnp.maximum(jnp.max(top, axis=0, keepdims=True), 1e-30)
            step = top * (1.0 / 32767.0)
            inverse = 1.0 / step
            for tz in range(4):
                code = jnp.round(blocks[tz] * inverse).astype(jnp.int32).astype(jnp.int16)
                sq2[target, iz, :, tz] = code.reshape(8, 16, 128)
            sstep2[target, iz] = jnp.broadcast_to(step, (8, 128))
        for d in range(1, 4):
            for copy in line_copies(iz, d, *backward, back_send, back_recv):
                copy.start()
        for copy in own_copies(iz, 1, *backward):
            copy.start()

    wanted = [
        (known[:, 2 * slot + 1 : 2 * slot + 2] * 64 + known[:, 2 * slot : 2 * slot + 1]).astype(jnp.int32)
        for slot in range(2)
    ]
    wanted = jnp.concatenate(wanted, axis=0)
    fetch[...] = jnp.where(iota((SLOTS, 512), 1) == wanted, 1.0, 0.0).astype(BF16)

    def reply(half):
        for part in range(8):
            lanes = slice((half * 8 + part) * 128, (half * 8 + part) * 128 + 128)
            to_blocks(part, jnp.dot(fetch[...], tiles[:, lanes], preferred_element_type=F32))
        reply_out[half] = stage[...].astype(BF16).reshape(128, 16, 128)
        exchange(reply_out.at[half], reply_in.at[half], reply_send.at[half], reply_recv.at[half])

    have_table(3)
    for iz in range(4):
        for d in range(1, 4):
            for copy in line_copies(iz, d, *backward, back_send, back_recv):
                copy.wait_recv()
        for copy in own_copies(iz, 1, *backward):
            copy.wait()
        sums = []
        for p in range(2):
            pieces = [
                decoded(rq2[p * 2 + h, iz].reshape(512, 128), rstep2[p * 2 + h, iz][0:1, :])
                for h in range(2)
            ]
            high, low = halves(jnp.concatenate(pieces, axis=1))
            sums.append(three(high, low, yout_ref[p, 0], yout_ref[p, 1]))
        for top, value in enumerate((sums[0] + sums[1], sums[0] - sums[1])):
            for half in range(2):
                lanes = slice(half * 128, half * 128 + 128)
                ty = top * 4 + half * 2
                for pair in range(4):
                    even = value[pair * 128 : pair * 128 + 64, lanes]
                    odd = value[pair * 128 + 64 : pair * 128 + 128, lanes]
                    span = slice((iz * 4 + pair) * 128, (iz * 4 + pair) * 128 + 128)
                    first = jnp.where(low_half, even, pltpu.roll(odd, 64, 1))
                    second = jnp.where(low_half, pltpu.roll(even, 64, 1), odd)
                    tiles[ty * 64 : ty * 64 + 64, span] = first.astype(BF16)
                    tiles[ty * 64 + 64 : ty * 64 + 128, span] = second.astype(BF16)
        if iz % 2 == 1:
            reply(iz // 2)

    for half in range(2):
        arrived(reply_in.at[half], reply_recv.at[half])
        stage[...] = reply_in[half].reshape(2048, 128).astype(F32)
        for part in range(8):
            lanes = slice((half * 8 + part) * 128, (half * 8 + part) * 128 + 128)
            out_ref[:, lanes] = jnp.dot(
                unpick[...], from_blocks(part), preferred_element_type=F32
            ).astype(BF16)

    sent(meta_out, meta_sem.at[0])
    for half in range(2):
        sent(brick_out.at[half], brick_send.at[half])
        sent(reply_out.at[half], reply_send.at[half])
    both = ((ends_out, ends_sem), (ends_step_out, ends_step_sem), (carry_out, carry_sem), (carry_step_out, carry_step_sem))
    for source, sem in both:
        for p in range(2):
            some = source.at[p, pl.ds(0, 31)]
            pltpu.make_async_copy(some, some, sem.at[0, p]).wait()
    for iz in range(4):
        for d in range(1, 4):
            for copy in line_copies(iz, d, *forward, line_send, line_recv):
                copy.wait_send()
            for copy in line_copies(iz, d, *backward, back_send, back_recv):
                copy.wait_send()


VMEM_LIMIT = 60 * 1024 * 1024


def on_device(bricks, owners, tile_ids, counts):
    vmem = pl.BlockSpec(memory_space=pltpu.VMEM)
    smem = pl.BlockSpec(memory_space=pltpu.SMEM)
    y_in, y_out, x_in, x_out = (jnp.asarray(t) for t in tables())
    codes = pltpu.VMEM((4, 4, 8, 4, 16, 128), jnp.int16)
    steps = pltpu.VMEM((4, 4, 8, 128), F32)
    known = pltpu.VMEM((32, 2, 8, 128), F32)
    share = pltpu.VMEM((2, 32, 16, 128), jnp.int16)
    grain = pltpu.VMEM((2, 32, 1, 128), F32)
    four = pltpu.SemaphoreType.DMA((2, 2))
    blocks = pltpu.VMEM((2, 128, 16, 128), BF16)
    table = pltpu.VMEM((2, 2, HALF, HALF), BF16)
    notes = pltpu.VMEM((128, 1, 128), F32)
    pair = pltpu.SemaphoreType.DMA((2,))
    line = pltpu.SemaphoreType.DMA((2, 3, 4))
    return pl.pallas_call(
        field_kernel,
        out_shape=jax.ShapeDtypeStruct((ROWS, CELLS), BF16),
        in_specs=[smem] + [vmem] * 4 + [pl.BlockSpec(memory_space=pl.ANY)] * 4,
        out_specs=vmem,
        scratch_shapes=[
            pltpu.VMEM((2, 512, 128), F32),
            table, table, table, table,
            pltpu.SemaphoreType.DMA((4,)),
            pltpu.VMEM((2048, 128), F32),
            blocks, blocks, notes, notes,
            pltpu.VMEM((128, 128), F32),
            blocks, blocks,
            pltpu.VMEM((ROWS, SLOTS), BF16),
            pltpu.VMEM((SLOTS, 512), BF16),
            pltpu.VMEM((512, SLOTS), BF16),
            pltpu.VMEM((2, 2048, HALF), BF16),
            pltpu.VMEM((2, 2048, HALF), BF16),
            codes, steps, codes, steps,
            pltpu.VMEM((16, 512, 128), F32),
            pltpu.VMEM((2, 2, HALF, HALF), BF16),
            known, known,
            share, share, share, share, grain, grain, grain, grain,
            pltpu.VMEM((16, 512, 128), BF16),
            pltpu.VMEM((16, 512, 128), BF16),
            codes, steps, codes, steps,
            pltpu.VMEM((512, CELLS), BF16),
            pair, pair, pair, pair, pair, line, line, four, four, four, four, line, line,
            pltpu.SemaphoreType.DMA((2, 2, 4)),
        ],
        compiler_params=pltpu.CompilerParams(
            collective_id=0, has_side_effects=True, vmem_limit_bytes=VMEM_LIMIT
        ),
        name="field",
    )(counts, bricks, owners.reshape(1, ROWS), tile_ids.reshape(1, ROWS), jnp.asarray(second_differences()), y_in, y_out, x_in, x_out)


def solution(mesh):
    in_specs = (P(("gz", "ma"), None), P(("gz", "ma"), None), P(("gz", "ma")), P(("gz", "ma")))
    out_specs = P(("gz", "ma"), None)
    return jax.shard_map(
        on_device, mesh=mesh, in_specs=in_specs, out_specs=out_specs, check_vma=False
    )
```

```python
import math

import jax
import jax.numpy as jnp
import ml_dtypes
import numpy as np
from jax import lax
from jax.experimental import pallas as pl
from jax.experimental.pallas import tpu as pltpu
from jax.sharding import PartitionSpec as P

N = 512
HALF = 256
SCREEN = 16
F32 = jnp.float32
BF16 = jnp.bfloat16
LOGICAL = pl.DeviceIdType.LOGICAL
SLOTS = 256
CELLS = 2048
ROWS = 128


def split_table(table):
    high = table.astype(ml_dtypes.bfloat16)
    low = (table - high.astype(np.float64)).astype(ml_dtypes.bfloat16)
    return high, low


def parity_table(parity, points):
    modes = 2 * np.arange(HALF) + parity
    angle = 2.0 * math.pi / N * ((modes[:, None] * points[None, :]) % N)
    return (np.cos(angle) + np.sin(angle)) / math.sqrt(N)


def stacked(tables):
    return np.stack([np.stack(split_table(t)) for t in tables])


def tables():
    natural = np.arange(HALF)
    m, ix, tx = np.meshgrid(np.arange(2), np.arange(8), np.arange(16), indexing="ij")
    order = (m * 128 + tx * 8 + ix).reshape(-1)
    y_tables = [parity_table(p, natural) for p in (0, 1)]
    x_tables = [parity_table(p, order) for p in (0, 1)]
    y_in = stacked([t.T for t in y_tables])
    x_in = stacked(x_tables)
    x_out = stacked([t.T for t in x_tables])
    return y_in, x_in, x_out


def second_differences():
    k = np.arange(128)
    rows = [2 * (128 * (c % 2) + k) + c // 2 for c in range(4)]
    values = (4.0 * np.sin(math.pi / N * np.stack(rows)) ** 2).astype(np.float32)
    return np.concatenate([values, values])


def handler(owner):
    core = (owner // 4) % 2
    y, t, m = owner // 32, (owner // 8) % 4, owner % 4
    place = (m - t - y + 8) % 4
    return jnp.where(core == 1, y * 32 + place * 8 + 4 + t, y * 32 + t * 8 + place)


def iota(shape, axis):
    return lax.broadcasted_iota(jnp.int32, shape, axis)


def pickers(owners_ref, count):
    row = jnp.broadcast_to(handler(owners_ref[...]), (ROWS, ROWS))
    column = jnp.transpose(row.astype(F32)).astype(jnp.int32)
    target = column[:, 0:1]
    same = column == row
    i, j = iota((ROWS, ROWS), 0), iota((ROWS, ROWS), 1)
    within_column = jnp.sum(jnp.where(same & (j < i), 1.0, 0.0), axis=1, keepdims=True)
    within_row = jnp.sum(jnp.where(same & (i < j), 1.0, 0.0), axis=0, keepdims=True)
    slot_column = target + ROWS * within_column.astype(jnp.int32)
    slot_row = row[0:1, :] + ROWS * within_row.astype(jnp.int32)
    down = (iota((SLOTS, ROWS), 0) == slot_row) & (iota((SLOTS, ROWS), 1) < count)
    across = iota((ROWS, SLOTS), 1) == slot_column
    return jnp.where(down, 1.0, 0.0).astype(BF16), jnp.where(across, 1.0, 0.0).astype(BF16)


def halves(value):
    high = value.astype(BF16)
    return high, (value - high.astype(F32)).astype(BF16)


def three(a_high, a_low, b_high, b_low, turned=False):
    dims = (((1,), (1 if turned else 0,)), ((), ()))
    total = lax.dot_general(a_high, b_high, dims, preferred_element_type=F32)
    total += lax.dot_general(a_high, b_low, dims, preferred_element_type=F32)
    total += lax.dot_general(a_low, b_high, dims, preferred_element_type=F32)
    return total


def coded(value):
    top = jnp.max(jnp.abs(value), axis=0, keepdims=True)
    step = jnp.maximum(top, 1e-30) * (1.0 / 32767.0)
    return jnp.round(value * (1.0 / step)).astype(jnp.int32).astype(jnp.int16), step


def decoded(code, step):
    return code.astype(jnp.int32).astype(F32) * step


def field_kernel(
    counts_ref, bricks_hbm, owners_ref, ids_ref, lam_ref, yin_hbm, xin_hbm, xout_hbm, out_ref,
    bricks_ref, rates_ref, yin_ref, xin_ref, xout_ref, table_sem,
    stage, brick_out, brick_in, meta_out, meta_in, meta, reply_out, reply_in, unpick, fetch, place, xhi, xlo, sq, sstep, rq, rstep, spec, last, known_ends, known_carry,
    ends_out, ends_in, carry_out, carry_in, ends_step_out, ends_step_in, carry_step_out, carry_step_in,
    mhi, mlo, sq2, sstep2, rq2, rstep2, tiles,
    brick_send, brick_recv, meta_sem, reply_send, reply_recv, line_send, line_recv, ends_sem, carry_sem, ends_step_sem, carry_step_sem, back_send, back_recv, own_sem,
):
    gz, ma = lax.axis_index("gz"), lax.axis_index("ma")
    y, x, core = gz // 8, (gz // 2) % 4, gz % 2
    me = gz * 4 + ma
    m = (x + y + ma) % 4
    t = core * ma + (1 - core) * x
    slab = y * 8 + t * 2 + core

    def wrap(value, size):
        return jnp.where(value >= size, value - size, value)

    def line_peer(p):
        place = (p - t - y + 8) % 4
        return y * 32 + core * (place * 8 + 4 + t) + (1 - core) * (t * 8 + place)

    def slab_peers():
        for dy in range(4):
            py = wrap(y + dy, 4)
            for dt in range(4):
                pt = wrap(t + dt, 4)
                place = (m - pt - py + 8) % 4
                for dc in range(2):
                    if dy or dt or dc:
                        pc = core if dc == 0 else 1 - core
                        where = py * 32 + jnp.where(pc == 1, place * 8 + 4 + pt, pt * 8 + place)
                        yield py * 8 + pt * 2 + pc, where

    def peers(body):
        def step(i, _):
            for k in range(8):
                body(wrap(me + (i * 8 + k + 1), 128))
            return 0

        lax.fori_loop(0, 15, step, 0)
        for d in range(121, 128):
            body(wrap(me + d, 128))

    pltpu.make_async_copy(bricks_hbm, bricks_ref, table_sem.at[3]).start()
    tables = ((yin_hbm, yin_ref), (xin_hbm, xin_ref), (xout_hbm, xout_ref))
    def have_table(i):
        pltpu.make_async_copy(*tables[i], table_sem.at[i]).wait()

    barrier = pltpu.get_barrier_semaphore()
    peers(lambda n: pl.semaphore_signal(barrier, inc=1, device_id=n, device_id_type=LOGICAL))

    def exchange(source, target, send, recv):
        def start(n):
            pltpu.make_async_remote_copy(
                src_ref=source.at[n], dst_ref=target.at[me], send_sem=send, recv_sem=recv,
                device_id=n, device_id_type=LOGICAL,
            ).start()

        peers(start)
        pltpu.make_async_copy(source.at[me], target.at[me], recv).start()

    def arrived(target, recv):
        pltpu.make_async_copy(target, target, recv).wait()

    def sent(source, send):
        some = source.at[pl.ds(0, 127)]
        pltpu.make_async_copy(some, some, send).wait()

    def to_blocks(part, block):
        for slot in range(2):
            stage[pl.ds(slot * 4 + part, 128, stride=8), :] = block[slot * 128 : slot * 128 + 128, :]

    def from_blocks(part):
        slots = [stage[pl.ds(slot * 4 + part, 128, stride=8), :] for slot in range(2)]
        return jnp.concatenate(slots, axis=0).astype(BF16)

    for i, (source, target) in enumerate(tables):
        pltpu.make_async_copy(source, target, table_sem.at[i]).start()

    pick, unpick[...] = pickers(owners_ref, counts_ref[0])
    pltpu.make_async_copy(bricks_hbm, bricks_ref, table_sem.at[3]).wait()

    def send_bricks(iz):
        for part in range(4):
            lanes = slice((iz * 4 + part) * 128, (iz * 4 + part) * 128 + 128)
            to_blocks(part, jnp.dot(pick, bricks_ref[:, lanes], preferred_element_type=F32))
        brick_out[iz] = stage[...].astype(BF16).reshape(128, 8, 128)
        if iz == 0:
            pl.semaphore_wait(barrier, 127)
        exchange(brick_out.at[iz], brick_in.at[iz], brick_send.at[iz], brick_recv.at[iz])

    send_bricks(0)
    ids = ids_ref[...]
    lane_row = iota((ROWS, ROWS), 0)
    for slot in range(2):
        info = jnp.where(lane_row == 2 * slot, ids // 8, jnp.where(lane_row == 2 * slot + 1, ids % 8, 0))
        info = jnp.transpose(info.astype(F32)).astype(BF16)
        part = jnp.dot(pick[slot * 128 : slot * 128 + 128, :], info, preferred_element_type=F32)
        meta[...] = part if slot == 0 else meta[...] + part

    def spread(i, _):
        for k in range(8):
            meta_out[i * 8 + k] = meta[pl.ds(i * 8 + k, 1), :]
        return 0

    lax.fori_loop(0, 16, spread, 0)
    exchange(meta_out, meta_in, meta_sem.at[0], meta_sem.at[1])
    for iz in range(1, 4):
        send_bricks(iz)

    lam_k = lam_ref[pl.ds(4 + m, 1), :]
    for block in range(4):
        lam_j = jnp.transpose(jnp.broadcast_to(lam_ref[block : block + 1, :], (128, 128)))
        excess = 1.0 / (SCREEN * SCREEN) + lam_j + lam_k
        root = jnp.sqrt(excess * (excess + 4.0))
        rates_ref[0, block * 128 : block * 128 + 128, :] = 2.0 / (2.0 + excess + root)
        rates_ref[1, block * 128 : block * 128 + 128, :] = 1.0 / root

    arrived(meta_in, meta_sem.at[1])

    def collect(i, _):
        for k in range(8):
            meta[pl.ds(i * 8 + k, 1), :] = meta_in[i * 8 + k]
        return 0

    lax.fori_loop(0, 16, collect, 0)

    known = meta[...]
    meta_rows = jnp.transpose(known)
    q_row = jnp.concatenate([meta_rows[0:1, :], meta_rows[2:3, :]], axis=1).astype(jnp.int32)
    ty_row = jnp.concatenate([meta_rows[1:2, :], meta_rows[3:4, :]], axis=1).astype(jnp.int32)
    for p in range(2):
        for ty in range(4):
            hit = q_row == iota((64, SLOTS), 0)
            second = -1.0 if p else 1.0
            value = jnp.where(ty_row == ty, 1.0, 0.0) + jnp.where(ty_row == ty + 4, second, 0.0)
            first = (p * 4 + ty) * 64
            place[first : first + 64, :] = jnp.where(hit, value, 0.0).astype(BF16)
    low_half = iota((64, 128), 1) < 64

    def deposit(iz):
        arrived(brick_in.at[iz], brick_recv.at[iz])
        stage[...] = brick_in[iz].reshape(1024, 128).astype(F32)
        for pair in range(4):
            laid = jnp.dot(place[...], from_blocks(pair), preferred_element_type=F32)
            for p in range(2):
                for side in range(2):
                    first = (p * 4 + side * 2) * 64
                    te, to = laid[first : first + 64, :], laid[first + 64 : first + 128, :]
                    even = jnp.where(low_half, te, pltpu.roll(to, 64, 1))
                    odd = jnp.where(low_half, pltpu.roll(te, 64, 1), to)
                    for k, value in enumerate((even, odd)):
                        row = (iz * 8 + pair * 2 + k) * 64
                        high, low = halves(value)
                        xhi[p, row : row + 64, side * 128 : side * 128 + 128] = high
                        xlo[p, row : row + 64, side * 128 : side * 128 + 128] = low

    def line_copies(iz, d, source, source_step, target, target_step, send, recv):
        peer = (m + d) % 4
        a = pltpu.make_async_remote_copy(
            src_ref=source.at[peer, iz], dst_ref=target.at[m, iz],
            send_sem=send.at[0, d - 1, iz], recv_sem=recv.at[0, d - 1, iz],
            device_id=line_peer(peer), device_id_type=LOGICAL,
        )
        b = pltpu.make_async_remote_copy(
            src_ref=source_step.at[peer, iz], dst_ref=target_step.at[m, iz],
            send_sem=send.at[1, d - 1, iz], recv_sem=recv.at[1, d - 1, iz],
            device_id=line_peer(peer), device_id_type=LOGICAL,
        )
        return a, b

    def own_copies(iz, which, source, source_step, target, target_step):
        a = pltpu.make_async_copy(source.at[m, iz], target.at[m, iz], own_sem.at[which, 0, iz])
        b = pltpu.make_async_copy(source_step.at[m, iz], target_step.at[m, iz], own_sem.at[which, 1, iz])
        return a, b

    have_table(0)
    forward = (sq, sstep, rq, rstep)
    for iz in range(4):
        deposit(iz)
        rows = slice(iz * 512, iz * 512 + 512)
        for p in range(2):
            value = three(xhi[p, rows, :], xlo[p, rows, :], yin_ref[p, 0], yin_ref[p, 1])
            code, step = coded(value)
            for h in range(2):
                sq[p * 2 + h, iz] = code[:, h * 128 : h * 128 + 128].reshape(8, 4, 16, 128)
                sstep[p * 2 + h, iz] = jnp.broadcast_to(step[:, h * 128 : h * 128 + 128], (8, 128))
        for d in range(1, 4):
            for copy in line_copies(iz, d, *forward, line_send, line_recv):
                copy.start()
        for copy in own_copies(iz, 0, *forward):
            copy.start()

    have_table(1)

    def folded(iz, tz):
        lines = []
        for source in range(4):
            step = rstep[source, iz][0:1, :]
            planes = [decoded(rq[source, iz, :, z].reshape(128, 128), step) for z in (tz, tz + 1)]
            lines.append(jnp.concatenate(planes, axis=1))
        plus = jnp.concatenate([lines[0] + lines[2], lines[1] + lines[3]], axis=0)
        minus = jnp.concatenate([lines[0] - lines[2], lines[1] - lines[3]], axis=0)
        return halves(plus), halves(minus)

    def along_x(p, iz, tz, pair):
        value = three(xin_ref[p, 0], xin_ref[p, 1], pair[0], pair[1])
        for k in range(2):
            spec[(tz + k) * 4 + iz, p * 256 : p * 256 + 256, :] = value[:, k * 128 : k * 128 + 128]

    def share_out(codes, steps, g, right, left):
        top = jnp.max(jnp.maximum(jnp.abs(right), jnp.abs(left)), axis=0, keepdims=True)
        step = jnp.maximum(top, 1e-30) * (1.0 / 32767.0)
        both = jnp.concatenate([right, left], axis=0) * (1.0 / step)
        codes[g] = jnp.round(both).astype(jnp.int32).astype(jnp.int16)
        steps[g] = step

    def share_in(codes, steps, g):
        both = decoded(codes[g], steps[g])
        return both[0:8, :], both[8:16, :]

    def slab_ends(p):
        def block(b, _):
            rows = pl.ds(pl.multiple_of(p * 256 + b * 16, 16), 16)
            rate = rates_ref[0, rows, :]
            planes = [spec[z, rows, :] for z in range(16)]
            right, left = planes[0], planes[15]
            for z in range(1, 16):
                right = right * rate + planes[z]
                left = left * rate + planes[15 - z]
            for k in range(2):
                some = slice(k * 8, k * 8 + 8)
                share_out(ends_out.at[p], ends_step_out.at[p], b * 2 + k, right[some, :], left[some, :])
            return 0

        lax.fori_loop(0, 16, block, 0)
        slab_exchange(p, ends_out, ends_in, ends_sem)
        slab_exchange(p, ends_step_out, ends_step_in, ends_step_sem)

    def slab_exchange(p, source, target, sem):
        for peer, where in slab_peers():
            pltpu.make_async_remote_copy(
                src_ref=source.at[p, peer], dst_ref=target.at[p, slab],
                send_sem=sem.at[0, p], recv_sem=sem.at[1, p],
                device_id=where, device_id_type=LOGICAL,
            ).start()
        pltpu.make_async_copy(source.at[p, slab], target.at[p, slab], sem.at[1, p]).start()

    for iz in range(4):
        for d in range(1, 4):
            for copy in line_copies(iz, d, *forward, line_send, line_recv):
                copy.wait_recv()
        for copy in own_copies(iz, 0, *forward):
            copy.wait()
        for tz in range(0, 4, 2):
            plus, minus = folded(iz, tz)
            along_x(0, iz, tz, plus)
            if iz < 3:
                along_x(1, iz, tz, minus)
            else:
                last[tz // 2, 0], last[tz // 2, 1] = minus
    slab_ends(0)
    for tz in range(0, 4, 2):
        along_x(1, 3, tz, (last[tz // 2, 0], last[tz // 2, 1]))
    slab_ends(1)

    def chain(p):
        arrived(ends_in.at[p], ends_sem.at[1, p])
        arrived(ends_step_in.at[p], ends_step_sem.at[1, p])
        rate = rates_ref[0, pl.ds(pl.multiple_of(p * 256 + slab * 8, 8), 8), :]
        r2 = rate * rate
        r4 = r2 * r2
        r8 = r4 * r4
        hop = r8 * r8
        far = hop
        for _ in range(5):
            far = far * far
        far = far * rate
        total_right = total_left = jnp.zeros((8, 128), F32)
        for g in range(32):
            values = share_in(ends_in.at[p], ends_step_in.at[p], g)
            known_ends[g, 0], known_ends[g, 1] = values
            total_right = total_right * hop + values[0]
        for g in range(32):
            total_left = total_left * hop + known_ends[31 - g, 1]
        scale = -rate / (1.0 - far * far)
        right = scale * (total_left - far * total_right)
        left = scale * (total_right - far * total_left)
        for g in range(32):
            known_carry[g, 0] = right
            known_carry[31 - g, 1] = left
            right = right * hop + known_ends[g, 0]
            left = left * hop + known_ends[31 - g, 1]
        for g in range(32):
            share_out(carry_out.at[p], carry_step_out.at[p], g, known_carry[g, 0], known_carry[g, 1])
        slab_exchange(p, carry_out, carry_in, carry_sem)
        slab_exchange(p, carry_step_out, carry_step_in, carry_step_sem)

    chain(0)
    chain(1)

    def filters(p):
        arrived(carry_in.at[p], carry_sem.at[1, p])
        arrived(carry_step_in.at[p], carry_step_sem.at[1, p])

        def block(b, _):
            rows = pl.ds(pl.multiple_of(p * 256 + b * 16, 16), 16)
            rate, gain = rates_ref[0, rows, :], rates_ref[1, rows, :]
            planes = [spec[z, rows, :] for z in range(16)]
            shares = [share_in(carry_in.at[p], carry_step_in.at[p], b * 2 + k) for k in range(2)]
            right = jnp.concatenate([shares[0][0], shares[1][0]], axis=0)
            left = jnp.concatenate([shares[0][1], shares[1][1]], axis=0)
            beyond = [None] * 16
            for z in range(15, -1, -1):
                beyond[z] = left * rate
                left = planes[z] + beyond[z]
            for z in range(16):
                right = planes[z] + right * rate
                high, low = halves((right + beyond[z]) * gain)
                mhi[z, rows, :] = high
                mlo[z, rows, :] = low
            return 0

        lax.fori_loop(0, 16, block, 0)

    filters(0)
    filters(1)

    have_table(2)
    backward = (sq2, sstep2, rq2, rstep2)
    for iz in range(4):
        parts = []
        for tz in range(0, 4, 2):
            sums = []
            for p in range(2):
                rows = slice(p * 256, p * 256 + 256)
                high = jnp.concatenate([mhi[(tz + k) * 4 + iz, rows, :] for k in range(2)], axis=1)
                low = jnp.concatenate([mlo[(tz + k) * 4 + iz, rows, :] for k in range(2)], axis=1)
                sums.append(three(xout_ref[p, 0], xout_ref[p, 1], high, low))
            parts.append((sums[0] + sums[1], sums[0] - sums[1]))
        for target in range(4):
            span = slice((target % 2) * 128, (target % 2) * 128 + 128)
            blocks = []
            for tz in range(4):
                block = parts[tz // 2][target // 2][span, (tz % 2) * 128 : (tz % 2) * 128 + 128]
                blocks.append(block)
            top = blocks[0]
            for block in blocks:
                top = jnp.maximum(jnp.abs(top), jnp.abs(block))
            top = jnp.maximum(jnp.max(top, axis=0, keepdims=True), 1e-30)
            step = top * (1.0 / 32767.0)
            inverse = 1.0 / step
            for tz in range(4):
                code = jnp.round(blocks[tz] * inverse).astype(jnp.int32).astype(jnp.int16)
                sq2[target, iz, :, tz] = code.reshape(8, 16, 128)
            sstep2[target, iz] = jnp.broadcast_to(step, (8, 128))
        for d in range(1, 4):
            for copy in line_copies(iz, d, *backward, back_send, back_recv):
                copy.start()
        for copy in own_copies(iz, 1, *backward):
            copy.start()

    wanted = [
        (known[:, 2 * slot + 1 : 2 * slot + 2] * 64 + known[:, 2 * slot : 2 * slot + 1]).astype(jnp.int32)
        for slot in range(2)
    ]
    wanted = jnp.concatenate(wanted, axis=0)
    fetch[...] = jnp.where(iota((SLOTS, 512), 1) == wanted, 1.0, 0.0).astype(BF16)

    def reply(iz):
        for part in range(4):
            lanes = slice((iz * 4 + part) * 128, (iz * 4 + part) * 128 + 128)
            to_blocks(part, jnp.dot(fetch[...], tiles[:, lanes], preferred_element_type=F32))
        reply_out[iz] = stage[...].astype(BF16).reshape(128, 8, 128)
        exchange(reply_out.at[iz], reply_in.at[iz], reply_send.at[iz], reply_recv.at[iz])

    for iz in range(4):
        for d in range(1, 4):
            for copy in line_copies(iz, d, *backward, back_send, back_recv):
                copy.wait_recv()
        for copy in own_copies(iz, 1, *backward):
            copy.wait()
        sums = []
        for p in range(2):
            pieces = [
                decoded(rq2[p * 2 + h, iz].reshape(512, 128), rstep2[p * 2 + h, iz][0:1, :])
                for h in range(2)
            ]
            high, low = halves(jnp.concatenate(pieces, axis=1))
            sums.append(three(high, low, yin_ref[p, 0], yin_ref[p, 1], True))
        for top, value in enumerate((sums[0] + sums[1], sums[0] - sums[1])):
            for half in range(2):
                lanes = slice(half * 128, half * 128 + 128)
                ty = top * 4 + half * 2
                for pair in range(4):
                    even = value[pair * 128 : pair * 128 + 64, lanes]
                    odd = value[pair * 128 + 64 : pair * 128 + 128, lanes]
                    span = slice((iz * 4 + pair) * 128, (iz * 4 + pair) * 128 + 128)
                    first = jnp.where(low_half, even, pltpu.roll(odd, 64, 1))
                    second = jnp.where(low_half, pltpu.roll(even, 64, 1), odd)
                    tiles[ty * 64 : ty * 64 + 64, span] = first.astype(BF16)
                    tiles[ty * 64 + 64 : ty * 64 + 128, span] = second.astype(BF16)
        reply(iz)

    for iz in range(4):
        arrived(reply_in.at[iz], reply_recv.at[iz])
        stage[...] = reply_in[iz].reshape(1024, 128).astype(F32)
        for part in range(4):
            lanes = slice((iz * 4 + part) * 128, (iz * 4 + part) * 128 + 128)
            out_ref[:, lanes] = jnp.dot(
                unpick[...], from_blocks(part), preferred_element_type=F32
            ).astype(BF16)

    sent(meta_out, meta_sem.at[0])
    for iz in range(4):
        sent(brick_out.at[iz], brick_send.at[iz])
        sent(reply_out.at[iz], reply_send.at[iz])
    both = ((ends_out, ends_sem), (ends_step_out, ends_step_sem), (carry_out, carry_sem), (carry_step_out, carry_step_sem))
    for source, sem in both:
        for p in range(2):
            some = source.at[p, pl.ds(0, 31)]
            pltpu.make_async_copy(some, some, sem.at[0, p]).wait()
    for iz in range(4):
        for d in range(1, 4):
            for copy in line_copies(iz, d, *forward, line_send, line_recv):
                copy.wait_send()
            for copy in line_copies(iz, d, *backward, back_send, back_recv):
                copy.wait_send()


VMEM_LIMIT = 60 * 1024 * 1024


def on_device(bricks, owners, tile_ids, counts):
    vmem = pl.BlockSpec(memory_space=pltpu.VMEM)
    smem = pl.BlockSpec(memory_space=pltpu.SMEM)
    hbm = pl.BlockSpec(memory_space=pl.ANY)
    y_in, x_in, x_out = (jnp.asarray(t) for t in tables())
    codes = pltpu.VMEM((4, 4, 8, 4, 16, 128), jnp.int16)
    steps = pltpu.VMEM((4, 4, 8, 128), F32)
    known = pltpu.VMEM((32, 2, 8, 128), F32)
    share = pltpu.VMEM((2, 32, 16, 128), jnp.int16)
    grain = pltpu.VMEM((2, 32, 1, 128), F32)
    four = pltpu.SemaphoreType.DMA((2, 2))
    blocks = pltpu.VMEM((4, 128, 8, 128), BF16)
    quad = pltpu.SemaphoreType.DMA((4,))
    table = pltpu.VMEM((2, 2, HALF, HALF), BF16)
    notes = pltpu.VMEM((128, 1, 128), F32)
    pair = pltpu.SemaphoreType.DMA((2,))
    line = pltpu.SemaphoreType.DMA((2, 3, 4))
    found = pl.pallas_call(
        field_kernel,
        out_shape=jax.ShapeDtypeStruct((ROWS, CELLS), BF16),
        in_specs=[smem, hbm, vmem, vmem, vmem, hbm, hbm, hbm],
        out_specs=vmem,
        scratch_shapes=[
            pltpu.VMEM((ROWS, CELLS), BF16),
            pltpu.VMEM((2, 512, 128), F32),
            table, table, table,
            pltpu.SemaphoreType.DMA((4,)),
            pltpu.VMEM((1024, 128), F32),
            blocks, blocks, notes, notes,
            pltpu.VMEM((128, 128), F32),
            blocks, blocks,
            pltpu.VMEM((ROWS, SLOTS), BF16),
            pltpu.VMEM((SLOTS, 512), BF16),
            pltpu.VMEM((512, SLOTS), BF16),
            pltpu.VMEM((2, 2048, HALF), BF16),
            pltpu.VMEM((2, 2048, HALF), BF16),
            codes, steps, codes, steps,
            pltpu.VMEM((16, 512, 128), F32),
            pltpu.VMEM((2, 2, HALF, HALF), BF16),
            known, known,
            share, share, share, share, grain, grain, grain, grain,
            pltpu.VMEM((16, 512, 128), BF16),
            pltpu.VMEM((16, 512, 128), BF16),
            codes, steps, codes, steps,
            pltpu.VMEM((512, CELLS), BF16),
            quad, quad, pair, quad, quad, line, line, four, four, four, four, line, line,
            pltpu.SemaphoreType.DMA((2, 2, 4)),
        ],
        compiler_params=pltpu.CompilerParams(
            collective_id=0, has_side_effects=True, vmem_limit_bytes=VMEM_LIMIT
        ),
        name="field",
    )(counts, bricks, owners.reshape(1, ROWS), tile_ids.reshape(1, ROWS), jnp.asarray(second_differences()), y_in, x_in, x_out)
    live = jnp.arange(ROWS, dtype=jnp.int32)[:, None] < counts[0]
    return jnp.where(live, found, jnp.zeros_like(found))


def solution(mesh):
    in_specs = (P(("gz", "ma"), None), P(("gz", "ma"), None), P(("gz", "ma")), P(("gz", "ma")))
    out_specs = P(("gz", "ma"), None)
    return jax.shard_map(
        on_device, mesh=mesh, in_specs=in_specs, out_specs=out_specs, check_vma=False
    )
```

```python
import math

import jax
import jax.numpy as jnp
import ml_dtypes
import numpy as np
from jax import lax
from jax.experimental import pallas as pl
from jax.experimental.pallas import tpu as pltpu
from jax.sharding import PartitionSpec as P

N = 512
HALF = 256
SCREEN = 16
F32 = jnp.float32
BF16 = jnp.bfloat16
LOGICAL = pl.DeviceIdType.LOGICAL
SLOTS = 256
CELLS = 2048
ROWS = 128


def split_table(table):
    high = table.astype(ml_dtypes.bfloat16)
    low = (table - high.astype(np.float64)).astype(ml_dtypes.bfloat16)
    return high, low


def parity_table(parity, points):
    modes = 2 * np.arange(HALF) + parity
    angle = 2.0 * math.pi / N * ((modes[:, None] * points[None, :]) % N)
    return (np.cos(angle) + np.sin(angle)) / math.sqrt(N)


def stacked(tables):
    return np.stack([np.stack(split_table(t)) for t in tables])


def tables():
    natural = np.arange(HALF)
    m, ix, tx = np.meshgrid(np.arange(2), np.arange(8), np.arange(16), indexing="ij")
    order = (m * 128 + tx * 8 + ix).reshape(-1)
    y_tables = [parity_table(p, natural) for p in (0, 1)]
    x_tables = [parity_table(p, order) for p in (0, 1)]
    y_in = stacked([t.T for t in y_tables])
    x_in = stacked(x_tables)
    x_out = stacked([t.T for t in x_tables])
    return y_in, x_in, x_out


def second_differences():
    k = np.arange(128)
    rows = [2 * (128 * (c % 2) + k) + c // 2 for c in range(4)]
    values = (4.0 * np.sin(math.pi / N * np.stack(rows)) ** 2).astype(np.float32)
    return np.concatenate([values, values])


def seat(core, u, v, w, m):
    q = (m - (u + v + w) + 8) % 4
    x = (2 * v + core + q // 2) % 4
    side = 2 * w + q % 2
    y = u + core * (side - u)
    z = side + core * (u - side)
    return y * 32 + x * 8 + core * 4 + z


def handler(owner):
    return seat((owner // 4) % 2, owner // 32, (owner // 16) % 2, (owner // 8) % 2, owner % 4)


def iota(shape, axis):
    return lax.broadcasted_iota(jnp.int32, shape, axis)


def pickers(owners_ref, count):
    row = jnp.broadcast_to(handler(owners_ref[...]), (ROWS, ROWS))
    column = jnp.transpose(row.astype(F32)).astype(jnp.int32)
    target = column[:, 0:1]
    same = column == row
    i, j = iota((ROWS, ROWS), 0), iota((ROWS, ROWS), 1)
    within_column = jnp.sum(jnp.where(same & (j < i), 1.0, 0.0), axis=1, keepdims=True)
    within_row = jnp.sum(jnp.where(same & (i < j), 1.0, 0.0), axis=0, keepdims=True)
    slot_column = target + ROWS * within_column.astype(jnp.int32)
    slot_row = row[0:1, :] + ROWS * within_row.astype(jnp.int32)
    down = (iota((SLOTS, ROWS), 0) == slot_row) & (iota((SLOTS, ROWS), 1) < count)
    across = iota((ROWS, SLOTS), 1) == slot_column
    return jnp.where(down, 1.0, 0.0).astype(BF16), jnp.where(across, 1.0, 0.0).astype(BF16)


def halves(value):
    high = value.astype(BF16)
    return high, (value - high.astype(F32)).astype(BF16)


def three(a_high, a_low, b_high, b_low, turned=False):
    dims = (((1,), (1 if turned else 0,)), ((), ()))
    total = lax.dot_general(a_high, b_high, dims, preferred_element_type=F32)
    total += lax.dot_general(a_high, b_low, dims, preferred_element_type=F32)
    total += lax.dot_general(a_low, b_high, dims, preferred_element_type=F32)
    return total


def coded(value):
    top = jnp.max(jnp.abs(value), axis=0, keepdims=True)
    step = jnp.maximum(top, 1e-30) * (1.0 / 32767.0)
    return jnp.round(value * (1.0 / step)).astype(jnp.int32).astype(jnp.int16), step


def decoded(code, step):
    return code.astype(jnp.int32).astype(F32) * step


def field_kernel(
    counts_ref, bricks_hbm, owners_ref, ids_ref, lam_ref, yin_hbm, xin_hbm, xout_hbm, out_ref,
    bricks_ref, rates_ref, yin_ref, xin_ref, xout_ref, table_sem,
    stage, brick_out, brick_in, meta_out, meta_in, meta, reply_out, reply_in, unpick, fetch, place, xhi, xlo, sq, sstep, rq, rstep, spec, last, known_ends, known_carry,
    ends_out, ends_in, carry_out, carry_in, ends_step_out, ends_step_in, carry_step_out, carry_step_in,
    mhi, mlo, sq2, sstep2, rq2, rstep2, tiles,
    brick_send, brick_recv, meta_sem, reply_send, reply_recv, line_send, line_recv, ends_sem, carry_sem, ends_step_sem, carry_step_sem, back_send, back_recv, own_sem,
):
    gz, ma = lax.axis_index("gz"), lax.axis_index("ma")
    y, x, core = gz // 8, (gz // 2) % 4, gz % 2
    me = gz * 4 + ma
    shifted = (x + 4 - core) % 4
    u, side = y + core * (ma - y), ma + core * (y - ma)
    v, w = shifted // 2, side // 2
    m = (2 * (shifted % 2) + side % 2 + u + v + w) % 4
    slab = u * 8 + v * 4 + w * 2 + core

    def wrap(value, size):
        return jnp.where(value >= size, value - size, value)

    def line_peer(p):
        return seat(core, u, v, w, p)

    def slab_peers():
        for du in range(4):
            pu = wrap(u + du, 4)
            for dv in range(2):
                pv = v if dv == 0 else 1 - v
                for dw in range(2):
                    pw = w if dw == 0 else 1 - w
                    for dc in range(2):
                        if du or dv or dw or dc:
                            pc = core if dc == 0 else 1 - core
                            yield pu * 8 + pv * 4 + pw * 2 + pc, seat(pc, pu, pv, pw, m)

    def peers(body):
        def step(i, _):
            for k in range(8):
                body(wrap(me + (i * 8 + k + 1), 128))
            return 0

        lax.fori_loop(0, 15, step, 0)
        for d in range(121, 128):
            body(wrap(me + d, 128))

    pltpu.make_async_copy(bricks_hbm, bricks_ref, table_sem.at[3]).start()
    tables = ((yin_hbm, yin_ref), (xin_hbm, xin_ref), (xout_hbm, xout_ref))
    def have_table(i):
        pltpu.make_async_copy(*tables[i], table_sem.at[i]).wait()

    barrier = pltpu.get_barrier_semaphore()
    peers(lambda n: pl.semaphore_signal(barrier, inc=1, device_id=n, device_id_type=LOGICAL))

    def exchange(source, target, send, recv):
        def start(n):
            pltpu.make_async_remote_copy(
                src_ref=source.at[n], dst_ref=target.at[me], send_sem=send, recv_sem=recv,
                device_id=n, device_id_type=LOGICAL,
            ).start()

        peers(start)
        pltpu.make_async_copy(source.at[me], target.at[me], recv).start()

    def arrived(target, recv):
        pltpu.make_async_copy(target, target, recv).wait()

    def sent(source, send):
        some = source.at[pl.ds(0, 127)]
        pltpu.make_async_copy(some, some, send).wait()

    def to_blocks(part, block):
        for slot in range(2):
            stage[pl.ds(slot * 4 + part, 128, stride=8), :] = block[slot * 128 : slot * 128 + 128, :]

    def from_blocks(part):
        slots = [stage[pl.ds(slot * 4 + part, 128, stride=8), :] for slot in range(2)]
        return jnp.concatenate(slots, axis=0).astype(BF16)

    for i, (source, target) in enumerate(tables):
        pltpu.make_async_copy(source, target, table_sem.at[i]).start()

    pick, unpick[...] = pickers(owners_ref, counts_ref[0])
    pltpu.make_async_copy(bricks_hbm, bricks_ref, table_sem.at[3]).wait()

    def send_bricks(iz):
        for part in range(4):
            lanes = slice((iz * 4 + part) * 128, (iz * 4 + part) * 128 + 128)
            to_blocks(part, jnp.dot(pick, bricks_ref[:, lanes], preferred_element_type=F32))
        brick_out[iz] = stage[...].astype(BF16).reshape(128, 8, 128)
        if iz == 0:
            pl.semaphore_wait(barrier, 127)
        exchange(brick_out.at[iz], brick_in.at[iz], brick_send.at[iz], brick_recv.at[iz])

    send_bricks(0)
    ids = ids_ref[...]
    lane_row = iota((ROWS, ROWS), 0)
    for slot in range(2):
        info = jnp.where(lane_row == 2 * slot, ids // 8, jnp.where(lane_row == 2 * slot + 1, ids % 8, 0))
        info = jnp.transpose(info.astype(F32)).astype(BF16)
        part = jnp.dot(pick[slot * 128 : slot * 128 + 128, :], info, preferred_element_type=F32)
        meta[...] = part if slot == 0 else meta[...] + part

    def spread(i, _):
        for k in range(8):
            meta_out[i * 8 + k] = meta[pl.ds(i * 8 + k, 1), :]
        return 0

    lax.fori_loop(0, 16, spread, 0)
    exchange(meta_out, meta_in, meta_sem.at[0], meta_sem.at[1])
    for iz in range(1, 4):
        send_bricks(iz)

    lam_k = lam_ref[pl.ds(4 + m, 1), :]
    for block in range(4):
        lam_j = jnp.transpose(jnp.broadcast_to(lam_ref[block : block + 1, :], (128, 128)))
        excess = 1.0 / (SCREEN * SCREEN) + lam_j + lam_k
        root = jnp.sqrt(excess * (excess + 4.0))
        rates_ref[0, block * 128 : block * 128 + 128, :] = 2.0 / (2.0 + excess + root)
        rates_ref[1, block * 128 : block * 128 + 128, :] = 1.0 / root

    arrived(meta_in, meta_sem.at[1])

    def collect(i, _):
        for k in range(8):
            meta[pl.ds(i * 8 + k, 1), :] = meta_in[i * 8 + k]
        return 0

    lax.fori_loop(0, 16, collect, 0)

    known = meta[...]
    meta_rows = jnp.transpose(known)
    q_row = jnp.concatenate([meta_rows[0:1, :], meta_rows[2:3, :]], axis=1).astype(jnp.int32)
    ty_row = jnp.concatenate([meta_rows[1:2, :], meta_rows[3:4, :]], axis=1).astype(jnp.int32)
    for p in range(2):
        for ty in range(4):
            hit = q_row == iota((64, SLOTS), 0)
            second = -1.0 if p else 1.0
            value = jnp.where(ty_row == ty, 1.0, 0.0) + jnp.where(ty_row == ty + 4, second, 0.0)
            first = (p * 4 + ty) * 64
            place[first : first + 64, :] = jnp.where(hit, value, 0.0).astype(BF16)
    low_half = iota((64, 128), 1) < 64

    def deposit(iz):
        arrived(brick_in.at[iz], brick_recv.at[iz])
        stage[...] = brick_in[iz].reshape(1024, 128).astype(F32)
        for pair in range(4):
            laid = jnp.dot(place[...], from_blocks(pair), preferred_element_type=F32)
            for p in range(2):
                for side in range(2):
                    first = (p * 4 + side * 2) * 64
                    te, to = laid[first : first + 64, :], laid[first + 64 : first + 128, :]
                    even = jnp.where(low_half, te, pltpu.roll(to, 64, 1))
                    odd = jnp.where(low_half, pltpu.roll(te, 64, 1), to)
                    for k, value in enumerate((even, odd)):
                        row = (iz * 8 + pair * 2 + k) * 64
                        high, low = halves(value)
                        xhi[p, row : row + 64, side * 128 : side * 128 + 128] = high
                        xlo[p, row : row + 64, side * 128 : side * 128 + 128] = low

    def line_copies(iz, d, source, source_step, target, target_step, send, recv):
        peer = (m + d) % 4
        a = pltpu.make_async_remote_copy(
            src_ref=source.at[peer, iz], dst_ref=target.at[m, iz],
            send_sem=send.at[0, d - 1, iz], recv_sem=recv.at[0, d - 1, iz],
            device_id=line_peer(peer), device_id_type=LOGICAL,
        )
        b = pltpu.make_async_remote_copy(
            src_ref=source_step.at[peer, iz], dst_ref=target_step.at[m, iz],
            send_sem=send.at[1, d - 1, iz], recv_sem=recv.at[1, d - 1, iz],
            device_id=line_peer(peer), device_id_type=LOGICAL,
        )
        return a, b

    def own_copies(iz, which, source, source_step, target, target_step):
        a = pltpu.make_async_copy(source.at[m, iz], target.at[m, iz], own_sem.at[which, 0, iz])
        b = pltpu.make_async_copy(source_step.at[m, iz], target_step.at[m, iz], own_sem.at[which, 1, iz])
        return a, b

    have_table(0)
    forward = (sq, sstep, rq, rstep)
    for iz in range(4):
        deposit(iz)
        rows = slice(iz * 512, iz * 512 + 512)
        for p in range(2):
            value = three(xhi[p, rows, :], xlo[p, rows, :], yin_ref[p, 0], yin_ref[p, 1])
            code, step = coded(value)
            for h in range(2):
                sq[p * 2 + h, iz] = code[:, h * 128 : h * 128 + 128].reshape(8, 4, 16, 128)
                sstep[p * 2 + h, iz] = jnp.broadcast_to(step[:, h * 128 : h * 128 + 128], (8, 128))
        for d in range(1, 4):
            for copy in line_copies(iz, d, *forward, line_send, line_recv):
                copy.start()
        for copy in own_copies(iz, 0, *forward):
            copy.start()

    have_table(1)

    def folded(iz, tz):
        lines = []
        for source in range(4):
            step = rstep[source, iz][0:1, :]
            planes = [decoded(rq[source, iz, :, z].reshape(128, 128), step) for z in (tz, tz + 1)]
            lines.append(jnp.concatenate(planes, axis=1))
        plus = jnp.concatenate([lines[0] + lines[2], lines[1] + lines[3]], axis=0)
        minus = jnp.concatenate([lines[0] - lines[2], lines[1] - lines[3]], axis=0)
        return halves(plus), halves(minus)

    def along_x(p, iz, tz, pair):
        value = three(xin_ref[p, 0], xin_ref[p, 1], pair[0], pair[1])
        for k in range(2):
            spec[(tz + k) * 4 + iz, p * 256 : p * 256 + 256, :] = value[:, k * 128 : k * 128 + 128]

    def share_out(codes, steps, g, right, left):
        top = jnp.max(jnp.maximum(jnp.abs(right), jnp.abs(left)), axis=0, keepdims=True)
        step = jnp.maximum(top, 1e-30) * (1.0 / 32767.0)
        both = jnp.concatenate([right, left], axis=0) * (1.0 / step)
        codes[g] = jnp.round(both).astype(jnp.int32).astype(jnp.int16)
        steps[g] = step

    def share_in(codes, steps, g):
        both = decoded(codes[g], steps[g])
        return both[0:8, :], both[8:16, :]

    def slab_ends(p):
        def block(b, _):
            rows = pl.ds(pl.multiple_of(p * 256 + b * 16, 16), 16)
            rate = rates_ref[0, rows, :]
            planes = [spec[z, rows, :] for z in range(16)]
            right, left = planes[0], planes[15]
            for z in range(1, 16):
                right = right * rate + planes[z]
                left = left * rate + planes[15 - z]
            for k in range(2):
                some = slice(k * 8, k * 8 + 8)
                share_out(ends_out.at[p], ends_step_out.at[p], b * 2 + k, right[some, :], left[some, :])
            return 0

        lax.fori_loop(0, 16, block, 0)
        slab_exchange(p, (ends_out, ends_in, ends_sem), (ends_step_out, ends_step_in, ends_step_sem))

    def slab_exchange(p, *arrays):
        for peer, where in slab_peers():
            for source, target, sem in arrays:
                pltpu.make_async_remote_copy(
                    src_ref=source.at[p, peer], dst_ref=target.at[p, slab],
                    send_sem=sem.at[0, p], recv_sem=sem.at[1, p],
                    device_id=where, device_id_type=LOGICAL,
                ).start()
        for source, target, sem in arrays:
            pltpu.make_async_copy(source.at[p, slab], target.at[p, slab], sem.at[1, p]).start()

    for iz in range(4):
        for d in range(1, 4):
            for copy in line_copies(iz, d, *forward, line_send, line_recv):
                copy.wait_recv()
        for copy in own_copies(iz, 0, *forward):
            copy.wait()
        for tz in range(0, 4, 2):
            plus, minus = folded(iz, tz)
            along_x(0, iz, tz, plus)
            if iz < 3:
                along_x(1, iz, tz, minus)
            else:
                last[tz // 2, 0], last[tz // 2, 1] = minus
    slab_ends(0)
    for tz in range(0, 4, 2):
        along_x(1, 3, tz, (last[tz // 2, 0], last[tz // 2, 1]))
    slab_ends(1)

    def chain(p):
        arrived(ends_in.at[p], ends_sem.at[1, p])
        arrived(ends_step_in.at[p], ends_step_sem.at[1, p])
        rate = rates_ref[0, pl.ds(pl.multiple_of(p * 256 + slab * 8, 8), 8), :]
        r2 = rate * rate
        r4 = r2 * r2
        r8 = r4 * r4
        hop = r8 * r8
        far = hop
        for _ in range(5):
            far = far * far
        far = far * rate
        total_right = total_left = jnp.zeros((8, 128), F32)
        for g in range(32):
            values = share_in(ends_in.at[p], ends_step_in.at[p], g)
            known_ends[g, 0], known_ends[g, 1] = values
            total_right = total_right * hop + values[0]
        for g in range(32):
            total_left = total_left * hop + known_ends[31 - g, 1]
        scale = -rate / (1.0 - far * far)
        right = scale * (total_left - far * total_right)
        left = scale * (total_right - far * total_left)
        for g in range(32):
            known_carry[g, 0] = right
            known_carry[31 - g, 1] = left
            right = right * hop + known_ends[g, 0]
            left = left * hop + known_ends[31 - g, 1]
        for g in range(32):
            share_out(carry_out.at[p], carry_step_out.at[p], g, known_carry[g, 0], known_carry[g, 1])
        slab_exchange(p, (carry_out, carry_in, carry_sem), (carry_step_out, carry_step_in, carry_step_sem))

    chain(0)
    chain(1)

    def filters(p):
        arrived(carry_in.at[p], carry_sem.at[1, p])
        arrived(carry_step_in.at[p], carry_step_sem.at[1, p])

        def block(b, _):
            rows = pl.ds(pl.multiple_of(p * 256 + b * 16, 16), 16)
            rate, gain = rates_ref[0, rows, :], rates_ref[1, rows, :]
            planes = [spec[z, rows, :] for z in range(16)]
            shares = [share_in(carry_in.at[p], carry_step_in.at[p], b * 2 + k) for k in range(2)]
            right = jnp.concatenate([shares[0][0], shares[1][0]], axis=0)
            left = jnp.concatenate([shares[0][1], shares[1][1]], axis=0)
            beyond = [None] * 16
            for z in range(15, -1, -1):
                beyond[z] = left * rate
                left = planes[z] + beyond[z]
            for z in range(16):
                right = planes[z] + right * rate
                high, low = halves((right + beyond[z]) * gain)
                mhi[z, rows, :] = high
                mlo[z, rows, :] = low
            return 0

        lax.fori_loop(0, 16, block, 0)

    filters(0)
    filters(1)

    have_table(2)
    backward = (sq2, sstep2, rq2, rstep2)
    for iz in range(4):
        parts = []
        for tz in range(0, 4, 2):
            sums = []
            for p in range(2):
                rows = slice(p * 256, p * 256 + 256)
                high = jnp.concatenate([mhi[(tz + k) * 4 + iz, rows, :] for k in range(2)], axis=1)
                low = jnp.concatenate([mlo[(tz + k) * 4 + iz, rows, :] for k in range(2)], axis=1)
                sums.append(three(xout_ref[p, 0], xout_ref[p, 1], high, low))
            parts.append((sums[0] + sums[1], sums[0] - sums[1]))
        for target in range(4):
            span = slice((target % 2) * 128, (target % 2) * 128 + 128)
            blocks = []
            for tz in range(4):
                block = parts[tz // 2][target // 2][span, (tz % 2) * 128 : (tz % 2) * 128 + 128]
                blocks.append(block)
            top = blocks[0]
            for block in blocks:
                top = jnp.maximum(jnp.abs(top), jnp.abs(block))
            top = jnp.maximum(jnp.max(top, axis=0, keepdims=True), 1e-30)
            step = top * (1.0 / 32767.0)
            inverse = 1.0 / step
            for tz in range(4):
                code = jnp.round(blocks[tz] * inverse).astype(jnp.int32).astype(jnp.int16)
                sq2[target, iz, :, tz] = code.reshape(8, 16, 128)
            sstep2[target, iz] = jnp.broadcast_to(step, (8, 128))
        for d in range(1, 4):
            for copy in line_copies(iz, d, *backward, back_send, back_recv):
                copy.start()
        for copy in own_copies(iz, 1, *backward):
            copy.start()

    wanted = [
        (known[:, 2 * slot + 1 : 2 * slot + 2] * 64 + known[:, 2 * slot : 2 * slot + 1]).astype(jnp.int32)
        for slot in range(2)
    ]
    wanted = jnp.concatenate(wanted, axis=0)
    fetch[...] = jnp.where(iota((SLOTS, 512), 1) == wanted, 1.0, 0.0).astype(BF16)

    def reply(iz):
        for part in range(4):
            lanes = slice((iz * 4 + part) * 128, (iz * 4 + part) * 128 + 128)
            to_blocks(part, jnp.dot(fetch[...], tiles[:, lanes], preferred_element_type=F32))
        reply_out[iz] = stage[...].astype(BF16).reshape(128, 8, 128)
        exchange(reply_out.at[iz], reply_in.at[iz], reply_send.at[iz], reply_recv.at[iz])

    for iz in range(4):
        for d in range(1, 4):
            for copy in line_copies(iz, d, *backward, back_send, back_recv):
                copy.wait_recv()
        for copy in own_copies(iz, 1, *backward):
            copy.wait()
        sums = []
        for p in range(2):
            pieces = [
                decoded(rq2[p * 2 + h, iz].reshape(512, 128), rstep2[p * 2 + h, iz][0:1, :])
                for h in range(2)
            ]
            high, low = halves(jnp.concatenate(pieces, axis=1))
            sums.append(three(high, low, yin_ref[p, 0], yin_ref[p, 1], True))
        for top, value in enumerate((sums[0] + sums[1], sums[0] - sums[1])):
            for half in range(2):
                lanes = slice(half * 128, half * 128 + 128)
                ty = top * 4 + half * 2
                for pair in range(4):
                    even = value[pair * 128 : pair * 128 + 64, lanes]
                    odd = value[pair * 128 + 64 : pair * 128 + 128, lanes]
                    span = slice((iz * 4 + pair) * 128, (iz * 4 + pair) * 128 + 128)
                    first = jnp.where(low_half, even, pltpu.roll(odd, 64, 1))
                    second = jnp.where(low_half, pltpu.roll(even, 64, 1), odd)
                    tiles[ty * 64 : ty * 64 + 64, span] = first.astype(BF16)
                    tiles[ty * 64 + 64 : ty * 64 + 128, span] = second.astype(BF16)
        reply(iz)

    for iz in range(4):
        arrived(reply_in.at[iz], reply_recv.at[iz])
        stage[...] = reply_in[iz].reshape(1024, 128).astype(F32)
        for part in range(4):
            lanes = slice((iz * 4 + part) * 128, (iz * 4 + part) * 128 + 128)
            out_ref[:, lanes] = jnp.dot(
                unpick[...], from_blocks(part), preferred_element_type=F32
            ).astype(BF16)

    sent(meta_out, meta_sem.at[0])
    for iz in range(4):
        sent(brick_out.at[iz], brick_send.at[iz])
        sent(reply_out.at[iz], reply_send.at[iz])
    both = ((ends_out, ends_sem), (ends_step_out, ends_step_sem), (carry_out, carry_sem), (carry_step_out, carry_step_sem))
    for source, sem in both:
        for p in range(2):
            some = source.at[p, pl.ds(0, 31)]
            pltpu.make_async_copy(some, some, sem.at[0, p]).wait()
    for iz in range(4):
        for d in range(1, 4):
            for copy in line_copies(iz, d, *forward, line_send, line_recv):
                copy.wait_send()
            for copy in line_copies(iz, d, *backward, back_send, back_recv):
                copy.wait_send()


VMEM_LIMIT = 60 * 1024 * 1024


def on_device(bricks, owners, tile_ids, counts):
    vmem = pl.BlockSpec(memory_space=pltpu.VMEM)
    smem = pl.BlockSpec(memory_space=pltpu.SMEM)
    hbm = pl.BlockSpec(memory_space=pl.ANY)
    y_in, x_in, x_out = (jnp.asarray(t) for t in tables())
    codes = pltpu.VMEM((4, 4, 8, 4, 16, 128), jnp.int16)
    steps = pltpu.VMEM((4, 4, 8, 128), F32)
    known = pltpu.VMEM((32, 2, 8, 128), F32)
    share = pltpu.VMEM((2, 32, 16, 128), jnp.int16)
    grain = pltpu.VMEM((2, 32, 1, 128), F32)
    four = pltpu.SemaphoreType.DMA((2, 2))
    blocks = pltpu.VMEM((4, 128, 8, 128), BF16)
    quad = pltpu.SemaphoreType.DMA((4,))
    table = pltpu.VMEM((2, 2, HALF, HALF), BF16)
    notes = pltpu.VMEM((128, 1, 128), F32)
    pair = pltpu.SemaphoreType.DMA((2,))
    line = pltpu.SemaphoreType.DMA((2, 3, 4))
    found = pl.pallas_call(
        field_kernel,
        out_shape=jax.ShapeDtypeStruct((ROWS, CELLS), BF16),
        in_specs=[smem, hbm, vmem, vmem, vmem, hbm, hbm, hbm],
        out_specs=vmem,
        scratch_shapes=[
            pltpu.VMEM((ROWS, CELLS), BF16),
            pltpu.VMEM((2, 512, 128), F32),
            table, table, table,
            pltpu.SemaphoreType.DMA((4,)),
            pltpu.VMEM((1024, 128), F32),
            blocks, blocks, notes, notes,
            pltpu.VMEM((128, 128), F32),
            blocks, blocks,
            pltpu.VMEM((ROWS, SLOTS), BF16),
            pltpu.VMEM((SLOTS, 512), BF16),
            pltpu.VMEM((512, SLOTS), BF16),
            pltpu.VMEM((2, 2048, HALF), BF16),
            pltpu.VMEM((2, 2048, HALF), BF16),
            codes, steps, codes, steps,
            pltpu.VMEM((16, 512, 128), F32),
            pltpu.VMEM((2, 2, HALF, HALF), BF16),
            known, known,
            share, share, share, share, grain, grain, grain, grain,
            pltpu.VMEM((16, 512, 128), BF16),
            pltpu.VMEM((16, 512, 128), BF16),
            codes, steps, codes, steps,
            pltpu.VMEM((512, CELLS), BF16),
            quad, quad, pair, quad, quad, line, line, four, four, four, four, line, line,
            pltpu.SemaphoreType.DMA((2, 2, 4)),
        ],
        compiler_params=pltpu.CompilerParams(
            collective_id=0, has_side_effects=True, vmem_limit_bytes=VMEM_LIMIT
        ),
        name="field",
    )(counts, bricks, owners.reshape(1, ROWS), tile_ids.reshape(1, ROWS), jnp.asarray(second_differences()), y_in, x_in, x_out)
    live = jnp.arange(ROWS, dtype=jnp.int32)[:, None] < counts[0]
    return jnp.where(live, found, jnp.zeros_like(found))


def solution(mesh):
    in_specs = (P(("gz", "ma"), None), P(("gz", "ma"), None), P(("gz", "ma")), P(("gz", "ma")))
    out_specs = P(("gz", "ma"), None)
    return jax.shard_map(
        on_device, mesh=mesh, in_specs=in_specs, out_specs=out_specs, check_vma=False
    )
```

```python
import math

import jax
import jax.numpy as jnp
import ml_dtypes
import numpy as np
from jax import lax
from jax.experimental import pallas as pl
from jax.experimental.pallas import tpu as pltpu
from jax.sharding import PartitionSpec as P

N = 512
HALF = 256
SCREEN = 16
F32 = jnp.float32
BF16 = jnp.bfloat16
LOGICAL = pl.DeviceIdType.LOGICAL
SLOTS = 256
CELLS = 2048
ROWS = 128


def split_table(table):
    high = table.astype(ml_dtypes.bfloat16)
    low = (table - high.astype(np.float64)).astype(ml_dtypes.bfloat16)
    return high, low


def parity_table(parity, points):
    modes = 2 * np.arange(HALF) + parity
    angle = 2.0 * math.pi / N * ((modes[:, None] * points[None, :]) % N)
    return (np.cos(angle) + np.sin(angle)) / math.sqrt(N)


def stacked(tables):
    return np.stack([np.stack(split_table(t)) for t in tables])


def tables():
    natural = np.arange(HALF)
    m, ix, tx = np.meshgrid(np.arange(2), np.arange(8), np.arange(16), indexing="ij")
    order = (m * 128 + tx * 8 + ix).reshape(-1)
    y_tables = [parity_table(p, natural) for p in (0, 1)]
    x_tables = [parity_table(p, order) for p in (0, 1)]
    y_in = stacked([t.T for t in y_tables])
    x_in = stacked(x_tables)
    x_out = stacked([t.T for t in x_tables])
    return y_in, x_in, x_out


def second_differences():
    k = np.arange(128)
    rows = [2 * (128 * (c % 2) + k) + c // 2 for c in range(4)]
    values = (4.0 * np.sin(math.pi / N * np.stack(rows)) ** 2).astype(np.float32)
    return np.concatenate([values, values])


def seat(core, u, v, w, m):
    q = (m - (u + v + w) + 8) % 4
    x = (2 * v + core + q // 2) % 4
    side = 2 * w + q % 2
    y = u + core * (side - u)
    z = side + core * (u - side)
    return y * 32 + x * 8 + core * 4 + z


def handler(owner):
    return seat((owner // 4) % 2, owner // 32, (owner // 16) % 2, (owner // 8) % 2, owner % 4)


def iota(shape, axis):
    return lax.broadcasted_iota(jnp.int32, shape, axis)


def pickers(owners_ref, count):
    row = jnp.broadcast_to(handler(owners_ref[...]), (ROWS, ROWS))
    column = jnp.transpose(row.astype(F32)).astype(jnp.int32)
    target = column[:, 0:1]
    same = column == row
    i, j = iota((ROWS, ROWS), 0), iota((ROWS, ROWS), 1)
    within_column = jnp.sum(jnp.where(same & (j < i), 1.0, 0.0), axis=1, keepdims=True)
    within_row = jnp.sum(jnp.where(same & (i < j), 1.0, 0.0), axis=0, keepdims=True)
    slot_column = target + ROWS * within_column.astype(jnp.int32)
    slot_row = row[0:1, :] + ROWS * within_row.astype(jnp.int32)
    down = (iota((SLOTS, ROWS), 0) == slot_row) & (iota((SLOTS, ROWS), 1) < count)
    across = iota((ROWS, SLOTS), 1) == slot_column
    return jnp.where(down, 1.0, 0.0).astype(BF16), jnp.where(across, 1.0, 0.0).astype(BF16)


def halves(value):
    high = value.astype(BF16)
    return high, (value - high.astype(F32)).astype(BF16)


def three(a_high, a_low, b_high, b_low, turned=False):
    dims = (((1,), (1 if turned else 0,)), ((), ()))
    total = lax.dot_general(a_high, b_high, dims, preferred_element_type=F32)
    total += lax.dot_general(a_high, b_low, dims, preferred_element_type=F32)
    total += lax.dot_general(a_low, b_high, dims, preferred_element_type=F32)
    return total


def coded(value):
    top = jnp.max(jnp.abs(value), axis=0, keepdims=True)
    step = jnp.maximum(top, 1e-30) * (1.0 / 32767.0)
    return jnp.round(value * (1.0 / step)).astype(jnp.int32).astype(jnp.int16), step


def decoded(code, step):
    return code.astype(jnp.int32).astype(F32) * step


def field_kernel(
    counts_ref, bricks_hbm, owners_ref, ids_ref, lam_ref, yin_hbm, xin_hbm, xout_hbm, out_ref,
    bricks_ref, rates_ref, yin_ref, xin_ref, xout_ref, table_sem,
    stage, brick_out, brick_in, meta_out, meta_in, meta, reply_out, reply_in, unpick, fetch, place, xhi, xlo, sq, sstep, rq, rstep, spec, last, known_ends, known_carry,
    ends_out, ends_in, carry_out, carry_in, ends_step_out, ends_step_in, carry_step_out, carry_step_in,
    powers, flow, early, sq2, sstep2, rq2, rstep2, tiles,
    brick_send, brick_recv, meta_sem, reply_send, reply_recv, line_send, line_recv, ends_sem, carry_sem, ends_step_sem, carry_step_sem, back_send, back_recv, own_sem,
):
    gz, ma = lax.axis_index("gz"), lax.axis_index("ma")
    y, x, core = gz // 8, (gz // 2) % 4, gz % 2
    me = gz * 4 + ma
    shifted = (x + 4 - core) % 4
    u, side = y + core * (ma - y), ma + core * (y - ma)
    v, w = shifted // 2, side // 2
    m = (2 * (shifted % 2) + side % 2 + u + v + w) % 4
    slab = u * 8 + v * 4 + w * 2 + core

    def wrap(value, size):
        return jnp.where(value >= size, value - size, value)

    def line_peer(p):
        return seat(core, u, v, w, p)

    def slab_peers():
        for du in range(4):
            pu = wrap(u + du, 4)
            for dv in range(2):
                pv = v if dv == 0 else 1 - v
                for dw in range(2):
                    pw = w if dw == 0 else 1 - w
                    for dc in range(2):
                        if du or dv or dw or dc:
                            pc = core if dc == 0 else 1 - core
                            yield pu * 8 + pv * 4 + pw * 2 + pc, seat(pc, pu, pv, pw, m)

    def peers(body):
        def step(i, _):
            for k in range(8):
                body(wrap(me + (i * 8 + k + 1), 128))
            return 0

        lax.fori_loop(0, 15, step, 0)
        for d in range(121, 128):
            body(wrap(me + d, 128))

    pltpu.make_async_copy(bricks_hbm, bricks_ref, table_sem.at[3]).start()
    tables = ((yin_hbm, yin_ref), (xin_hbm, xin_ref), (xout_hbm, xout_ref))
    def have_table(i):
        pltpu.make_async_copy(*tables[i], table_sem.at[i]).wait()

    barrier = pltpu.get_barrier_semaphore()
    peers(lambda n: pl.semaphore_signal(barrier, inc=1, device_id=n, device_id_type=LOGICAL))

    def exchange(source, target, send, recv):
        def start(n):
            pltpu.make_async_remote_copy(
                src_ref=source.at[n], dst_ref=target.at[me], send_sem=send, recv_sem=recv,
                device_id=n, device_id_type=LOGICAL,
            ).start()

        peers(start)
        pltpu.make_async_copy(source.at[me], target.at[me], recv).start()

    def arrived(target, recv):
        pltpu.make_async_copy(target, target, recv).wait()

    def sent(source, send):
        some = source.at[pl.ds(0, 127)]
        pltpu.make_async_copy(some, some, send).wait()

    def to_blocks(part, block):
        for slot in range(2):
            stage[pl.ds(slot * 4 + part, 128, stride=8), :] = block[slot * 128 : slot * 128 + 128, :]

    def from_blocks(part):
        slots = [stage[pl.ds(slot * 4 + part, 128, stride=8), :] for slot in range(2)]
        return jnp.concatenate(slots, axis=0).astype(BF16)

    for i, (source, target) in enumerate(tables):
        pltpu.make_async_copy(source, target, table_sem.at[i]).start()

    pick, unpick[...] = pickers(owners_ref, counts_ref[0])
    pltpu.make_async_copy(bricks_hbm, bricks_ref, table_sem.at[3]).wait()

    def send_bricks(iz):
        for part in range(4):
            lanes = slice((iz * 4 + part) * 128, (iz * 4 + part) * 128 + 128)
            to_blocks(part, jnp.dot(pick, bricks_ref[:, lanes], preferred_element_type=F32))
        brick_out[iz] = stage[...].astype(BF16).reshape(128, 8, 128)
        if iz == 0:
            pl.semaphore_wait(barrier, 127)
        exchange(brick_out.at[iz], brick_in.at[iz], brick_send.at[iz], brick_recv.at[iz])

    send_bricks(0)
    ids = ids_ref[...]
    lane_row = iota((ROWS, ROWS), 0)
    for slot in range(2):
        info = jnp.where(lane_row == 2 * slot, ids // 8, jnp.where(lane_row == 2 * slot + 1, ids % 8, 0))
        info = jnp.transpose(info.astype(F32)).astype(BF16)
        part = jnp.dot(pick[slot * 128 : slot * 128 + 128, :], info, preferred_element_type=F32)
        meta[...] = part if slot == 0 else meta[...] + part

    def spread(i, _):
        for k in range(8):
            meta_out[i * 8 + k] = meta[pl.ds(i * 8 + k, 1), :]
        return 0

    lax.fori_loop(0, 16, spread, 0)
    exchange(meta_out, meta_in, meta_sem.at[0], meta_sem.at[1])
    for iz in range(1, 4):
        send_bricks(iz)

    others = list(slab_peers())

    lam_k = lam_ref[pl.ds(4 + m, 1), :]
    for block in range(4):
        lam_j = jnp.transpose(jnp.broadcast_to(lam_ref[block : block + 1, :], (128, 128)))
        excess = 1.0 / (SCREEN * SCREEN) + lam_j + lam_k
        root = jnp.sqrt(excess * (excess + 4.0))
        rows = slice(block * 128, block * 128 + 128)
        rates_ref[0, rows, :] = 2.0 / (2.0 + excess + root)
        rates_ref[1, rows, :] = 1.0 / root

    def raise_rates(b, _):
        rows = pl.ds(pl.multiple_of(b * 32, 32), 32)
        rate = rates_ref[0, rows, :]
        power = jnp.ones((32, 128), F32)
        for z in range(16):
            powers[z, rows, :] = power
            power = power * rate
        return 0

    lax.fori_loop(0, 16, raise_rates, 0)

    arrived(meta_in, meta_sem.at[1])

    def collect(i, _):
        for k in range(8):
            meta[pl.ds(i * 8 + k, 1), :] = meta_in[i * 8 + k]
        return 0

    lax.fori_loop(0, 16, collect, 0)

    known = meta[...]
    meta_rows = jnp.transpose(known)
    q_row = jnp.concatenate([meta_rows[0:1, :], meta_rows[2:3, :]], axis=1).astype(jnp.int32)
    ty_row = jnp.concatenate([meta_rows[1:2, :], meta_rows[3:4, :]], axis=1).astype(jnp.int32)
    for p in range(2):
        for ty in range(4):
            hit = q_row == iota((64, SLOTS), 0)
            second = -1.0 if p else 1.0
            value = jnp.where(ty_row == ty, 1.0, 0.0) + jnp.where(ty_row == ty + 4, second, 0.0)
            first = (p * 4 + ty) * 64
            place[first : first + 64, :] = jnp.where(hit, value, 0.0).astype(BF16)
    low_half = iota((64, 128), 1) < 64

    def deposit(iz):
        arrived(brick_in.at[iz], brick_recv.at[iz])
        stage[...] = brick_in[iz].reshape(1024, 128).astype(F32)
        for pair in range(4):
            laid = jnp.dot(place[...], from_blocks(pair), preferred_element_type=F32)
            for p in range(2):
                for side in range(2):
                    first = (p * 4 + side * 2) * 64
                    te, to = laid[first : first + 64, :], laid[first + 64 : first + 128, :]
                    even = jnp.where(low_half, te, pltpu.roll(to, 64, 1))
                    odd = jnp.where(low_half, pltpu.roll(te, 64, 1), to)
                    for k, value in enumerate((even, odd)):
                        row = (iz * 8 + pair * 2 + k) * 64
                        high, low = halves(value)
                        xhi[p, row : row + 64, side * 128 : side * 128 + 128] = high
                        xlo[p, row : row + 64, side * 128 : side * 128 + 128] = low

    def line_copies(iz, d, source, source_step, target, target_step, send, recv):
        peer = (m + d) % 4
        a = pltpu.make_async_remote_copy(
            src_ref=source.at[peer, iz], dst_ref=target.at[m, iz],
            send_sem=send.at[0, d - 1, iz], recv_sem=recv.at[0, d - 1, iz],
            device_id=line_peer(peer), device_id_type=LOGICAL,
        )
        b = pltpu.make_async_remote_copy(
            src_ref=source_step.at[peer, iz], dst_ref=target_step.at[m, iz],
            send_sem=send.at[1, d - 1, iz], recv_sem=recv.at[1, d - 1, iz],
            device_id=line_peer(peer), device_id_type=LOGICAL,
        )
        return a, b

    def own_copies(iz, which, source, source_step, target, target_step):
        a = pltpu.make_async_copy(source.at[m, iz], target.at[m, iz], own_sem.at[which, 0, iz])
        b = pltpu.make_async_copy(source_step.at[m, iz], target_step.at[m, iz], own_sem.at[which, 1, iz])
        return a, b

    have_table(0)
    forward = (sq, sstep, rq, rstep)
    for iz in range(4):
        deposit(iz)
        rows = slice(iz * 512, iz * 512 + 512)
        for p in range(2):
            value = three(xhi[p, rows, :], xlo[p, rows, :], yin_ref[p, 0], yin_ref[p, 1])
            code, step = coded(value)
            for h in range(2):
                sq[p * 2 + h, iz] = code[:, h * 128 : h * 128 + 128].reshape(8, 4, 16, 128)
                sstep[p * 2 + h, iz] = jnp.broadcast_to(step[:, h * 128 : h * 128 + 128], (8, 128))
        for d in range(1, 4):
            for copy in line_copies(iz, d, *forward, line_send, line_recv):
                copy.start()
        for copy in own_copies(iz, 0, *forward):
            copy.start()

    have_table(1)

    def folded(iz, tz):
        lines = []
        for source in range(4):
            step = rstep[source, iz][0:1, :]
            planes = [decoded(rq[source, iz, :, z].reshape(128, 128), step) for z in (tz, tz + 1)]
            lines.append(jnp.concatenate(planes, axis=1))
        plus = jnp.concatenate([lines[0] + lines[2], lines[1] + lines[3]], axis=0)
        minus = jnp.concatenate([lines[0] - lines[2], lines[1] - lines[3]], axis=0)
        return halves(plus), halves(minus)

    def along_x(p, iz, tz, pair):
        value = three(xin_ref[p, 0], xin_ref[p, 1], pair[0], pair[1])
        rows = slice(p * 256, p * 256 + 256)
        right = left = None
        for k in range(2):
            z, plane = (tz + k) * 4 + iz, value[:, k * 128 : k * 128 + 128]
            spec[z, rows, :] = plane
            to_right, to_left = plane * powers[15 - z, rows, :], plane * powers[z, rows, :]
            right = to_right if right is None else right + to_right
            left = to_left if left is None else left + to_left
        if iz == 0 and tz == 0:
            flow[0, rows, :], flow[1, rows, :] = right, left
        else:
            flow[0, rows, :] += right
            flow[1, rows, :] += left

    def share_out(codes, steps, g, right, left):
        top = jnp.max(jnp.maximum(jnp.abs(right), jnp.abs(left)), axis=0, keepdims=True)
        step = jnp.maximum(top, 1e-30) * (1.0 / 32767.0)
        both = jnp.concatenate([right, left], axis=0) * (1.0 / step)
        codes[g] = jnp.round(both).astype(jnp.int32).astype(jnp.int16)
        steps[g] = step

    def share_in(codes, steps, g):
        both = decoded(codes[g], steps[g])
        return both[0:8, :], both[8:16, :]

    def slab_ends(p):
        def block(b, _):
            for k in range(8):
                rows = pl.ds(pl.multiple_of(p * 256 + b * 64 + k * 8, 8), 8)
                share_out(ends_out.at[p], ends_step_out.at[p], b * 8 + k, flow[0, rows, :], flow[1, rows, :])
            return 0

        lax.fori_loop(0, 4, block, 0)
        slab_exchange(p, (ends_out, ends_in, ends_sem), (ends_step_out, ends_step_in, ends_step_sem))

    def slab_exchange(p, *arrays):
        for peer, where in others:
            for source, target, sem in arrays:
                pltpu.make_async_remote_copy(
                    src_ref=source.at[p, peer], dst_ref=target.at[p, slab],
                    send_sem=sem.at[0, p], recv_sem=sem.at[1, p],
                    device_id=where, device_id_type=LOGICAL,
                ).start()
        for source, target, sem in arrays:
            pltpu.make_async_copy(source.at[p, slab], target.at[p, slab], sem.at[1, p]).start()

    for iz in range(4):
        for d in range(1, 4):
            for copy in line_copies(iz, d, *forward, line_send, line_recv):
                copy.wait_recv()
        for copy in own_copies(iz, 0, *forward):
            copy.wait()
        for tz in range(0, 4, 2):
            plus, minus = folded(iz, tz)
            along_x(0, iz, tz, plus)
            if iz < 3:
                along_x(1, iz, tz, minus)
            else:
                last[tz // 2, 0], last[tz // 2, 1] = minus
    slab_ends(0)
    for tz in range(0, 4, 2):
        along_x(1, 3, tz, (last[tz // 2, 0], last[tz // 2, 1]))
    slab_ends(1)

    def chain(p):
        arrived(ends_in.at[p], ends_sem.at[1, p])
        arrived(ends_step_in.at[p], ends_step_sem.at[1, p])
        some = pl.ds(pl.multiple_of(p * 256 + slab * 8, 8), 8)
        rate = rates_ref[0, some, :]
        weight = rate * rates_ref[1, some, :]
        r2 = rate * rate
        r4 = r2 * r2
        r8 = r4 * r4
        hop = r8 * r8
        far = hop
        for _ in range(5):
            far = far * far
        far = far * rate
        total_right = total_left = jnp.zeros((8, 128), F32)
        for g in range(32):
            values = share_in(ends_in.at[p], ends_step_in.at[p], g)
            known_ends[g, 0], known_ends[g, 1] = values
            total_right = total_right * hop + values[0]
        for g in range(32):
            total_left = total_left * hop + known_ends[31 - g, 1]
        scale = -rate / (1.0 - far * far)
        right = scale * (total_left - far * total_right)
        left = scale * (total_right - far * total_left)
        for g in range(32):
            known_carry[g, 0] = right * weight
            known_carry[31 - g, 1] = left * weight
            right = right * hop + known_ends[g, 0]
            left = left * hop + known_ends[31 - g, 1]
        for g in range(32):
            share_out(carry_out.at[p], carry_step_out.at[p], g, known_carry[g, 0], known_carry[g, 1])
        slab_exchange(p, (carry_out, carry_in, carry_sem), (carry_step_out, carry_step_in, carry_step_sem))

    def filters(p):
        def block(b, _):
            rows = pl.ds(pl.multiple_of(p * 256 + b * 16, 16), 16)
            rate, gain = rates_ref[0, rows, :], rates_ref[1, rows, :]
            planes = [spec[z, rows, :] for z in range(16)]
            beyond, left = [None] * 16, planes[15]
            for z in range(14, -1, -1):
                beyond[z] = left * rate
                left = planes[z] + beyond[z]
            right = planes[0]
            for z in range(16):
                if z:
                    right = planes[z] + right * rate
                both = right if z == 15 else right + beyond[z]
                spec[z, rows, :] = both * gain
            return 0

        lax.fori_loop(0, 16, block, 0)

    def carries(p):
        arrived(carry_in.at[p], carry_sem.at[1, p])
        arrived(carry_step_in.at[p], carry_step_sem.at[1, p])
        for g in range(32):
            rows = slice(p * 256 + g * 8, p * 256 + g * 8 + 8)
            flow[0, rows, :], flow[1, rows, :] = share_in(carry_in.at[p], carry_step_in.at[p], g)

    def back_along_x(p, iz, tz):
        rows = slice(p * 256, p * 256 + 256)
        planes = []
        for z in (tz * 4 + iz, tz * 4 + 4 + iz):
            planes.append(
                spec[z, rows, :]
                + flow[0, rows, :] * powers[z, rows, :]
                + flow[1, rows, :] * powers[15 - z, rows, :]
            )
        high, low = halves(jnp.concatenate(planes, axis=1))
        return three(xout_ref[p, 0], xout_ref[p, 1], high, low)

    filters(0)
    filters(1)
    chain(0)
    chain(1)
    have_table(2)
    carries(0)
    for tz in range(0, 4, 2):
        early[tz // 2] = back_along_x(0, 0, tz)
    carries(1)

    backward = (sq2, sstep2, rq2, rstep2)
    for iz in range(4):
        parts = []
        for tz in range(0, 4, 2):
            even = early[tz // 2] if iz == 0 else back_along_x(0, iz, tz)
            odd = back_along_x(1, iz, tz)
            parts.append((even + odd, even - odd))
        for target in range(4):
            span = slice((target % 2) * 128, (target % 2) * 128 + 128)
            blocks = []
            for tz in range(4):
                block = parts[tz // 2][target // 2][span, (tz % 2) * 128 : (tz % 2) * 128 + 128]
                blocks.append(block)
            top = blocks[0]
            for block in blocks:
                top = jnp.maximum(jnp.abs(top), jnp.abs(block))
            top = jnp.maximum(jnp.max(top, axis=0, keepdims=True), 1e-30)
            step = top * (1.0 / 32767.0)
            inverse = 1.0 / step
            for tz in range(4):
                code = jnp.round(blocks[tz] * inverse).astype(jnp.int32).astype(jnp.int16)
                sq2[target, iz, :, tz] = code.reshape(8, 16, 128)
            sstep2[target, iz] = jnp.broadcast_to(step, (8, 128))
        for d in range(1, 4):
            for copy in line_copies(iz, d, *backward, back_send, back_recv):
                copy.start()
        for copy in own_copies(iz, 1, *backward):
            copy.start()

    wanted = [
        (known[:, 2 * slot + 1 : 2 * slot + 2] * 64 + known[:, 2 * slot : 2 * slot + 1]).astype(jnp.int32)
        for slot in range(2)
    ]
    wanted = jnp.concatenate(wanted, axis=0)
    fetch[...] = jnp.where(iota((SLOTS, 512), 1) == wanted, 1.0, 0.0).astype(BF16)

    def reply(iz):
        for part in range(4):
            lanes = slice((iz * 4 + part) * 128, (iz * 4 + part) * 128 + 128)
            to_blocks(part, jnp.dot(fetch[...], tiles[:, lanes], preferred_element_type=F32))
        reply_out[iz] = stage[...].astype(BF16).reshape(128, 8, 128)
        exchange(reply_out.at[iz], reply_in.at[iz], reply_send.at[iz], reply_recv.at[iz])

    for iz in range(4):
        for d in range(1, 4):
            for copy in line_copies(iz, d, *backward, back_send, back_recv):
                copy.wait_recv()
        for copy in own_copies(iz, 1, *backward):
            copy.wait()
        sums = []
        for p in range(2):
            pieces = [
                decoded(rq2[p * 2 + h, iz].reshape(512, 128), rstep2[p * 2 + h, iz][0:1, :])
                for h in range(2)
            ]
            high, low = halves(jnp.concatenate(pieces, axis=1))
            sums.append(three(high, low, yin_ref[p, 0], yin_ref[p, 1], True))
        for top, value in enumerate((sums[0] + sums[1], sums[0] - sums[1])):
            for half in range(2):
                lanes = slice(half * 128, half * 128 + 128)
                ty = top * 4 + half * 2
                for pair in range(4):
                    even = value[pair * 128 : pair * 128 + 64, lanes]
                    odd = value[pair * 128 + 64 : pair * 128 + 128, lanes]
                    span = slice((iz * 4 + pair) * 128, (iz * 4 + pair) * 128 + 128)
                    first = jnp.where(low_half, even, pltpu.roll(odd, 64, 1))
                    second = jnp.where(low_half, pltpu.roll(even, 64, 1), odd)
                    tiles[ty * 64 : ty * 64 + 64, span] = first.astype(BF16)
                    tiles[ty * 64 + 64 : ty * 64 + 128, span] = second.astype(BF16)
        reply(iz)

    for iz in range(4):
        arrived(reply_in.at[iz], reply_recv.at[iz])
        stage[...] = reply_in[iz].reshape(1024, 128).astype(F32)
        for part in range(4):
            lanes = slice((iz * 4 + part) * 128, (iz * 4 + part) * 128 + 128)
            out_ref[:, lanes] = jnp.dot(
                unpick[...], from_blocks(part), preferred_element_type=F32
            ).astype(BF16)

    sent(meta_out, meta_sem.at[0])
    for iz in range(4):
        sent(brick_out.at[iz], brick_send.at[iz])
        sent(reply_out.at[iz], reply_send.at[iz])
    both = ((ends_out, ends_sem), (ends_step_out, ends_step_sem), (carry_out, carry_sem), (carry_step_out, carry_step_sem))
    for source, sem in both:
        for p in range(2):
            some = source.at[p, pl.ds(0, 31)]
            pltpu.make_async_copy(some, some, sem.at[0, p]).wait()
    for iz in range(4):
        for d in range(1, 4):
            for copy in line_copies(iz, d, *forward, line_send, line_recv):
                copy.wait_send()
            for copy in line_copies(iz, d, *backward, back_send, back_recv):
                copy.wait_send()


VMEM_LIMIT = 60 * 1024 * 1024


def on_device(bricks, owners, tile_ids, counts):
    vmem = pl.BlockSpec(memory_space=pltpu.VMEM)
    smem = pl.BlockSpec(memory_space=pltpu.SMEM)
    hbm = pl.BlockSpec(memory_space=pl.ANY)
    y_in, x_in, x_out = (jnp.asarray(t) for t in tables())
    codes = pltpu.VMEM((4, 4, 8, 4, 16, 128), jnp.int16)
    steps = pltpu.VMEM((4, 4, 8, 128), F32)
    known = pltpu.VMEM((32, 2, 8, 128), F32)
    share = pltpu.VMEM((2, 32, 16, 128), jnp.int16)
    grain = pltpu.VMEM((2, 32, 1, 128), F32)
    four = pltpu.SemaphoreType.DMA((2, 2))
    blocks = pltpu.VMEM((4, 128, 8, 128), BF16)
    quad = pltpu.SemaphoreType.DMA((4,))
    table = pltpu.VMEM((2, 2, HALF, HALF), BF16)
    notes = pltpu.VMEM((128, 1, 128), F32)
    pair = pltpu.SemaphoreType.DMA((2,))
    line = pltpu.SemaphoreType.DMA((2, 3, 4))
    found = pl.pallas_call(
        field_kernel,
        out_shape=jax.ShapeDtypeStruct((ROWS, CELLS), BF16),
        in_specs=[smem, hbm, vmem, vmem, vmem, hbm, hbm, hbm],
        out_specs=vmem,
        scratch_shapes=[
            pltpu.VMEM((ROWS, CELLS), BF16),
            pltpu.VMEM((2, 512, 128), F32),
            table, table, table,
            pltpu.SemaphoreType.DMA((4,)),
            pltpu.VMEM((1024, 128), F32),
            blocks, blocks, notes, notes,
            pltpu.VMEM((128, 128), F32),
            blocks, blocks,
            pltpu.VMEM((ROWS, SLOTS), BF16),
            pltpu.VMEM((SLOTS, 512), BF16),
            pltpu.VMEM((512, SLOTS), BF16),
            pltpu.VMEM((2, 2048, HALF), BF16),
            pltpu.VMEM((2, 2048, HALF), BF16),
            codes, steps, codes, steps,
            pltpu.VMEM((16, 512, 128), F32),
            pltpu.VMEM((2, 2, HALF, HALF), BF16),
            known, known,
            share, share, share, share, grain, grain, grain, grain,
            pltpu.VMEM((16, 512, 128), F32),
            pltpu.VMEM((2, 512, 128), F32),
            pltpu.VMEM((2, HALF, HALF), F32),
            codes, steps, codes, steps,
            pltpu.VMEM((512, CELLS), BF16),
            quad, quad, pair, quad, quad, line, line, four, four, four, four, line, line,
            pltpu.SemaphoreType.DMA((2, 2, 4)),
        ],
        compiler_params=pltpu.CompilerParams(
            collective_id=0, has_side_effects=True, vmem_limit_bytes=VMEM_LIMIT
        ),
        name="field",
    )(counts, bricks, owners.reshape(1, ROWS), tile_ids.reshape(1, ROWS), jnp.asarray(second_differences()), y_in, x_in, x_out)
    live = jnp.arange(ROWS, dtype=jnp.int32)[:, None] < counts[0]
    return jnp.where(live, found, jnp.zeros_like(found))


def solution(mesh):
    in_specs = (P(("gz", "ma"), None), P(("gz", "ma"), None), P(("gz", "ma")), P(("gz", "ma")))
    out_specs = P(("gz", "ma"), None)
    return jax.shard_map(
        on_device, mesh=mesh, in_specs=in_specs, out_specs=out_specs, check_vma=False
    )
```

```python
import math

import jax
import jax.numpy as jnp
import ml_dtypes
import numpy as np
from jax import lax
from jax.experimental import pallas as pl
from jax.experimental.pallas import tpu as pltpu
from jax.sharding import PartitionSpec as P

N = 512
HALF = 256
SCREEN = 16
F32 = jnp.float32
BF16 = jnp.bfloat16
LOGICAL = pl.DeviceIdType.LOGICAL
SLOTS = 256
CELLS = 2048
ROWS = 128


def split_table(table):
    high = table.astype(ml_dtypes.bfloat16)
    low = (table - high.astype(np.float64)).astype(ml_dtypes.bfloat16)
    return high, low


def parity_table(parity, points):
    modes = 2 * np.arange(HALF) + parity
    angle = 2.0 * math.pi / N * ((modes[:, None] * points[None, :]) % N)
    return (np.cos(angle) + np.sin(angle)) / math.sqrt(N)


def stacked(tables):
    return np.stack([np.stack(split_table(t)) for t in tables])


def tables():
    natural = np.arange(HALF)
    m, ix, tx = np.meshgrid(np.arange(2), np.arange(8), np.arange(16), indexing="ij")
    order = (m * 128 + tx * 8 + ix).reshape(-1)
    y_tables = [parity_table(p, natural) for p in (0, 1)]
    x_tables = [parity_table(p, order) for p in (0, 1)]
    y_in = stacked([t.T for t in y_tables])
    x_in = stacked(x_tables)
    x_out = stacked([t.T for t in x_tables])
    return np.stack([y_in, x_in, x_out])


def second_differences():
    k = np.arange(128)
    rows = [2 * (128 * (c % 2) + k) + c // 2 for c in range(4)]
    values = (4.0 * np.sin(math.pi / N * np.stack(rows)) ** 2).astype(np.float32)
    return np.concatenate([values, values])


def seat(core, u, v, w, m):
    q = (m - (u + v + w) + 8) % 4
    x = (2 * v + core + q // 2) % 4
    side = 2 * w + q % 2
    y = u + core * (side - u)
    z = side + core * (u - side)
    return y * 32 + x * 8 + core * 4 + z


def handler(owner):
    return seat((owner // 4) % 2, owner // 32, (owner // 16) % 2, (owner // 8) % 2, owner % 4)


def iota(shape, axis):
    return lax.broadcasted_iota(jnp.int32, shape, axis)


def pickers(owners_ref, count):
    row = jnp.broadcast_to(handler(owners_ref[...]), (ROWS, ROWS))
    column = jnp.transpose(row.astype(F32)).astype(jnp.int32)
    target = column[:, 0:1]
    same = column == row
    i, j = iota((ROWS, ROWS), 0), iota((ROWS, ROWS), 1)
    within_column = jnp.sum(jnp.where(same & (j < i), 1.0, 0.0), axis=1, keepdims=True)
    within_row = jnp.sum(jnp.where(same & (i < j), 1.0, 0.0), axis=0, keepdims=True)
    slot_column = target + ROWS * within_column.astype(jnp.int32)
    slot_row = row[0:1, :] + ROWS * within_row.astype(jnp.int32)
    down = (iota((SLOTS, ROWS), 0) == slot_row) & (iota((SLOTS, ROWS), 1) < count)
    across = iota((ROWS, SLOTS), 1) == slot_column
    return jnp.where(down, 1.0, 0.0).astype(BF16), jnp.where(across, 1.0, 0.0).astype(BF16)


def halves(value):
    high = value.astype(BF16)
    return high, (value - high.astype(F32)).astype(BF16)


def three(a_high, a_low, b_high, b_low, turned=False):
    dims = (((1,), (1 if turned else 0,)), ((), ()))
    total = lax.dot_general(a_high, b_high, dims, preferred_element_type=F32)
    total += lax.dot_general(a_high, b_low, dims, preferred_element_type=F32)
    total += lax.dot_general(a_low, b_high, dims, preferred_element_type=F32)
    return total


def coded(value):
    top = jnp.max(jnp.abs(value), axis=0, keepdims=True)
    step = jnp.maximum(top, 1e-30) * (1.0 / 32767.0)
    return jnp.round(value * (1.0 / step)).astype(jnp.int32).astype(jnp.int16), step


def decoded(code, step):
    return code.astype(jnp.int32).astype(F32) * step


def field_kernel(
    counts_ref, bricks_hbm, owners_ref, ids_ref, lam_ref, tables_hbm, out_ref,
    bricks_ref, rates_ref, yin_ref, xin_ref, xout_ref, table_sem,
    stage, brick_out, brick_in, meta_out, meta_in, meta, reply_out, reply_in, unpick, fetch, place, xhi, xlo, sq, sstep, rq, rstep, spec, last, known_ends, known_carry,
    ends_out, ends_in, carry_out, carry_in, ends_step_out, ends_step_in, carry_step_out, carry_step_in,
    powers, flow, early, sq2, sstep2, rq2, rstep2, tiles,
    brick_send, brick_recv, meta_sem, reply_send, reply_recv, line_send, line_recv, ends_sem, carry_sem, ends_step_sem, carry_step_sem, back_send, back_recv, own_sem,
):
    gz, ma = lax.axis_index("gz"), lax.axis_index("ma")
    y, x, core = gz // 8, (gz // 2) % 4, gz % 2
    me = gz * 4 + ma
    shifted = (x + 4 - core) % 4
    u, side = y + core * (ma - y), ma + core * (y - ma)
    v, w = shifted // 2, side // 2
    m = (2 * (shifted % 2) + side % 2 + u + v + w) % 4
    slab = u * 8 + v * 4 + w * 2 + core

    def wrap(value, size):
        return jnp.where(value >= size, value - size, value)

    def line_peer(p):
        return seat(core, u, v, w, p)

    def slab_peers():
        for du in range(4):
            pu = wrap(u + du, 4)
            for dv in range(2):
                pv = v if dv == 0 else 1 - v
                for dw in range(2):
                    pw = w if dw == 0 else 1 - w
                    for dc in range(2):
                        if du or dv or dw or dc:
                            pc = core if dc == 0 else 1 - core
                            yield pu * 8 + pv * 4 + pw * 2 + pc, seat(pc, pu, pv, pw, m)

    def peers(body):
        def step(i, _):
            for k in range(8):
                body(wrap(me + (i * 8 + k + 1), 128))
            return 0

        lax.fori_loop(0, 15, step, 0)
        for d in range(121, 128):
            body(wrap(me + d, 128))

    pltpu.make_async_copy(bricks_hbm, bricks_ref, table_sem.at[3]).start()
    tables = [(tables_hbm.at[i], ref) for i, ref in enumerate((yin_ref, xin_ref, xout_ref))]
    def have_table(i):
        pltpu.make_async_copy(*tables[i], table_sem.at[i]).wait()

    barrier = pltpu.get_barrier_semaphore()
    peers(lambda n: pl.semaphore_signal(barrier, inc=1, device_id=n, device_id_type=LOGICAL))

    def exchange(source, target, send, recv):
        def start(n):
            pltpu.make_async_remote_copy(
                src_ref=source.at[n], dst_ref=target.at[me], send_sem=send, recv_sem=recv,
                device_id=n, device_id_type=LOGICAL,
            ).start()

        peers(start)
        pltpu.make_async_copy(source.at[me], target.at[me], recv).start()

    def arrived(target, recv):
        pltpu.make_async_copy(target, target, recv).wait()

    def sent(source, send):
        some = source.at[pl.ds(0, 127)]
        pltpu.make_async_copy(some, some, send).wait()

    def to_blocks(part, block):
        for slot in range(2):
            stage[pl.ds(slot * 4 + part, 128, stride=8), :] = block[slot * 128 : slot * 128 + 128, :]

    def from_blocks(part):
        slots = [stage[pl.ds(slot * 4 + part, 128, stride=8), :] for slot in range(2)]
        return jnp.concatenate(slots, axis=0).astype(BF16)

    for i, (source, target) in enumerate(tables):
        pltpu.make_async_copy(source, target, table_sem.at[i]).start()

    pick, unpick[...] = pickers(owners_ref, counts_ref[0])
    pltpu.make_async_copy(bricks_hbm, bricks_ref, table_sem.at[3]).wait()

    def send_bricks(iz):
        for part in range(4):
            lanes = slice((iz * 4 + part) * 128, (iz * 4 + part) * 128 + 128)
            to_blocks(part, jnp.dot(pick, bricks_ref[:, lanes], preferred_element_type=F32))
        brick_out[iz] = stage[...].astype(BF16).reshape(128, 8, 128)
        if iz == 0:
            pl.semaphore_wait(barrier, 127)
        exchange(brick_out.at[iz], brick_in.at[iz], brick_send.at[iz], brick_recv.at[iz])

    send_bricks(0)
    ids = ids_ref[...]
    lane_row = iota((ROWS, ROWS), 0)
    for slot in range(2):
        info = jnp.where(lane_row == 2 * slot, ids // 8, jnp.where(lane_row == 2 * slot + 1, ids % 8, 0))
        info = jnp.transpose(info.astype(F32)).astype(BF16)
        part = jnp.dot(pick[slot * 128 : slot * 128 + 128, :], info, preferred_element_type=F32)
        meta[...] = part if slot == 0 else meta[...] + part

    def spread(i, _):
        for k in range(8):
            meta_out[i * 8 + k] = meta[pl.ds(i * 8 + k, 1), :]
        return 0

    lax.fori_loop(0, 16, spread, 0)
    exchange(meta_out, meta_in, meta_sem.at[0], meta_sem.at[1])
    for iz in range(1, 4):
        send_bricks(iz)

    others = list(slab_peers())

    lam_k = lam_ref[pl.ds(4 + m, 1), :]
    for block in range(4):
        lam_j = jnp.transpose(jnp.broadcast_to(lam_ref[block : block + 1, :], (128, 128)))
        excess = 1.0 / (SCREEN * SCREEN) + lam_j + lam_k
        root = jnp.sqrt(excess * (excess + 4.0))
        rows = slice(block * 128, block * 128 + 128)
        rates_ref[0, rows, :] = 2.0 / (2.0 + excess + root)
        rates_ref[1, rows, :] = 1.0 / root

    def raise_rates(b, _):
        rows = pl.ds(pl.multiple_of(b * 32, 32), 32)
        rate = rates_ref[0, rows, :]
        power = jnp.ones((32, 128), F32)
        for z in range(16):
            powers[z, rows, :] = power
            power = power * rate
        return 0

    lax.fori_loop(0, 16, raise_rates, 0)

    arrived(meta_in, meta_sem.at[1])

    def collect(i, _):
        for k in range(8):
            meta[pl.ds(i * 8 + k, 1), :] = meta_in[i * 8 + k]
        return 0

    lax.fori_loop(0, 16, collect, 0)

    known = meta[...]
    meta_rows = jnp.transpose(known)
    q_row = jnp.concatenate([meta_rows[0:1, :], meta_rows[2:3, :]], axis=1).astype(jnp.int32)
    ty_row = jnp.concatenate([meta_rows[1:2, :], meta_rows[3:4, :]], axis=1).astype(jnp.int32)
    for p in range(2):
        for ty in range(4):
            hit = q_row == iota((64, SLOTS), 0)
            second = -1.0 if p else 1.0
            value = jnp.where(ty_row == ty, 1.0, 0.0) + jnp.where(ty_row == ty + 4, second, 0.0)
            first = (p * 4 + ty) * 64
            place[first : first + 64, :] = jnp.where(hit, value, 0.0).astype(BF16)
    low_half = iota((64, 128), 1) < 64

    def deposit(iz):
        arrived(brick_in.at[iz], brick_recv.at[iz])
        stage[...] = brick_in[iz].reshape(1024, 128).astype(F32)
        for pair in range(4):
            laid = jnp.dot(place[...], from_blocks(pair), preferred_element_type=F32)
            for p in range(2):
                for side in range(2):
                    first = (p * 4 + side * 2) * 64
                    te, to = laid[first : first + 64, :], laid[first + 64 : first + 128, :]
                    even = jnp.where(low_half, te, pltpu.roll(to, 64, 1))
                    odd = jnp.where(low_half, pltpu.roll(te, 64, 1), to)
                    for k, value in enumerate((even, odd)):
                        row = (iz * 8 + pair * 2 + k) * 64
                        high, low = halves(value)
                        xhi[p, row : row + 64, side * 128 : side * 128 + 128] = high
                        xlo[p, row : row + 64, side * 128 : side * 128 + 128] = low

    def line_copies(iz, d, source, source_step, target, target_step, send, recv):
        peer = (m + d) % 4
        a = pltpu.make_async_remote_copy(
            src_ref=source.at[peer, iz], dst_ref=target.at[m, iz],
            send_sem=send.at[0, d - 1, iz], recv_sem=recv.at[0, d - 1, iz],
            device_id=line_peer(peer), device_id_type=LOGICAL,
        )
        b = pltpu.make_async_remote_copy(
            src_ref=source_step.at[peer, iz], dst_ref=target_step.at[m, iz],
            send_sem=send.at[1, d - 1, iz], recv_sem=recv.at[1, d - 1, iz],
            device_id=line_peer(peer), device_id_type=LOGICAL,
        )
        return a, b

    def own_copies(iz, which, source, source_step, target, target_step):
        a = pltpu.make_async_copy(source.at[m, iz], target.at[m, iz], own_sem.at[which, 0, iz])
        b = pltpu.make_async_copy(source_step.at[m, iz], target_step.at[m, iz], own_sem.at[which, 1, iz])
        return a, b

    have_table(0)
    forward = (sq, sstep, rq, rstep)
    for iz in range(4):
        deposit(iz)
        rows = slice(iz * 512, iz * 512 + 512)
        for p in range(2):
            value = three(xhi[p, rows, :], xlo[p, rows, :], yin_ref[p, 0], yin_ref[p, 1])
            code, step = coded(value)
            for h in range(2):
                sq[p * 2 + h, iz] = code[:, h * 128 : h * 128 + 128].reshape(8, 4, 16, 128)
                sstep[p * 2 + h, iz] = jnp.broadcast_to(step[:, h * 128 : h * 128 + 128], (8, 128))
        for d in range(1, 4):
            for copy in line_copies(iz, d, *forward, line_send, line_recv):
                copy.start()
        for copy in own_copies(iz, 0, *forward):
            copy.start()

    have_table(1)

    def folded(iz, tz):
        lines = []
        for source in range(4):
            step = rstep[source, iz][0:1, :]
            planes = [decoded(rq[source, iz, :, z].reshape(128, 128), step) for z in (tz, tz + 1)]
            lines.append(jnp.concatenate(planes, axis=1))
        plus = jnp.concatenate([lines[0] + lines[2], lines[1] + lines[3]], axis=0)
        minus = jnp.concatenate([lines[0] - lines[2], lines[1] - lines[3]], axis=0)
        return halves(plus), halves(minus)

    def along_x(p, iz, tz, pair):
        value = three(xin_ref[p, 0], xin_ref[p, 1], pair[0], pair[1])
        rows = slice(p * 256, p * 256 + 256)
        right = left = None
        for k in range(2):
            z, plane = (tz + k) * 4 + iz, value[:, k * 128 : k * 128 + 128]
            spec[z, rows, :] = plane
            to_right, to_left = plane * powers[15 - z, rows, :], plane * powers[z, rows, :]
            right = to_right if right is None else right + to_right
            left = to_left if left is None else left + to_left
        if iz == 0 and tz == 0:
            flow[0, rows, :], flow[1, rows, :] = right, left
        else:
            flow[0, rows, :] += right
            flow[1, rows, :] += left

    def share_out(codes, steps, g, right, left):
        top = jnp.max(jnp.maximum(jnp.abs(right), jnp.abs(left)), axis=0, keepdims=True)
        step = jnp.maximum(top, 1e-30) * (1.0 / 32767.0)
        both = jnp.concatenate([right, left], axis=0) * (1.0 / step)
        codes[g] = jnp.round(both).astype(jnp.int32).astype(jnp.int16)
        steps[g] = step

    def share_in(codes, steps, g):
        both = decoded(codes[g], steps[g])
        return both[0:8, :], both[8:16, :]

    def slab_ends(p):
        def block(b, _):
            for k in range(8):
                rows = pl.ds(pl.multiple_of(p * 256 + b * 64 + k * 8, 8), 8)
                share_out(ends_out.at[p], ends_step_out.at[p], b * 8 + k, flow[0, rows, :], flow[1, rows, :])
            return 0

        lax.fori_loop(0, 4, block, 0)
        slab_exchange(p, (ends_out, ends_in, ends_sem), (ends_step_out, ends_step_in, ends_step_sem))

    def slab_exchange(p, *arrays):
        for peer, where in others:
            for source, target, sem in arrays:
                pltpu.make_async_remote_copy(
                    src_ref=source.at[p, peer], dst_ref=target.at[p, slab],
                    send_sem=sem.at[0, p], recv_sem=sem.at[1, p],
                    device_id=where, device_id_type=LOGICAL,
                ).start()
        for source, target, sem in arrays:
            pltpu.make_async_copy(source.at[p, slab], target.at[p, slab], sem.at[1, p]).start()

    for iz in range(4):
        for d in range(1, 4):
            for copy in line_copies(iz, d, *forward, line_send, line_recv):
                copy.wait_recv()
        for copy in own_copies(iz, 0, *forward):
            copy.wait()
        for tz in range(0, 4, 2):
            plus, minus = folded(iz, tz)
            along_x(0, iz, tz, plus)
            if iz < 3:
                along_x(1, iz, tz, minus)
            else:
                last[tz // 2, 0], last[tz // 2, 1] = minus
    slab_ends(0)
    for tz in range(0, 4, 2):
        along_x(1, 3, tz, (last[tz // 2, 0], last[tz // 2, 1]))
    slab_ends(1)

    def chain(p):
        arrived(ends_in.at[p], ends_sem.at[1, p])
        arrived(ends_step_in.at[p], ends_step_sem.at[1, p])
        some = pl.ds(pl.multiple_of(p * 256 + slab * 8, 8), 8)
        rate = rates_ref[0, some, :]
        weight = rate * rates_ref[1, some, :]
        r2 = rate * rate
        r4 = r2 * r2
        r8 = r4 * r4
        hop = r8 * r8
        far = hop
        for _ in range(5):
            far = far * far
        far = far * rate
        total_right = total_left = jnp.zeros((8, 128), F32)
        for g in range(32):
            values = share_in(ends_in.at[p], ends_step_in.at[p], g)
            known_ends[g, 0], known_ends[g, 1] = values
            total_right = total_right * hop + values[0]
        for g in range(32):
            total_left = total_left * hop + known_ends[31 - g, 1]
        scale = -rate / (1.0 - far * far)
        right = scale * (total_left - far * total_right)
        left = scale * (total_right - far * total_left)
        for g in range(32):
            known_carry[g, 0] = right * weight
            known_carry[31 - g, 1] = left * weight
            right = right * hop + known_ends[g, 0]
            left = left * hop + known_ends[31 - g, 1]
        for g in range(32):
            share_out(carry_out.at[p], carry_step_out.at[p], g, known_carry[g, 0], known_carry[g, 1])
        slab_exchange(p, (carry_out, carry_in, carry_sem), (carry_step_out, carry_step_in, carry_step_sem))

    def filters(p):
        def block(b, _):
            rows = pl.ds(pl.multiple_of(p * 256 + b * 16, 16), 16)
            rate, gain = rates_ref[0, rows, :], rates_ref[1, rows, :]
            planes = [spec[z, rows, :] for z in range(16)]
            beyond, left = [None] * 16, planes[15]
            for z in range(14, -1, -1):
                beyond[z] = left * rate
                left = planes[z] + beyond[z]
            right = planes[0]
            for z in range(16):
                if z:
                    right = planes[z] + right * rate
                both = right if z == 15 else right + beyond[z]
                spec[z, rows, :] = both * gain
            return 0

        lax.fori_loop(0, 16, block, 0)

    def carries(p):
        arrived(carry_in.at[p], carry_sem.at[1, p])
        arrived(carry_step_in.at[p], carry_step_sem.at[1, p])
        for g in range(32):
            rows = slice(p * 256 + g * 8, p * 256 + g * 8 + 8)
            flow[0, rows, :], flow[1, rows, :] = share_in(carry_in.at[p], carry_step_in.at[p], g)

    def back_along_x(p, iz, tz):
        rows = slice(p * 256, p * 256 + 256)
        planes = []
        for z in (tz * 4 + iz, tz * 4 + 4 + iz):
            planes.append(
                spec[z, rows, :]
                + flow[0, rows, :] * powers[z, rows, :]
                + flow[1, rows, :] * powers[15 - z, rows, :]
            )
        high, low = halves(jnp.concatenate(planes, axis=1))
        return three(xout_ref[p, 0], xout_ref[p, 1], high, low)

    filters(0)
    filters(1)
    chain(0)
    chain(1)
    have_table(2)
    carries(0)
    for tz in range(0, 4, 2):
        early[tz // 2] = back_along_x(0, 0, tz)
    carries(1)

    backward = (sq2, sstep2, rq2, rstep2)
    for iz in range(4):
        parts = []
        for tz in range(0, 4, 2):
            even = early[tz // 2] if iz == 0 else back_along_x(0, iz, tz)
            odd = back_along_x(1, iz, tz)
            parts.append((even + odd, even - odd))
        for target in range(4):
            span = slice((target % 2) * 128, (target % 2) * 128 + 128)
            blocks = []
            for tz in range(4):
                block = parts[tz // 2][target // 2][span, (tz % 2) * 128 : (tz % 2) * 128 + 128]
                blocks.append(block)
            top = blocks[0]
            for block in blocks:
                top = jnp.maximum(jnp.abs(top), jnp.abs(block))
            top = jnp.maximum(jnp.max(top, axis=0, keepdims=True), 1e-30)
            step = top * (1.0 / 32767.0)
            inverse = 1.0 / step
            for tz in range(4):
                code = jnp.round(blocks[tz] * inverse).astype(jnp.int32).astype(jnp.int16)
                sq2[target, iz, :, tz] = code.reshape(8, 16, 128)
            sstep2[target, iz] = jnp.broadcast_to(step, (8, 128))
        for d in range(1, 4):
            for copy in line_copies(iz, d, *backward, back_send, back_recv):
                copy.start()
        for copy in own_copies(iz, 1, *backward):
            copy.start()

    wanted = [
        (known[:, 2 * slot + 1 : 2 * slot + 2] * 64 + known[:, 2 * slot : 2 * slot + 1]).astype(jnp.int32)
        for slot in range(2)
    ]
    wanted = jnp.concatenate(wanted, axis=0)
    fetch[...] = jnp.where(iota((SLOTS, 512), 1) == wanted, 1.0, 0.0).astype(BF16)

    def reply(iz):
        for part in range(4):
            lanes = slice((iz * 4 + part) * 128, (iz * 4 + part) * 128 + 128)
            to_blocks(part, jnp.dot(fetch[...], tiles[:, lanes], preferred_element_type=F32))
        reply_out[iz] = stage[...].astype(BF16).reshape(128, 8, 128)
        exchange(reply_out.at[iz], reply_in.at[iz], reply_send.at[iz], reply_recv.at[iz])

    for iz in range(4):
        for d in range(1, 4):
            for copy in line_copies(iz, d, *backward, back_send, back_recv):
                copy.wait_recv()
        for copy in own_copies(iz, 1, *backward):
            copy.wait()
        sums = []
        for p in range(2):
            pieces = [
                decoded(rq2[p * 2 + h, iz].reshape(512, 128), rstep2[p * 2 + h, iz][0:1, :])
                for h in range(2)
            ]
            high, low = halves(jnp.concatenate(pieces, axis=1))
            sums.append(three(high, low, yin_ref[p, 0], yin_ref[p, 1], True))
        for top, value in enumerate((sums[0] + sums[1], sums[0] - sums[1])):
            for half in range(2):
                lanes = slice(half * 128, half * 128 + 128)
                ty = top * 4 + half * 2
                for pair in range(4):
                    even = value[pair * 128 : pair * 128 + 64, lanes]
                    odd = value[pair * 128 + 64 : pair * 128 + 128, lanes]
                    span = slice((iz * 4 + pair) * 128, (iz * 4 + pair) * 128 + 128)
                    first = jnp.where(low_half, even, pltpu.roll(odd, 64, 1))
                    second = jnp.where(low_half, pltpu.roll(even, 64, 1), odd)
                    tiles[ty * 64 : ty * 64 + 64, span] = first.astype(BF16)
                    tiles[ty * 64 + 64 : ty * 64 + 128, span] = second.astype(BF16)
        reply(iz)

    for iz in range(4):
        arrived(reply_in.at[iz], reply_recv.at[iz])
        stage[...] = reply_in[iz].reshape(1024, 128).astype(F32)
        for part in range(4):
            lanes = slice((iz * 4 + part) * 128, (iz * 4 + part) * 128 + 128)
            out_ref[:, lanes] = jnp.dot(
                unpick[...], from_blocks(part), preferred_element_type=F32
            ).astype(BF16)

    sent(meta_out, meta_sem.at[0])
    for iz in range(4):
        sent(brick_out.at[iz], brick_send.at[iz])
        sent(reply_out.at[iz], reply_send.at[iz])
    both = ((ends_out, ends_sem), (ends_step_out, ends_step_sem), (carry_out, carry_sem), (carry_step_out, carry_step_sem))
    for source, sem in both:
        for p in range(2):
            some = source.at[p, pl.ds(0, 31)]
            pltpu.make_async_copy(some, some, sem.at[0, p]).wait()
    for iz in range(4):
        for d in range(1, 4):
            for copy in line_copies(iz, d, *forward, line_send, line_recv):
                copy.wait_send()
            for copy in line_copies(iz, d, *backward, back_send, back_recv):
                copy.wait_send()


VMEM_LIMIT = 54400 * 1024


def on_device(bricks, owners, tile_ids, counts):
    vmem = pl.BlockSpec(memory_space=pltpu.VMEM)
    smem = pl.BlockSpec(memory_space=pltpu.SMEM)
    hbm = pl.BlockSpec(memory_space=pl.ANY)
    codes = pltpu.VMEM((4, 4, 8, 4, 16, 128), jnp.int16)
    steps = pltpu.VMEM((4, 4, 8, 128), F32)
    known = pltpu.VMEM((32, 2, 8, 128), F32)
    share = pltpu.VMEM((2, 32, 16, 128), jnp.int16)
    grain = pltpu.VMEM((2, 32, 1, 128), F32)
    four = pltpu.SemaphoreType.DMA((2, 2))
    blocks = pltpu.VMEM((4, 128, 8, 128), BF16)
    quad = pltpu.SemaphoreType.DMA((4,))
    table = pltpu.VMEM((2, 2, HALF, HALF), BF16)
    notes = pltpu.VMEM((128, 1, 128), F32)
    pair = pltpu.SemaphoreType.DMA((2,))
    line = pltpu.SemaphoreType.DMA((2, 3, 4))
    found = pl.pallas_call(
        field_kernel,
        out_shape=jax.ShapeDtypeStruct((ROWS, CELLS), BF16),
        in_specs=[smem, hbm, vmem, vmem, vmem, hbm],
        out_specs=vmem,
        scratch_shapes=[
            pltpu.VMEM((ROWS, CELLS), BF16),
            pltpu.VMEM((2, 512, 128), F32),
            table, table, table,
            pltpu.SemaphoreType.DMA((4,)),
            pltpu.VMEM((1024, 128), F32),
            blocks, blocks, notes, notes,
            pltpu.VMEM((128, 128), F32),
            blocks, blocks,
            pltpu.VMEM((ROWS, SLOTS), BF16),
            pltpu.VMEM((SLOTS, 512), BF16),
            pltpu.VMEM((512, SLOTS), BF16),
            pltpu.VMEM((2, 2048, HALF), BF16),
            pltpu.VMEM((2, 2048, HALF), BF16),
            codes, steps, codes, steps,
            pltpu.VMEM((16, 512, 128), F32),
            pltpu.VMEM((2, 2, HALF, HALF), BF16),
            known, known,
            share, share, share, share, grain, grain, grain, grain,
            pltpu.VMEM((16, 512, 128), F32),
            pltpu.VMEM((2, 512, 128), F32),
            pltpu.VMEM((2, HALF, HALF), F32),
            codes, steps, codes, steps,
            pltpu.VMEM((512, CELLS), BF16),
            quad, quad, pair, quad, quad, line, line, four, four, four, four, line, line,
            pltpu.SemaphoreType.DMA((2, 2, 4)),
        ],
        compiler_params=pltpu.CompilerParams(
            collective_id=0, has_side_effects=True, vmem_limit_bytes=VMEM_LIMIT
        ),
        name="field",
    )(counts, bricks, owners.reshape(1, ROWS), tile_ids.reshape(1, ROWS), jnp.asarray(second_differences()), jnp.asarray(tables()))
    live = jnp.arange(ROWS, dtype=jnp.int32)[:, None] < counts[0]
    return jnp.where(live, found, jnp.zeros_like(found))


def solution(mesh):
    in_specs = (P(("gz", "ma"), None), P(("gz", "ma"), None), P(("gz", "ma")), P(("gz", "ma")))
    out_specs = P(("gz", "ma"), None)
    return jax.shard_map(
        on_device, mesh=mesh, in_specs=in_specs, out_specs=out_specs, check_vma=False
    )
```

```python
import math

import jax
import jax.numpy as jnp
import ml_dtypes
import numpy as np
from jax import lax
from jax.experimental import pallas as pl
from jax.experimental.pallas import tpu as pltpu
from jax.sharding import PartitionSpec as P

N = 512
HALF = 256
SCREEN = 16
F32 = jnp.float32
BF16 = jnp.bfloat16
LOGICAL = pl.DeviceIdType.LOGICAL
SLOTS = 256
CELLS = 2048
ROWS = 128


def split_table(table):
    high = table.astype(ml_dtypes.bfloat16)
    low = (table - high.astype(np.float64)).astype(ml_dtypes.bfloat16)
    return high, low


def parity_table(parity, points):
    modes = 2 * np.arange(HALF) + parity
    angle = 2.0 * math.pi / N * ((modes[:, None] * points[None, :]) % N)
    return (np.cos(angle) + np.sin(angle)) / math.sqrt(N)


def stacked(tables):
    return np.stack([np.stack(split_table(t)) for t in tables])


def tables():
    natural = np.arange(HALF)
    m, ix, tx = np.meshgrid(np.arange(2), np.arange(8), np.arange(16), indexing="ij")
    order = (m * 128 + tx * 8 + ix).reshape(-1)
    y_tables = [parity_table(p, natural) for p in (0, 1)]
    x_tables = [parity_table(p, order) for p in (0, 1)]
    y_in = stacked([t.T for t in y_tables])
    x_in = stacked(x_tables)
    x_out = stacked([t.T for t in x_tables])
    return np.stack([y_in, x_in, x_out])


def second_differences():
    k = np.arange(128)
    rows = [2 * (128 * (c % 2) + k) + c // 2 for c in range(4)]
    values = (4.0 * np.sin(math.pi / N * np.stack(rows)) ** 2).astype(np.float32)
    return np.concatenate([values, values])


def seat(core, u, v, w, m):
    q = (m - (u + v + w) + 8) % 4
    x = (2 * v + core + q // 2) % 4
    side = 2 * w + q % 2
    y = u + core * (side - u)
    z = side + core * (u - side)
    return y * 32 + x * 8 + core * 4 + z


def handler(owner):
    return seat((owner // 4) % 2, owner // 32, (owner // 16) % 2, (owner // 8) % 2, owner % 4)


def iota(shape, axis):
    return lax.broadcasted_iota(jnp.int32, shape, axis)


def pickers(owners_ref, count):
    row = jnp.broadcast_to(handler(owners_ref[...]), (ROWS, ROWS))
    column = jnp.transpose(row.astype(F32)).astype(jnp.int32)
    target = column[:, 0:1]
    same = column == row
    i, j = iota((ROWS, ROWS), 0), iota((ROWS, ROWS), 1)
    within_column = jnp.sum(jnp.where(same & (j < i), 1.0, 0.0), axis=1, keepdims=True)
    within_row = jnp.sum(jnp.where(same & (i < j), 1.0, 0.0), axis=0, keepdims=True)
    slot_column = target + ROWS * within_column.astype(jnp.int32)
    slot_row = row[0:1, :] + ROWS * within_row.astype(jnp.int32)
    down = (iota((SLOTS, ROWS), 0) == slot_row) & (iota((SLOTS, ROWS), 1) < count)
    across = iota((ROWS, SLOTS), 1) == slot_column
    return jnp.where(down, 1.0, 0.0).astype(BF16), jnp.where(across, 1.0, 0.0).astype(BF16)


def halves(value):
    high = value.astype(BF16)
    return high, (value - high.astype(F32)).astype(BF16)


def three(a_high, a_low, b_high, b_low, turned=False):
    dims = (((1,), (1 if turned else 0,)), ((), ()))
    total = lax.dot_general(a_high, b_high, dims, preferred_element_type=F32)
    total += lax.dot_general(a_high, b_low, dims, preferred_element_type=F32)
    total += lax.dot_general(a_low, b_high, dims, preferred_element_type=F32)
    return total


def coded(value):
    top = jnp.max(jnp.abs(value), axis=0, keepdims=True)
    step = jnp.maximum(top, 1e-30) * (1.0 / 32767.0)
    return jnp.round(value * (1.0 / step)).astype(jnp.int32).astype(jnp.int16), step


def decoded(code, step):
    return code.astype(jnp.int32).astype(F32) * step


def field_kernel(
    counts_ref, bricks_hbm, owners_ref, ids_ref, lam_ref, tables_hbm, out_ref,
    bricks_ref, rates_ref, yin_ref, xin_ref, xout_ref, table_sem,
    stage, brick_out, brick_in, meta_out, meta_in, meta, reply_out, reply_in, unpick, fetch, place, xhi, xlo, sq, sstep, rq, rstep, spec, last, known_ends, known_carry,
    ends_out, ends_in, carry_out, carry_in, ends_step_out, ends_step_in, carry_step_out, carry_step_in,
    powers, flow, early, sq2, sstep2, rq2, rstep2, tiles,
    brick_send, brick_recv, meta_sem, reply_send, reply_recv, line_send, line_recv, ends_sem, carry_sem, ends_step_sem, carry_step_sem, back_send, back_recv, own_sem,
):
    gz, ma = lax.axis_index("gz"), lax.axis_index("ma")
    y, x, core = gz // 8, (gz // 2) % 4, gz % 2
    me = gz * 4 + ma
    shifted = (x + 4 - core) % 4
    u, side = y + core * (ma - y), ma + core * (y - ma)
    v, w = shifted // 2, side // 2
    m = (2 * (shifted % 2) + side % 2 + u + v + w) % 4
    slab = u * 8 + v * 4 + w * 2 + core

    def wrap(value, size):
        return jnp.where(value >= size, value - size, value)

    turn = u + v + w
    corner = (m - turn + 8) % 4
    others_of_line = {}
    for d, q in ((3, 3 - corner), (1, corner + 1 - 2 * (corner % 2)), (2, (corner + 2) % 4)):
        p = (q + turn) % 4
        others_of_line[d] = (p, seat(core, u, v, w, p))

    def slab_peers():
        for du in range(4):
            pu = wrap(u + du, 4)
            for dv in range(2):
                pv = v if dv == 0 else 1 - v
                for dw in range(2):
                    pw = w if dw == 0 else 1 - w
                    for dc in range(2):
                        if du or dv or dw or dc:
                            pc = core if dc == 0 else 1 - core
                            yield pu * 8 + pv * 4 + pw * 2 + pc, seat(pc, pu, pv, pw, m)

    def peers(body):
        def step(i, _):
            for k in range(8):
                body(wrap(me + (i * 8 + k + 1), 128))
            return 0

        lax.fori_loop(0, 15, step, 0)
        for d in range(121, 128):
            body(wrap(me + d, 128))

    pltpu.make_async_copy(bricks_hbm, bricks_ref, table_sem.at[3]).start()
    tables = [(tables_hbm.at[i], ref) for i, ref in enumerate((yin_ref, xin_ref, xout_ref))]
    def have_table(i):
        pltpu.make_async_copy(*tables[i], table_sem.at[i]).wait()

    barrier = pltpu.get_barrier_semaphore()
    peers(lambda n: pl.semaphore_signal(barrier, inc=1, device_id=n, device_id_type=LOGICAL))

    def exchange(source, target, send, recv):
        def start(n):
            pltpu.make_async_remote_copy(
                src_ref=source.at[n], dst_ref=target.at[me], send_sem=send, recv_sem=recv,
                device_id=n, device_id_type=LOGICAL,
            ).start()

        peers(start)
        pltpu.make_async_copy(source.at[me], target.at[me], recv).start()

    def arrived(target, recv):
        pltpu.make_async_copy(target, target, recv).wait()

    def sent(source, send):
        some = source.at[pl.ds(0, 127)]
        pltpu.make_async_copy(some, some, send).wait()

    def to_blocks(part, block):
        for slot in range(2):
            stage[pl.ds(slot * 4 + part, 128, stride=8), :] = block[slot * 128 : slot * 128 + 128, :]

    def from_blocks(part):
        slots = [stage[pl.ds(slot * 4 + part, 128, stride=8), :] for slot in range(2)]
        return jnp.concatenate(slots, axis=0).astype(BF16)

    for i, (source, target) in enumerate(tables):
        pltpu.make_async_copy(source, target, table_sem.at[i]).start()

    pick, unpick[...] = pickers(owners_ref, counts_ref[0])
    pltpu.make_async_copy(bricks_hbm, bricks_ref, table_sem.at[3]).wait()

    def send_bricks(iz):
        for part in range(4):
            lanes = slice((iz * 4 + part) * 128, (iz * 4 + part) * 128 + 128)
            to_blocks(part, jnp.dot(pick, bricks_ref[:, lanes], preferred_element_type=F32))
        brick_out[iz] = stage[...].astype(BF16).reshape(128, 8, 128)
        if iz == 0:
            pl.semaphore_wait(barrier, 127)
        exchange(brick_out.at[iz], brick_in.at[iz], brick_send.at[iz], brick_recv.at[iz])

    send_bricks(0)
    ids = ids_ref[...]
    lane_row = iota((ROWS, ROWS), 0)
    for slot in range(2):
        info = jnp.where(lane_row == 2 * slot, ids // 8, jnp.where(lane_row == 2 * slot + 1, ids % 8, 0))
        info = jnp.transpose(info.astype(F32)).astype(BF16)
        part = jnp.dot(pick[slot * 128 : slot * 128 + 128, :], info, preferred_element_type=F32)
        meta[...] = part if slot == 0 else meta[...] + part

    def spread(i, _):
        for k in range(8):
            meta_out[i * 8 + k] = meta[pl.ds(i * 8 + k, 1), :]
        return 0

    lax.fori_loop(0, 16, spread, 0)
    exchange(meta_out, meta_in, meta_sem.at[0], meta_sem.at[1])
    for iz in range(1, 4):
        send_bricks(iz)

    others = list(slab_peers())

    lam_k = lam_ref[pl.ds(4 + m, 1), :]
    for block in range(4):
        lam_j = jnp.transpose(jnp.broadcast_to(lam_ref[block : block + 1, :], (128, 128)))
        excess = 1.0 / (SCREEN * SCREEN) + lam_j + lam_k
        root = jnp.sqrt(excess * (excess + 4.0))
        rows = slice(block * 128, block * 128 + 128)
        rates_ref[0, rows, :] = 2.0 / (2.0 + excess + root)
        rates_ref[1, rows, :] = 1.0 / root

    def raise_rates(b, _):
        rows = pl.ds(pl.multiple_of(b * 32, 32), 32)
        rate = rates_ref[0, rows, :]
        power = jnp.ones((32, 128), F32)
        for z in range(16):
            powers[z, rows, :] = power
            power = power * rate
        return 0

    lax.fori_loop(0, 16, raise_rates, 0)

    arrived(meta_in, meta_sem.at[1])

    def collect(i, _):
        for k in range(8):
            meta[pl.ds(i * 8 + k, 1), :] = meta_in[i * 8 + k]
        return 0

    lax.fori_loop(0, 16, collect, 0)

    known = meta[...]
    meta_rows = jnp.transpose(known)
    q_row = jnp.concatenate([meta_rows[0:1, :], meta_rows[2:3, :]], axis=1).astype(jnp.int32)
    ty_row = jnp.concatenate([meta_rows[1:2, :], meta_rows[3:4, :]], axis=1).astype(jnp.int32)
    for p in range(2):
        for ty in range(4):
            hit = q_row == iota((64, SLOTS), 0)
            second = -1.0 if p else 1.0
            value = jnp.where(ty_row == ty, 1.0, 0.0) + jnp.where(ty_row == ty + 4, second, 0.0)
            first = (p * 4 + ty) * 64
            place[first : first + 64, :] = jnp.where(hit, value, 0.0).astype(BF16)
    low_half = iota((64, 128), 1) < 64

    def deposit(iz):
        arrived(brick_in.at[iz], brick_recv.at[iz])
        stage[...] = brick_in[iz].reshape(1024, 128).astype(F32)
        for pair in range(4):
            laid = jnp.dot(place[...], from_blocks(pair), preferred_element_type=F32)
            for p in range(2):
                for side in range(2):
                    first = (p * 4 + side * 2) * 64
                    te, to = laid[first : first + 64, :], laid[first + 64 : first + 128, :]
                    even = jnp.where(low_half, te, pltpu.roll(to, 64, 1))
                    odd = jnp.where(low_half, pltpu.roll(te, 64, 1), to)
                    for k, value in enumerate((even, odd)):
                        row = (iz * 8 + pair * 2 + k) * 64
                        high, low = halves(value)
                        xhi[p, row : row + 64, side * 128 : side * 128 + 128] = high
                        xlo[p, row : row + 64, side * 128 : side * 128 + 128] = low

    def line_copies(iz, d, source, source_step, target, target_step, send, recv):
        peer, where = others_of_line[d]
        a = pltpu.make_async_remote_copy(
            src_ref=source.at[peer, iz], dst_ref=target.at[m, iz],
            send_sem=send.at[0, d - 1, iz], recv_sem=recv.at[0, d - 1, iz],
            device_id=where, device_id_type=LOGICAL,
        )
        b = pltpu.make_async_remote_copy(
            src_ref=source_step.at[peer, iz], dst_ref=target_step.at[m, iz],
            send_sem=send.at[1, d - 1, iz], recv_sem=recv.at[1, d - 1, iz],
            device_id=where, device_id_type=LOGICAL,
        )
        return a, b

    def own_copies(iz, which, source, source_step, target, target_step):
        a = pltpu.make_async_copy(source.at[m, iz], target.at[m, iz], own_sem.at[which, 0, iz])
        b = pltpu.make_async_copy(source_step.at[m, iz], target_step.at[m, iz], own_sem.at[which, 1, iz])
        return a, b

    have_table(0)
    forward = (sq, sstep, rq, rstep)
    for iz in range(4):
        deposit(iz)
        rows = slice(iz * 512, iz * 512 + 512)
        for p in range(2):
            value = three(xhi[p, rows, :], xlo[p, rows, :], yin_ref[p, 0], yin_ref[p, 1])
            code, step = coded(value)
            for h in range(2):
                sq[p * 2 + h, iz] = code[:, h * 128 : h * 128 + 128].reshape(8, 4, 16, 128)
                sstep[p * 2 + h, iz] = jnp.broadcast_to(step[:, h * 128 : h * 128 + 128], (8, 128))
        for d in (3, 1, 2):
            for copy in line_copies(iz, d, *forward, line_send, line_recv):
                copy.start()
        for copy in own_copies(iz, 0, *forward):
            copy.start()

    have_table(1)

    def folded(iz, tz):
        lines = []
        for source in range(4):
            step = rstep[source, iz][0:1, :]
            planes = [decoded(rq[source, iz, :, z].reshape(128, 128), step) for z in (tz, tz + 1)]
            lines.append(jnp.concatenate(planes, axis=1))
        plus = jnp.concatenate([lines[0] + lines[2], lines[1] + lines[3]], axis=0)
        minus = jnp.concatenate([lines[0] - lines[2], lines[1] - lines[3]], axis=0)
        return halves(plus), halves(minus)

    def along_x(p, iz, tz, pair):
        value = three(xin_ref[p, 0], xin_ref[p, 1], pair[0], pair[1])
        rows = slice(p * 256, p * 256 + 256)
        right = left = None
        for k in range(2):
            z, plane = (tz + k) * 4 + iz, value[:, k * 128 : k * 128 + 128]
            spec[z, rows, :] = plane
            to_right, to_left = plane * powers[15 - z, rows, :], plane * powers[z, rows, :]
            right = to_right if right is None else right + to_right
            left = to_left if left is None else left + to_left
        if iz == 0 and tz == 0:
            flow[0, rows, :], flow[1, rows, :] = right, left
        else:
            flow[0, rows, :] += right
            flow[1, rows, :] += left

    def share_out(codes, steps, g, right, left):
        top = jnp.max(jnp.maximum(jnp.abs(right), jnp.abs(left)), axis=0, keepdims=True)
        step = jnp.maximum(top, 1e-30) * (1.0 / 32767.0)
        both = jnp.concatenate([right, left], axis=0) * (1.0 / step)
        codes[g] = jnp.round(both).astype(jnp.int32).astype(jnp.int16)
        steps[g] = step

    def share_in(codes, steps, g):
        both = decoded(codes[g], steps[g])
        return both[0:8, :], both[8:16, :]

    def slab_ends(p):
        def block(b, _):
            for k in range(8):
                rows = pl.ds(pl.multiple_of(p * 256 + b * 64 + k * 8, 8), 8)
                share_out(ends_out.at[p], ends_step_out.at[p], b * 8 + k, flow[0, rows, :], flow[1, rows, :])
            return 0

        lax.fori_loop(0, 4, block, 0)
        slab_exchange(p, (ends_out, ends_in, ends_sem), (ends_step_out, ends_step_in, ends_step_sem))

    def slab_exchange(p, *arrays):
        for peer, where in others:
            for source, target, sem in arrays:
                pltpu.make_async_remote_copy(
                    src_ref=source.at[p, peer], dst_ref=target.at[p, slab],
                    send_sem=sem.at[0, p], recv_sem=sem.at[1, p],
                    device_id=where, device_id_type=LOGICAL,
                ).start()
        for source, target, sem in arrays:
            pltpu.make_async_copy(source.at[p, slab], target.at[p, slab], sem.at[1, p]).start()

    for iz in range(4):
        for d in (3, 1, 2):
            for copy in line_copies(iz, d, *forward, line_send, line_recv):
                copy.wait_recv()
        for copy in own_copies(iz, 0, *forward):
            copy.wait()
        for tz in range(0, 4, 2):
            plus, minus = folded(iz, tz)
            along_x(0, iz, tz, plus)
            if iz < 3:
                along_x(1, iz, tz, minus)
            else:
                last[tz // 2, 0], last[tz // 2, 1] = minus
    slab_ends(0)
    for tz in range(0, 4, 2):
        along_x(1, 3, tz, (last[tz // 2, 0], last[tz // 2, 1]))
    slab_ends(1)

    def chain(p):
        arrived(ends_in.at[p], ends_sem.at[1, p])
        arrived(ends_step_in.at[p], ends_step_sem.at[1, p])
        some = pl.ds(pl.multiple_of(p * 256 + slab * 8, 8), 8)
        rate = rates_ref[0, some, :]
        weight = rate * rates_ref[1, some, :]
        r2 = rate * rate
        r4 = r2 * r2
        r8 = r4 * r4
        hop = r8 * r8
        far = hop
        for _ in range(5):
            far = far * far
        far = far * rate
        total_right = total_left = jnp.zeros((8, 128), F32)
        for g in range(32):
            values = share_in(ends_in.at[p], ends_step_in.at[p], g)
            known_ends[g, 0], known_ends[g, 1] = values
            total_right = total_right * hop + values[0]
        for g in range(32):
            total_left = total_left * hop + known_ends[31 - g, 1]
        scale = -rate / (1.0 - far * far)
        right = scale * (total_left - far * total_right)
        left = scale * (total_right - far * total_left)
        for g in range(32):
            known_carry[g, 0] = right * weight
            known_carry[31 - g, 1] = left * weight
            right = right * hop + known_ends[g, 0]
            left = left * hop + known_ends[31 - g, 1]
        for g in range(32):
            share_out(carry_out.at[p], carry_step_out.at[p], g, known_carry[g, 0], known_carry[g, 1])
        slab_exchange(p, (carry_out, carry_in, carry_sem), (carry_step_out, carry_step_in, carry_step_sem))

    def filters(p):
        def block(b, _):
            rows = pl.ds(pl.multiple_of(p * 256 + b * 16, 16), 16)
            rate, gain = rates_ref[0, rows, :], rates_ref[1, rows, :]
            planes = [spec[z, rows, :] for z in range(16)]
            beyond, left = [None] * 16, planes[15]
            for z in range(14, -1, -1):
                beyond[z] = left * rate
                left = planes[z] + beyond[z]
            right = planes[0]
            for z in range(16):
                if z:
                    right = planes[z] + right * rate
                both = right if z == 15 else right + beyond[z]
                spec[z, rows, :] = both * gain
            return 0

        lax.fori_loop(0, 16, block, 0)

    def carries(p):
        arrived(carry_in.at[p], carry_sem.at[1, p])
        arrived(carry_step_in.at[p], carry_step_sem.at[1, p])
        for g in range(32):
            rows = slice(p * 256 + g * 8, p * 256 + g * 8 + 8)
            flow[0, rows, :], flow[1, rows, :] = share_in(carry_in.at[p], carry_step_in.at[p], g)

    def back_along_x(p, iz, tz):
        rows = slice(p * 256, p * 256 + 256)
        planes = []
        for z in (tz * 4 + iz, tz * 4 + 4 + iz):
            planes.append(
                spec[z, rows, :]
                + flow[0, rows, :] * powers[z, rows, :]
                + flow[1, rows, :] * powers[15 - z, rows, :]
            )
        high, low = halves(jnp.concatenate(planes, axis=1))
        return three(xout_ref[p, 0], xout_ref[p, 1], high, low)

    filters(0)
    filters(1)
    chain(0)
    chain(1)
    have_table(2)
    carries(0)
    for tz in range(0, 4, 2):
        early[tz // 2] = back_along_x(0, 0, tz)
    carries(1)

    backward = (sq2, sstep2, rq2, rstep2)
    for iz in range(4):
        parts = []
        for tz in range(0, 4, 2):
            even = early[tz // 2] if iz == 0 else back_along_x(0, iz, tz)
            odd = back_along_x(1, iz, tz)
            parts.append((even + odd, even - odd))
        for target in range(4):
            span = slice((target % 2) * 128, (target % 2) * 128 + 128)
            blocks = []
            for tz in range(4):
                block = parts[tz // 2][target // 2][span, (tz % 2) * 128 : (tz % 2) * 128 + 128]
                blocks.append(block)
            top = blocks[0]
            for block in blocks:
                top = jnp.maximum(jnp.abs(top), jnp.abs(block))
            top = jnp.maximum(jnp.max(top, axis=0, keepdims=True), 1e-30)
            step = top * (1.0 / 32767.0)
            inverse = 1.0 / step
            for tz in range(4):
                code = jnp.round(blocks[tz] * inverse).astype(jnp.int32).astype(jnp.int16)
                sq2[target, iz, :, tz] = code.reshape(8, 16, 128)
            sstep2[target, iz] = jnp.broadcast_to(step, (8, 128))
        for d in (3, 1, 2):
            for copy in line_copies(iz, d, *backward, back_send, back_recv):
                copy.start()
        for copy in own_copies(iz, 1, *backward):
            copy.start()

    wanted = [
        (known[:, 2 * slot + 1 : 2 * slot + 2] * 64 + known[:, 2 * slot : 2 * slot + 1]).astype(jnp.int32)
        for slot in range(2)
    ]
    wanted = jnp.concatenate(wanted, axis=0)
    fetch[...] = jnp.where(iota((SLOTS, 512), 1) == wanted, 1.0, 0.0).astype(BF16)

    def reply(iz):
        for part in range(4):
            lanes = slice((iz * 4 + part) * 128, (iz * 4 + part) * 128 + 128)
            to_blocks(part, jnp.dot(fetch[...], tiles[:, lanes], preferred_element_type=F32))
        reply_out[iz] = stage[...].astype(BF16).reshape(128, 8, 128)
        exchange(reply_out.at[iz], reply_in.at[iz], reply_send.at[iz], reply_recv.at[iz])

    for iz in range(4):
        for d in (3, 1, 2):
            for copy in line_copies(iz, d, *backward, back_send, back_recv):
                copy.wait_recv()
        for copy in own_copies(iz, 1, *backward):
            copy.wait()
        sums = []
        for p in range(2):
            pieces = [
                decoded(rq2[p * 2 + h, iz].reshape(512, 128), rstep2[p * 2 + h, iz][0:1, :])
                for h in range(2)
            ]
            high, low = halves(jnp.concatenate(pieces, axis=1))
            sums.append(three(high, low, yin_ref[p, 0], yin_ref[p, 1], True))
        for top, value in enumerate((sums[0] + sums[1], sums[0] - sums[1])):
            for half in range(2):
                lanes = slice(half * 128, half * 128 + 128)
                ty = top * 4 + half * 2
                for pair in range(4):
                    even = value[pair * 128 : pair * 128 + 64, lanes]
                    odd = value[pair * 128 + 64 : pair * 128 + 128, lanes]
                    span = slice((iz * 4 + pair) * 128, (iz * 4 + pair) * 128 + 128)
                    first = jnp.where(low_half, even, pltpu.roll(odd, 64, 1))
                    second = jnp.where(low_half, pltpu.roll(even, 64, 1), odd)
                    tiles[ty * 64 : ty * 64 + 64, span] = first.astype(BF16)
                    tiles[ty * 64 + 64 : ty * 64 + 128, span] = second.astype(BF16)
        reply(iz)

    for iz in range(4):
        arrived(reply_in.at[iz], reply_recv.at[iz])
        stage[...] = reply_in[iz].reshape(1024, 128).astype(F32)
        for part in range(4):
            lanes = slice((iz * 4 + part) * 128, (iz * 4 + part) * 128 + 128)
            out_ref[:, lanes] = jnp.dot(
                unpick[...], from_blocks(part), preferred_element_type=F32
            ).astype(BF16)

    sent(meta_out, meta_sem.at[0])
    for iz in range(4):
        sent(brick_out.at[iz], brick_send.at[iz])
        sent(reply_out.at[iz], reply_send.at[iz])
    both = ((ends_out, ends_sem), (ends_step_out, ends_step_sem), (carry_out, carry_sem), (carry_step_out, carry_step_sem))
    for source, sem in both:
        for p in range(2):
            some = source.at[p, pl.ds(0, 31)]
            pltpu.make_async_copy(some, some, sem.at[0, p]).wait()
    for iz in range(4):
        for d in (3, 1, 2):
            for copy in line_copies(iz, d, *forward, line_send, line_recv):
                copy.wait_send()
            for copy in line_copies(iz, d, *backward, back_send, back_recv):
                copy.wait_send()


VMEM_LIMIT = 54400 * 1024


def on_device(bricks, owners, tile_ids, counts):
    vmem = pl.BlockSpec(memory_space=pltpu.VMEM)
    smem = pl.BlockSpec(memory_space=pltpu.SMEM)
    hbm = pl.BlockSpec(memory_space=pl.ANY)
    codes = pltpu.VMEM((4, 4, 8, 4, 16, 128), jnp.int16)
    steps = pltpu.VMEM((4, 4, 8, 128), F32)
    known = pltpu.VMEM((32, 2, 8, 128), F32)
    share = pltpu.VMEM((2, 32, 16, 128), jnp.int16)
    grain = pltpu.VMEM((2, 32, 1, 128), F32)
    four = pltpu.SemaphoreType.DMA((2, 2))
    blocks = pltpu.VMEM((4, 128, 8, 128), BF16)
    quad = pltpu.SemaphoreType.DMA((4,))
    table = pltpu.VMEM((2, 2, HALF, HALF), BF16)
    notes = pltpu.VMEM((128, 1, 128), F32)
    pair = pltpu.SemaphoreType.DMA((2,))
    line = pltpu.SemaphoreType.DMA((2, 3, 4))
    found = pl.pallas_call(
        field_kernel,
        out_shape=jax.ShapeDtypeStruct((ROWS, CELLS), BF16),
        in_specs=[smem, hbm, vmem, vmem, vmem, hbm],
        out_specs=vmem,
        scratch_shapes=[
            pltpu.VMEM((ROWS, CELLS), BF16),
            pltpu.VMEM((2, 512, 128), F32),
            table, table, table,
            pltpu.SemaphoreType.DMA((4,)),
            pltpu.VMEM((1024, 128), F32),
            blocks, blocks, notes, notes,
            pltpu.VMEM((128, 128), F32),
            blocks, blocks,
            pltpu.VMEM((ROWS, SLOTS), BF16),
            pltpu.VMEM((SLOTS, 512), BF16),
            pltpu.VMEM((512, SLOTS), BF16),
            pltpu.VMEM((2, 2048, HALF), BF16),
            pltpu.VMEM((2, 2048, HALF), BF16),
            codes, steps, codes, steps,
            pltpu.VMEM((16, 512, 128), F32),
            pltpu.VMEM((2, 2, HALF, HALF), BF16),
            known, known,
            share, share, share, share, grain, grain, grain, grain,
            pltpu.VMEM((16, 512, 128), F32),
            pltpu.VMEM((2, 512, 128), F32),
            pltpu.VMEM((2, HALF, HALF), F32),
            codes, steps, codes, steps,
            pltpu.VMEM((512, CELLS), BF16),
            quad, quad, pair, quad, quad, line, line, four, four, four, four, line, line,
            pltpu.SemaphoreType.DMA((2, 2, 4)),
        ],
        compiler_params=pltpu.CompilerParams(
            collective_id=0, has_side_effects=True, vmem_limit_bytes=VMEM_LIMIT
        ),
        name="field",
    )(counts, bricks, owners.reshape(1, ROWS), tile_ids.reshape(1, ROWS), jnp.asarray(second_differences()), jnp.asarray(tables()))
    live = jnp.arange(ROWS, dtype=jnp.int32)[:, None] < counts[0]
    return jnp.where(live, found, jnp.zeros_like(found))


def solution(mesh):
    in_specs = (P(("gz", "ma"), None), P(("gz", "ma"), None), P(("gz", "ma")), P(("gz", "ma")))
    out_specs = P(("gz", "ma"), None)
    return jax.shard_map(
        on_device, mesh=mesh, in_specs=in_specs, out_specs=out_specs, check_vma=False
    )
```
